32 devices in a mesh: space: 16 (over z, x, core), band: 2 (over y).
Axes of the slice: x: 2, y: 2, z: 4, core: 2. Of those that a mesh axis runs over, the one named last changes fastest.
Arguments:
- wave_in: bfloat16 [256, 16, 16, 256], P('space', None, None, 'band'), parts along dimension 3, may hold values from -6 to 6
- mass_scale: float32 [256, 256], P('space'), may hold values from 0.5 to 1
- potential: float32 [256, 256], P('space'), may hold values from -2 to 1
- elem_scale: float32 [32, 2, 2], P('space'), may hold values from 0.5 to 1.5
- stiffness: bfloat16 [729, 729], replicated, as said below
- proj_lower: bfloat16 [16, 729, 32], P('space'), may hold values from -0.21875 to 0.21875
- proj_upper: bfloat16 [16, 729, 32], P('space'), may hold values from -0.21875 to 0.21875
- kb_coef: float32 [16, 32], P('space'), may hold values from -3 to 3
- atom_column: int32 [16], P('space'), may hold values from 0 to 3
- chan_count: int32 [16], P('space'), may hold values from 8 to 32
- upper_column: int32 [16], P('space'), may hold values from 0 to 3
Outputs:
- filtered: bfloat16 [256, 16, 16, 256], P('space', None, None, 'band'), parts along dimension 3
- coefficients: float32 [16, 32, 256], P('space', None, 'band'), parts along dimension 2
The draws below stay inside these ranges and needn't reach their ends.
There are 2 independent parts, one for each index of `band`. The reference program is written for one: setup_inputs(seed, part) draws one part's arguments, and reference() takes and returns one part's arrays. A program takes and returns all parts, laid end to end along the dimension named above; an argument that names none is the same for every part. Nothing has to cross between parts.
Inputs may be any that keep to these rules, and one draw needn't show every extreme that they name: stiffness is symmetric.
All inputs are finite; a program needn't handle non-finite values.
Results may differ from the reference program's by a relative error of at most 0.006.
Values may be sent and summed in bfloat16 or wider, within the bound.
No kernel may reach another device: no remote copies, remote signals or barrier semaphores. Data moves between devices by JAX's collectives and lax.ppermute only.
A program may use at most 64 MiB of HBM per device.

```python
import math
import jax
import jax.numpy as jnp
from jax import lax

ORDER = 8
CH = 32
NB = 128
ATOM_DEV = 1
CS = 16
ELN = 729
NZ = 256
EZ = 32
ATOMS = 16
N_SPACE = 16


def draw_stiffness(key, part):
    off_key, diag_key = jax.random.split(jax.random.fold_in(key, 17))
    spread = 0.5 / ELN ** 0.5
    off_diagonal = jnp.clip(jax.random.normal(off_key, (ELN, ELN), jnp.float32) * spread, -4.0 * spread, 4.0 * spread)
    symmetric = 0.5 * (off_diagonal + off_diagonal.T)
    diagonal = jax.random.uniform(diag_key, (ELN,), jnp.float32, 0.5, 1.0)
    return (symmetric + jnp.diag(diagonal)).astype(jnp.bfloat16)


def plant(result, own_key, least, high):
    spot = [jax.random.randint(jax.random.fold_in(own_key, axis), (), 0, length) for axis, length in enumerate(result.shape)]
    main_axis = result.shape.index(max(result.shape))
    next_to = spot[:main_axis] + [(spot[main_axis] + 1) % result.shape[main_axis]] + spot[main_axis + 1:]
    return result.at[tuple(spot)].set(least).at[tuple(next_to)].set(high)


def block_levels(rng, dims, cuts, low, top_value):
    def one(axis_at, parts):
        steps = jax.random.uniform(jax.random.fold_in(jax.random.fold_in(rng, 6), axis_at), (parts,), jnp.float32, low / len(cuts), top_value / len(cuts))
        return jnp.repeat(jnp.exp(steps), dims[axis_at] // parts).reshape((-1,) + (1,) * (len(dims) - axis_at - 1))

    factor_of = one(*cuts[0])
    for cut in cuts[1:]:
        factor_of = factor_of * one(*cut)
    return factor_of


def gaussian(stream_key, shape, width, limit, shards=(), kind=jnp.bfloat16):
    result = width * jax.random.normal(stream_key, shape, jnp.float32)
    if shards:
        result = result * block_levels(stream_key, shape, shards, -0.22, 0.18)
    return jnp.clip(result, -limit, limit).astype(kind)


def setup_inputs(seed: int = 0, part: int = 0) -> dict:
    key_of = jax.random.split(jax.random.key(seed), 12)
    part_keys = jax.random.split(jax.random.fold_in(key_of[11], part), 12)
    wave_in = gaussian(part_keys[0], (NZ, CS, CS, NB), 1.0, 6.0, ((0, 16),))
    mass_scale = jnp.clip(jnp.exp(math.log(1.0) - 0.6931472 * jax.random.uniform(key_of[1], (NZ, CS * CS), jnp.float32) ** block_levels(key_of[1], (NZ, CS * CS), ((0, 16),), -0.2, 0.2)), 0.5, 1.0)
    potential = jnp.clip(-2.0 + 3.0 * jax.random.uniform(key_of[2], (NZ, CS * CS), jnp.float32) ** block_levels(key_of[2], (NZ, CS * CS), ((0, 16),), -0.2, 0.2), -2.0, 1.0)
    elem_scale = jnp.clip(jnp.exp(math.log(1.5) - 1.0986123 * jax.random.uniform(key_of[3], (EZ, 2, 2), jnp.float32) ** block_levels(key_of[3], (EZ, 2, 2), ((0, 16),), -0.2, 0.2)), 0.5, 1.5)
    stiffness = draw_stiffness(jax.random.fold_in(key_of[11], 71), part)
    proj_lower = gaussian(key_of[5], (ATOMS, ELN, CH), ELN ** -0.5, 0.21875, ((0, 16),))
    proj_upper = gaussian(key_of[6], (ATOMS, ELN, CH), ELN ** -0.5, 0.21875, ((0, 16),))
    kb_coef = jnp.clip(jax.random.uniform(key_of[7], (ATOMS, CH), jnp.float32, -3.0, 3.0) * block_levels(key_of[7], (ATOMS, CH), ((0, 16),), -0.4, 0.0), -3.0, 3.0)
    atom_column = plant(jax.random.randint(key_of[8], (ATOMS,), 0, 4), jax.random.fold_in(key_of[8], 1), 0, 3).astype(jnp.int32)
    chan_count = plant(jax.random.randint(key_of[9], (ATOMS,), CH // 4, CH + 1), jax.random.fold_in(key_of[9], 1), CH // 4, CH).astype(jnp.int32)
    upper_column = plant(jax.random.randint(key_of[10], (ATOMS,), 0, 4), jax.random.fold_in(key_of[10], 1), 0, 3).astype(jnp.int32)
    return dict(wave_in=wave_in, mass_scale=mass_scale, potential=potential, elem_scale=elem_scale, stiffness=stiffness, proj_lower=proj_lower, proj_upper=proj_upper, kb_coef=kb_coef, atom_column=atom_column, chan_count=chan_count, upper_column=upper_column)


spectrum_center = 1.0
spectrum_half = 6.0
highest = lax.Precision.HIGHEST


def wrap_sides(planes):
    planes = jnp.concatenate([planes, planes[:, :1]], axis=1)
    return jnp.concatenate([planes, planes[:, :, :1]], axis=2)


def layer_blocks(layer_nodes, degree):
    points = degree + 1
    gathered = []
    for across in range(2):
        for column in range(2):
            portion = layer_nodes[:, across * degree:across * degree + points, column * degree:column * degree + points]
            gathered.append(portion.reshape(points * points * points, layer_nodes.shape[-1]))
    return jnp.stack(gathered)


def assemble_blocks(results, degree):
    points = degree + 1
    extent = 2 * degree + 1
    band_count = results.shape[-1]
    summed = jnp.zeros((extent, extent, extent, band_count), jnp.float32)
    number = 0
    for height in range(2):
        for across in range(2):
            for column in range(2):
                summed = summed.at[height * degree:height * degree + points, across * degree:across * degree + points, column * degree:column * degree + points].add(results[number].reshape(points, points, points, band_count))
                number = number + 1
    summed = summed[:, :, :-1].at[:, :, 0].add(summed[:, :, -1])
    summed = summed[:, :-1].at[:, 0].add(summed[:, -1])
    return summed


def split_slab(slab_nodes, next_plane, degree):
    bottom_blocks = layer_blocks(wrap_sides(slab_nodes[:degree + 1]), degree)
    top_blocks = layer_blocks(wrap_sides(jnp.concatenate([slab_nodes[degree:], next_plane[None]], axis=0)), degree)
    return bottom_blocks, top_blocks


def project_ref(projector, blocks, columns):
    chosen = jnp.take(blocks, columns, axis=0)
    return jnp.einsum("anc,anb->acb", projector.astype(jnp.float32), chosen.astype(jnp.float32), precision=highest)


def scatter_ref(projector, coef_block, columns):
    values = jnp.einsum("anc,acb->anb", projector.astype(jnp.float32), coef_block.astype(jnp.float32), precision=highest)
    onehot = (columns[:, None] == jnp.arange(4, dtype=jnp.int32)[None, :]).astype(jnp.float32)
    return jnp.einsum("ak,anb->knb", onehot, values, precision=highest)


def coefficient_sums(nodal_field, lower_slabs, upper_slabs, own_columns, upper_columns, degree):
    next_planes = jnp.roll(nodal_field[:, 0], -1, axis=0)

    def one_slab(slab_items):
        slab_nodes, next_plane, lower_proj, upper_proj, lower_cols, upper_cols = slab_items
        bottom_blocks, top_blocks = split_slab(slab_nodes, next_plane, degree)
        return project_ref(upper_proj, bottom_blocks, upper_cols), project_ref(lower_proj, top_blocks, lower_cols)

    held_part, own_part = lax.map(one_slab, (nodal_field, next_planes, lower_slabs, upper_slabs, own_columns, upper_columns))
    return own_part + jnp.roll(held_part, -1, axis=0)


def operator_ref(nodal_field, stiffness, scales, mass_nodes, local_potential, lower_slabs, upper_slabs, weights, own_columns, upper_columns, degree):
    coef_total = coefficient_sums(nodal_field, lower_slabs, upper_slabs, own_columns, upper_columns, degree)
    scaled = (coef_total * weights[..., None]).astype(jnp.bfloat16)
    below_scaled = jnp.roll(scaled, 1, axis=0)
    next_planes = jnp.roll(nodal_field[:, 0], -1, axis=0)
    stiff_f32 = stiffness.astype(jnp.float32)

    def one_slab(slab_items):
        slab_nodes, next_plane, slab_scale, lower_proj, upper_proj, own_coef, below_coef, lower_cols, upper_cols = slab_items
        bottom_blocks, top_blocks = split_slab(slab_nodes, next_plane, degree)
        local_bottom = jnp.einsum("ij,ejb->eib", stiff_f32, bottom_blocks.astype(jnp.float32), precision=highest) * slab_scale[:4, None, None]
        local_top = jnp.einsum("ij,ejb->eib", stiff_f32, top_blocks.astype(jnp.float32), precision=highest) * slab_scale[4:, None, None]
        results = jnp.concatenate([local_bottom + scatter_ref(upper_proj, below_coef, upper_cols), local_top + scatter_ref(lower_proj, own_coef, lower_cols)])
        summed = assemble_blocks(results, degree)
        return summed[:-1], summed[-1]

    inner_nodes, rim_planes = lax.map(one_slab, (nodal_field, next_planes, scales, lower_slabs, upper_slabs, scaled, below_scaled, own_columns, upper_columns))
    assembled = inner_nodes.at[:, 0].add(jnp.roll(rim_planes, 1, axis=0))
    return mass_nodes * (assembled + local_potential * nodal_field.astype(jnp.float32))


def reference(wave_in, mass_scale, potential, elem_scale, stiffness, proj_lower, proj_upper, kb_coef, atom_column, chan_count, upper_column):
    degree = ORDER
    extent = 2 * degree
    band_count = wave_in.shape[-1]
    nodal_field = wave_in.reshape(N_SPACE, extent, extent, extent, band_count)
    mass_nodes = mass_scale.reshape(N_SPACE, extent, extent, extent, 1)
    local_potential = potential.reshape(N_SPACE, extent, extent, extent, 1)
    scales = elem_scale.reshape(N_SPACE, 8)
    lower_slabs = proj_lower.reshape(N_SPACE, ATOM_DEV, ELN, CH)
    upper_slabs = proj_upper.reshape(N_SPACE, ATOM_DEV, ELN, CH)
    live_channels = (jnp.arange(CH, dtype=jnp.int32)[None, :] < chan_count[:, None]).astype(jnp.float32)
    weights = (kb_coef * live_channels).reshape(N_SPACE, ATOM_DEV, CH)
    own_columns = atom_column.reshape(N_SPACE, ATOM_DEV)
    upper_columns = upper_column.reshape(N_SPACE, ATOM_DEV)
    initial = nodal_field.astype(jnp.float32)
    scaled_start = (mass_nodes * initial).astype(jnp.bfloat16)
    image_one = operator_ref(scaled_start, stiffness, scales, mass_nodes, local_potential, lower_slabs, upper_slabs, weights, own_columns, upper_columns, degree)
    step_one = ((image_one - spectrum_center * initial) / spectrum_half).astype(jnp.bfloat16)
    scaled_step = (mass_nodes * step_one.astype(jnp.float32)).astype(jnp.bfloat16)
    image_two = operator_ref(scaled_step, stiffness, scales, mass_nodes, local_potential, lower_slabs, upper_slabs, weights, own_columns, upper_columns, degree)
    filtered = (2.0 * (image_two - spectrum_center * step_one.astype(jnp.float32)) / spectrum_half - initial).astype(jnp.bfloat16)
    coefficients = coefficient_sums(filtered, lower_slabs, upper_slabs, own_columns, upper_columns, degree)
    return filtered.reshape(wave_in.shape), coefficients.reshape(N_SPACE * ATOM_DEV, CH, band_count)
```

```python
import functools

import jax
import jax.numpy as jnp
import numpy as np
from jax import lax
from jax.experimental import pallas as pl
from jax.experimental.pallas import tpu as pltpu
from jax.sharding import PartitionSpec as P

spectrum_center = 1.0
spectrum_half = 6.0
f32 = jnp.float32
bf16 = jnp.bfloat16
LANES = 128
FACE = 96
CONST_ROWS = 16


def shifted(value, axis, steps):
    count = lax.axis_size(axis)
    pairs = [(source, (source + steps) % count) for source in range(count)]
    return lax.ppermute(value, axis, pairs)


def row_order(degree):
    points = degree + 1

    def natural(i, j, l):
        return (i * points + j) * points + l

    inner = range(degree)
    order = [natural(degree, j, l) for j in inner for l in inner]
    order += [natural(degree, degree, l) for l in inner]
    order += [natural(degree, j, degree) for j in inner]
    order += [natural(degree, degree, degree)] + [-1] * (degree - 1)
    order += [natural(i, j, l) for i in inner for j in inner for l in inner]
    order += [natural(i, degree, l) for i in inner for l in inner]
    order += [natural(i, j, degree) for i in inner for j in inner]
    order += [natural(i, degree, degree) for i in inner]
    used = len(order)
    order += [-1] * (-used % 256)
    return np.asarray(order, np.int32), used


def dot(a, b):
    return jnp.dot(a, b, preferred_element_type=f32)


def dot_nt(a, b):
    return lax.dot_general(a, b, (((1,), (1,)), ((), ())), preferred_element_type=f32)


def onehot_rows(perm, count):
    return (perm == lax.broadcasted_iota(jnp.int32, (perm.shape[0], count), 1)).astype(bf16)


class Mesh1:
    def __init__(self, degree, channels, used, padded):
        self.d = degree
        self.e = 2 * degree
        self.plane = self.e * self.e
        self.nodes = self.e * self.plane
        self.ch = channels
        self.face_groups = degree + 3
        self.used = used
        self.padded = padded

    def far(self, index):
        return (1 - index) * self.d

    def aligned(self, value):
        return value if isinstance(value, int) else pl.multiple_of(value, self.d)

    def face_places(self, base, a, b):
        d, e = self.d, self.e
        near = base + a * d * e + b * d
        places = [(self.aligned(near + j * e), 1) for j in range(d)]
        places.append((self.aligned(base + self.far(a) * e + b * d), 1))
        places.append((base + a * d * e + self.far(b), e))
        places.append((self.aligned(base + self.far(a) * e + self.far(b)), 0))
        return places

    def layer_places(self, base, a, b):
        d, e, plane = self.d, self.e, self.plane
        near = base + a * d * e + b * d
        places = [(self.aligned(near + i * plane + j * e), 1) for i in range(d) for j in range(d)]
        places += [
            (self.aligned(base + i * plane + self.far(a) * e + b * d), 1) for i in range(d)
        ]
        places += [(base + i * plane + a * d * e + self.far(b), e) for i in range(d)]
        places.append((base + self.far(a) * e + self.far(b), plane))
        return places

    def take(self, ref, place):
        start, stride = place
        if stride > 1:
            return ref[pl.ds(start, self.d, stride=stride), :]
        value = ref[pl.ds(start, self.d), :]
        if stride == 0:
            first = lax.broadcasted_iota(jnp.int32, value.shape, 0) == 0
            value = jnp.where(first, value, 0.0)
        return value

    def put_add(self, ref, place, value):
        start, stride = place
        if stride > 1:
            rows = pl.ds(start, self.d, stride=stride)
        else:
            rows = pl.ds(start, self.d)
            if stride == 0:
                first = lax.broadcasted_iota(jnp.int32, value.shape, 0) == 0
                value = jnp.where(first, value, 0.0)
        ref[rows, :] = ref[rows, :] + value

    def pack(self, ref, lane, groups, first_row=0):
        lanes = pl.ds(lane, LANES)
        for at in range(0, len(groups), 2):
            pair = jnp.concatenate([groups[at], groups[at + 1]], axis=0).astype(bf16)
            ref[pl.ds(first_row + at * self.d, 2 * self.d), lanes] = pair

    def gather_element(self, slab, ref, lane, base, a, b, with_face):
        d = self.d
        zero = jnp.zeros((d, LANES), f32)
        if with_face:
            groups = [self.take(slab, p) for p in self.face_places(base + d * self.plane, a, b)]
        else:
            groups = [zero] * self.face_groups
        groups += [self.take(slab, p) for p in self.layer_places(base, a, b)]
        groups += [zero] * ((self.padded - self.used) // d)
        self.pack(ref, lane, groups)

    def gather_face(self, slab, ref, lane, base, a, b):
        zero = jnp.zeros((self.d, LANES), f32)
        groups = [self.take(slab, p) for p in self.face_places(base, a, b)]
        groups += [zero] * (LANES // self.d - len(groups))
        self.pack(ref, lane, groups)

    def add_face(self, ref, base, a, b, load):
        for g, place in enumerate(self.face_places(base, a, b)):
            self.put_add(ref, place, load(g))

    def add_layer(self, ref, base, a, b, load, start=0):
        for g, place in enumerate(self.layer_places(base, a, b)):
            if g >= start:
                self.put_add(ref, place, load(self.face_groups + g))


def live_weights(kb, count):
    lane = lax.broadcasted_iota(jnp.int32, kb.shape, 1)
    return kb * jnp.where(lane < count, 1.0, 0.0)


def as_column(row):
    size = row.shape[1]
    shape = (size, size)
    eye = lax.broadcasted_iota(jnp.int32, shape, 0) == lax.broadcasted_iota(jnp.int32, shape, 1)
    return jnp.sum(jnp.where(eye, jnp.broadcast_to(row, shape), 0.0), axis=1, keepdims=True)


def split_element(column):
    return column // 2, column % 2


def outgoing(g, acol, ucol, scale, slab, x, kface, both_t, face_sums, up, down, own_out, held_out):
    d, ch = g.d, g.ch
    half = 4 * LANES
    own = dot(both_t[ch:, :], x[:, pl.ds(pl.multiple_of(half + acol * LANES, LANES), LANES)])
    held = dot(both_t[:ch, :], x[:, pl.ds(pl.multiple_of(ucol * LANES, LANES), LANES)])
    own_out[...] = own
    held_out[...] = held
    sums = dot(kface, x[:, half:])
    face_sums[...] = jnp.zeros_like(face_sums)
    for a in range(2):
        for b in range(2):
            lane = (a * 2 + b) * LANES
            part = sums[:, lane : lane + LANES] * scale[1, a, b]
            g.add_face(face_sums, 0, a, b, lambda k: part[k * d : (k + 1) * d])
    up[: g.plane, :] = face_sums[...].astype(bf16)
    up[g.plane : g.plane + ch, :] = own.astype(bf16)
    down[: g.plane, :] = slab[: g.plane, :].astype(bf16)
    down[g.plane :, :] = held.astype(bf16)


def gather_all(g, slab, x):
    for a in range(2):
        for b in range(2):
            lane = (a * 2 + b) * LANES
            g.gather_element(slab, x, lane, 0, a, b, True)
            g.gather_element(slab, x, 4 * LANES + lane, g.d * g.plane, a, b, False)


def start_kernel(
    g, acol, ucol, count, scale, wave, mass, perm, stiff, plow, pup, kb,
    slab, x, mass_wide, both, both_t, own_out, held_out, up, down, face_sums,
):
    ch = g.ch
    mass_t = mass[...].T
    for p in range(g.e):
        wide = jnp.broadcast_to(mass_t[:, p : p + 1], (g.plane, LANES))
        rows = pl.ds(p * g.plane, g.plane)
        mass_wide[rows, :] = wide
        start = wave[p].astype(f32).reshape(g.plane, LANES)
        slab[rows, :] = (wide * start).astype(bf16).astype(f32)
    pick = onehot_rows(perm[...], stiff.shape[0])
    pair = jnp.concatenate([pup[0], plow[0]], axis=1)
    ordered = dot(pick, pair).astype(bf16)
    both[...] = ordered
    turned = ordered.astype(f32).T.astype(bf16)
    both_t[...] = turned
    kface = dot_nt(dot(pick[:FACE], stiff[...]).astype(bf16), pick).astype(bf16)
    gather_all(g, slab, x)
    outgoing(g, acol[0], ucol[0], scale, slab, x, kface, both_t, face_sums, up, down, own_out, held_out)
    at = g.plane + ch
    up[at : at + FACE, :] = jnp.zeros((FACE, LANES), bf16)
    up[at : at + FACE, :ch] = ordered[:FACE, ch:]
    shape = (CONST_ROWS, LANES)
    row = lax.broadcasted_iota(jnp.int32, shape, 0)
    values = jnp.zeros(shape, f32)
    for k in range(4):
        chosen = jnp.where(acol[0] == k, 1.0, 0.0)
        values = jnp.where(row == k, chosen, values)
        full = jnp.full(shape, scale[1, k // 2, k % 2], f32)
        high = full.astype(bf16).astype(f32)
        values = jnp.where(row == 4 + k, high, values)
        values = jnp.where(row == 8 + k, full - high, values)
    weights = live_weights(kb[...], count[0])
    weights = jnp.concatenate([weights, jnp.zeros((1, LANES - ch), f32)], axis=1)
    full = jnp.broadcast_to(weights, shape)
    high = full.astype(bf16).astype(f32)
    values = jnp.where(row == 12, high, values)
    values = jnp.where(row == 13, full - high, values)
    up[at + FACE :, :] = values.astype(bf16)


def order_kernel(stiff, perm, ordered):
    pick = onehot_rows(perm[...], stiff.shape[0])
    part = perm.shape[0] // 3
    for k in range(3):
        rows = slice(k * part, (k + 1) * part)
        half = dot(pick[rows], stiff[...]).astype(bf16)
        ordered[rows, :] = dot_nt(half, pick).astype(bf16)


def bulk_kernel(g, scale, ordered, x, slab, potential, total, face_own, x_face, z):
    d = g.d
    pot_t = potential[...].T
    for p in range(g.e):
        wide = jnp.broadcast_to(pot_t[:, p : p + 1], (g.plane, LANES))
        rows = pl.ds(p * g.plane, g.plane)
        total[rows, :] = wide * slab[rows, :]
    for layer in range(2):
        for a in range(2):
            lane = (layer * 2 + a) * 2 * LANES
            z[...] = dot(ordered[: g.used, :], x[:, lane : lane + 2 * LANES])
            for b in range(2):
                factor = scale[layer, a, b]

                def load(k):
                    return z[k * d : (k + 1) * d, b * LANES : (b + 1) * LANES] * factor

                base = layer * d * g.plane
                if layer == 0:
                    g.add_face(total, d * g.plane, a, b, load)
                g.add_layer(total, base, a, b, load)
    for a in range(2):
        for b in range(2):
            g.gather_face(slab, x_face, (a * 2 + b) * LANES, 0, a, b)
    face_own[...] = dot(ordered[:FACE, :LANES], x_face[...])


def complete(
    g, acol, ucol, count, scale, total, face_own, x_face, ordered, both, both_t, own, held, kb,
    face_low, consts, up, down, sums, next_plane, x_next,
):
    d, ch = g.d, g.ch
    next_plane[...] = down[: g.plane, :].astype(f32)
    for a in range(2):
        for b in range(2):
            g.gather_face(next_plane, x_next, (a * 2 + b) * LANES, 0, a, b)
    mine = own[...] + down[g.plane :, :].astype(f32)
    column = pl.ds(pl.multiple_of(acol * LANES, LANES), LANES)
    mine = mine + dot(both_t[ch:, :LANES], x_next[:, column])
    mine = (as_column(live_weights(kb[...], count)) * mine).astype(bf16)
    const = consts.astype(f32)
    one_hot = [const[k : k + 1, :] for k in range(4)]
    scale_low = [const[4 + k : 5 + k, :] + const[8 + k : 9 + k, :] for k in range(4)]
    weights_low = as_column(const[12:13, :ch] + const[13:14, :ch])
    low = up[g.plane : g.plane + ch, :].astype(f32) + held[...]
    low = low + dot_chosen(face_low, x_face, one_hot)
    low = (weights_low * low).astype(bf16)
    lifted_low = dot(face_low, low)
    upper = dot(ordered[: g.used, :LANES], x_next[...])
    lifted = dot(both[: g.used, ch:], mine)
    half = d * g.plane
    sums[:half, :] = total[:half, :]
    for a in range(2):
        for b in range(2):
            lane = (a * 2 + b) * LANES
            here = jnp.where(acol == a * 2 + b, 1.0, 0.0)
            factor = scale[1, a, b]

            def load(k):
                rows = slice(k * d, (k + 1) * d)
                return upper[rows, lane : lane + LANES] * factor + lifted[rows] * here

            near = half + a * d * g.e + b * d
            for i in range(d):
                for j in range(d):
                    rows = pl.ds(near + i * g.plane + j * g.e, d)
                    sums[rows, :] = total[rows, :] + load(g.face_groups + i * d + j)
    for a in range(2):
        for b in range(2):
            lane = (a * 2 + b) * LANES
            here = jnp.where(acol == a * 2 + b, 1.0, 0.0)
            factor = scale[1, a, b]

            def load(k):
                rows = slice(k * d, (k + 1) * d)
                return upper[rows, lane : lane + LANES] * factor + lifted[rows] * here

            g.add_layer(sums, half, a, b, load, start=d * d)
    sums[: g.plane, :] = sums[: g.plane, :] + up[: g.plane, :].astype(f32)
    for a in range(2):
        for b in range(2):
            k4 = a * 2 + b
            part = face_own[:, k4 * LANES : (k4 + 1) * LANES] * scale_low[k4]
            part = part + lifted_low * one_hot[k4]
            g.add_face(sums, 0, a, b, lambda k: part[k * d : (k + 1) * d])
    lifted_up = dot(both[: g.used, :ch], low)
    a, b = split_element(ucol)

    def load_up(k):
        return lifted_up[k * d : (k + 1) * d]

    g.add_face(sums, half, a, b, load_up)
    g.add_layer(sums, 0, a, b, load_up)


def dot_chosen(face, x_face, one_hot):
    rows = face.shape[0]
    chosen = jnp.zeros((rows, LANES), f32)
    for k in range(4):
        chosen = chosen + x_face[:rows, k * LANES : (k + 1) * LANES].astype(f32) * one_hot[k]
    face_t = face.astype(f32).T.astype(bf16)
    return dot(face_t, chosen.astype(bf16))


def middle_kernel(
    g, acol, ucol, count, scale, wave, mass_wide, total, face_own, x_face, ordered, both, both_t,
    own, held, kb, up, down,
    slab, x, step, own_out, held_out, up_out, down_out,
    sums, next_plane, x_next, face_sums,
):
    at = g.plane + g.ch
    complete(
        g, acol[0], ucol[0], count[0], scale, total, face_own, x_face, ordered, both, both_t, own, held, kb,
        up[at : at + FACE, : g.ch], up[at + FACE :, :], up, down, sums, next_plane, x_next,
    )
    for p in range(g.e):
        rows = pl.ds(p * g.plane, g.plane)
        wide = mass_wide[rows, :]
        before = wave[p].astype(f32).reshape(g.plane, LANES)
        image = wide * sums[rows, :]
        one = ((image - spectrum_center * before) * (1.0 / spectrum_half)).astype(bf16)
        step[rows, :] = one
        slab[rows, :] = (wide * one.astype(f32)).astype(bf16).astype(f32)
    gather_all(g, slab, x)
    outgoing(
        g, acol[0], ucol[0], scale, slab, x, ordered[:FACE, :], both_t, face_sums, up_out, down_out,
        own_out, held_out,
    )


def last_kernel(
    g, acol, ucol, count, scale, wave, mass_wide, total, face_own, x_face, ordered, both, both_t,
    own, held, kb, up_first, up, down, step,
    filtered, own_out, held_out,
    sums, next_plane, x_next, x_pair,
):
    at = g.plane + g.ch
    d, ch = g.d, g.ch
    face_low = up_first[at : at + FACE, :ch]
    consts = up_first[at + FACE :, :]
    complete(
        g, acol[0], ucol[0], count[0], scale, total, face_own, x_face, ordered, both, both_t, own, held, kb,
        face_low, consts, up, down, sums, next_plane, x_next,
    )
    for p in range(g.e):
        rows = pl.ds(p * g.plane, g.plane)
        before = wave[p].astype(f32).reshape(g.plane, LANES)
        image = mass_wide[rows, :] * sums[rows, :]
        one = step[rows, :].astype(f32)
        new = (image - spectrum_center * one) * (2.0 / spectrum_half) - before
        new = new.astype(bf16)
        filtered[p] = new.reshape(g.e, g.e, LANES)
        sums[rows, :] = new.astype(f32)
    a, b = split_element(acol[0])
    g.gather_element(sums, x_pair, 0, d * g.plane, a, b, False)
    own_out[...] = dot(both_t[ch:, :], x_pair[:, :LANES])
    a, b = split_element(ucol[0])
    g.gather_element(sums, x_pair, LANES, 0, a, b, True)
    for a in range(2):
        for b in range(2):
            g.gather_face(sums, x_next, (a * 2 + b) * LANES, 0, a, b)
    const = consts.astype(f32)
    one_hot = [const[k : k + 1, :] for k in range(4)]
    held_out[...] = dot(both_t[:ch, :], x_pair[:, LANES:]) + dot_chosen(face_low, x_next, one_hot)


def call(kernel, name, operands, outs, scratch, flops, limit=24 << 20):
    smem = pl.BlockSpec(memory_space=pltpu.SMEM)
    vmem = pl.BlockSpec(memory_space=pltpu.VMEM)
    specs = [smem if value.ndim == 1 or value.shape == (2, 2, 2) else vmem for value in operands]
    moved = sum(v.size * v.dtype.itemsize for v in operands)
    return pl.pallas_call(
        kernel,
        name=name,
        out_shape=[jax.ShapeDtypeStruct(s, t) for s, t in outs],
        in_specs=specs,
        out_specs=[vmem] * len(outs),
        scratch_shapes=[pltpu.VMEM(s, t) for s, t in scratch],
        compiler_params=pltpu.CompilerParams(vmem_limit_bytes=limit),
        cost_estimate=pl.CostEstimate(flops=flops, bytes_accessed=moved, transcendentals=0),
    )(*operands)


def per_device(
    wave_in, mass_scale, potential, elem_scale, stiffness, proj_lower, proj_upper, kb_coef,
    atom_column, chan_count, upper_column,
):
    extent = wave_in.shape[0]
    degree = extent // 2
    ch = kb_coef.shape[-1]
    order, used = row_order(degree)
    padded = order.shape[0]
    perm = jnp.asarray(order)[:, None]
    g = Mesh1(degree, ch, used, padded)
    plane, nodes = g.plane, g.nodes
    scalars = (atom_column, upper_column, chan_count, elem_scale)
    part = ((ch, LANES), f32)
    slab_s, x_s = ((nodes, LANES), f32), ((padded, 8 * LANES), bf16)
    down_s, up_s = ((plane + ch, LANES), bf16), ((plane + ch, LANES), bf16)
    up_first_s = ((plane + ch + FACE + CONST_ROWS, LANES), bf16)
    plane_s, face_s = ((plane, LANES), f32), ((LANES, 4 * LANES), bf16)

    slab, x, mass_wide, both, both_t, own, held, up, down = call(
        functools.partial(start_kernel, g), "start",
        (*scalars, wave_in, mass_scale, perm, stiffness, proj_lower, proj_upper, kb_coef),
        [slab_s, x_s, slab_s, ((padded, 2 * ch), bf16), ((2 * ch, padded), bf16), part, part, up_first_s, down_s],
        [plane_s], 10**8,
    )
    up_first = shifted(up, "space", 1)
    down = shifted(down, "space", -1)
    (ordered,) = call(order_kernel, "order", (stiffness, perm), [((padded, padded), bf16)], [], 2 * 10**9)

    def bulk(slab, x):
        return call(
            functools.partial(bulk_kernel, g), "bulk", (elem_scale, ordered, x, slab, potential),
            [slab_s, ((FACE, 4 * LANES), f32), face_s], [((used, 2 * LANES), f32)], 2 * 10**9,
        )

    total, face_own, x_face = bulk(slab, x)
    shared = (ordered, both, both_t)
    slab, x, step, own, held, up, down = call(
        functools.partial(middle_kernel, g), "middle",
        (*scalars, wave_in, mass_wide, total, face_own, x_face, *shared, own, held, kb_coef, up_first, down),
        [slab_s, x_s, ((nodes, LANES), bf16), part, part, up_s, down_s],
        [slab_s, plane_s, face_s, plane_s], 10**8,
    )
    up = shifted(up, "space", 1)
    down = shifted(down, "space", -1)
    total, face_own, x_face = bulk(slab, x)
    filtered, own, held = call(
        functools.partial(last_kernel, g), "last",
        (*scalars, wave_in, mass_wide, total, face_own, x_face, *shared, own, held, kb_coef, up_first, up, down, step),
        [(wave_in.shape, bf16), part, part],
        [slab_s, plane_s, face_s, ((padded, 2 * LANES), bf16)], 10**8,
    )
    return filtered, (own + shifted(held, "space", -1))[None]


def solution(mesh):
    in_specs = (
        P("space", None, None, "band"),
        P("space", None),
        P("space", None),
        P("space", None, None),
        P(),
        P("space", None, None),
        P("space", None, None),
        P("space", None),
        P("space"),
        P("space"),
        P("space"),
    )
    out_specs = (P("space", None, None, "band"), P("space", None, "band"))
    return jax.shard_map(
        per_device, mesh=mesh, in_specs=in_specs, out_specs=out_specs, check_vma=False
    )
```

```python
import functools

import jax
import jax.numpy as jnp
import numpy as np
from jax import lax
from jax.experimental import pallas as pl
from jax.experimental.pallas import tpu as pltpu
from jax.sharding import PartitionSpec as P

spectrum_center = 1.0
spectrum_half = 6.0
f32 = jnp.float32
bf16 = jnp.bfloat16
LANES = 128
FACE = 96
CONST_ROWS = 16


def shifted(value, axis, steps):
    count = lax.axis_size(axis)
    pairs = [(source, (source + steps) % count) for source in range(count)]
    return lax.ppermute(value, axis, pairs)


def swapped(inner, outer, axis):
    count = lax.axis_size(axis)
    within = [(source, source ^ 1) for source in range(count)]
    across = [(source, (source + (1 if source % 2 else -1)) % count) for source in range(count)]
    return lax.ppermute(inner, axis, within), lax.ppermute(outer, axis, across)


def is_odd():
    return lax.rem(lax.axis_index("space"), 2) == 1


def post(up, down, inner, outer):
    @pl.when(is_odd())
    def _():
        inner[: down.shape[0], :] = down[...]
        outer[: up.shape[0], :] = up[...]

    @pl.when(jnp.logical_not(is_odd()))
    def _():
        inner[: up.shape[0], :] = up[...]
        outer[: down.shape[0], :] = down[...]


def collect(inner, outer, up, down):
    @pl.when(is_odd())
    def _():
        up[...] = inner[: up.shape[0], :]
        down[...] = outer[: down.shape[0], :]

    @pl.when(jnp.logical_not(is_odd()))
    def _():
        up[...] = outer[: up.shape[0], :]
        down[...] = inner[: down.shape[0], :]


def row_order(degree):
    points = degree + 1

    def natural(i, j, l):
        return (i * points + j) * points + l

    inner = range(degree)
    order = [natural(degree, j, l) for j in inner for l in inner]
    order += [natural(degree, degree, l) for l in inner]
    order += [natural(degree, j, degree) for j in inner]
    order += [natural(degree, degree, degree)] + [-1] * (degree - 1)
    order += [natural(i, j, l) for i in inner for j in inner for l in inner]
    order += [natural(i, degree, l) for i in inner for l in inner]
    order += [natural(i, j, degree) for i in inner for j in inner]
    order += [natural(i, degree, degree) for i in inner]
    used = len(order)
    order += [-1] * (-used % 256)
    return np.asarray(order, np.int32), used


def dot(a, b):
    return jnp.dot(a, b, preferred_element_type=f32)


def dot_nt(a, b):
    return lax.dot_general(a, b, (((1,), (1,)), ((), ())), preferred_element_type=f32)


def onehot_rows(perm, count):
    rows = perm.shape[1]
    column = jnp.broadcast_to(perm, (8, rows)).T[:, :1]
    lane = lax.broadcasted_iota(jnp.int32, (rows, count), 1).astype(f32)
    return (column == lane).astype(bf16)


class Mesh1:
    def __init__(self, degree, channels, used, padded):
        self.d = degree
        self.e = 2 * degree
        self.plane = self.e * self.e
        self.nodes = self.e * self.plane
        self.ch = channels
        self.face_groups = degree + 3
        self.used = used
        self.padded = padded

    def far(self, index):
        return (1 - index) * self.d

    def aligned(self, value):
        return value if isinstance(value, int) else pl.multiple_of(value, self.d)

    def face_places(self, base, a, b):
        d, e = self.d, self.e
        near = base + a * d * e + b * d
        places = [(self.aligned(near + j * e), 1) for j in range(d)]
        places.append((self.aligned(base + self.far(a) * e + b * d), 1))
        places.append((base + a * d * e + self.far(b), e))
        places.append((self.aligned(base + self.far(a) * e + self.far(b)), 0))
        return places

    def layer_places(self, base, a, b):
        d, e, plane = self.d, self.e, self.plane
        near = base + a * d * e + b * d
        places = [(self.aligned(near + i * plane + j * e), 1) for i in range(d) for j in range(d)]
        places += [
            (self.aligned(base + i * plane + self.far(a) * e + b * d), 1) for i in range(d)
        ]
        places += [(base + i * plane + a * d * e + self.far(b), e) for i in range(d)]
        places.append((base + self.far(a) * e + self.far(b), plane))
        return places

    def take(self, ref, place):
        start, stride = place
        if stride > 1:
            return ref[pl.ds(start, self.d, stride=stride), :]
        value = ref[pl.ds(start, self.d), :]
        if stride == 0:
            first = lax.broadcasted_iota(jnp.int32, value.shape, 0) == 0
            value = jnp.where(first, value, 0.0)
        return value

    def put_add(self, ref, place, value):
        start, stride = place
        if stride > 1:
            rows = pl.ds(start, self.d, stride=stride)
        else:
            rows = pl.ds(start, self.d)
            if stride == 0:
                first = lax.broadcasted_iota(jnp.int32, value.shape, 0) == 0
                value = jnp.where(first, value, 0.0)
        ref[rows, :] = ref[rows, :] + value

    def pack(self, ref, lane, groups, first_row=0):
        lanes = pl.ds(lane, LANES)
        for at in range(0, len(groups), 2):
            pair = jnp.concatenate([groups[at], groups[at + 1]], axis=0).astype(bf16)
            ref[pl.ds(first_row + at * self.d, 2 * self.d), lanes] = pair

    def gather_element(self, slab, ref, lane, base, a, b, with_face):
        d = self.d
        zero = jnp.zeros((d, LANES), f32)
        if with_face:
            groups = [self.take(slab, p) for p in self.face_places(base + d * self.plane, a, b)]
        else:
            groups = [zero] * self.face_groups
        groups += [self.take(slab, p) for p in self.layer_places(base, a, b)]
        groups += [zero] * ((self.padded - self.used) // d)
        self.pack(ref, lane, groups)

    def gather_face(self, slab, ref, lane, base, a, b):
        zero = jnp.zeros((self.d, LANES), f32)
        groups = [self.take(slab, p) for p in self.face_places(base, a, b)]
        groups += [zero] * (LANES // self.d - len(groups))
        self.pack(ref, lane, groups)

    def add_face(self, ref, base, a, b, load):
        for g, place in enumerate(self.face_places(base, a, b)):
            self.put_add(ref, place, load(g))

    def add_layer(self, ref, base, a, b, load, start=0):
        for g, place in enumerate(self.layer_places(base, a, b)):
            if g >= start:
                self.put_add(ref, place, load(self.face_groups + g))


def live_weights(kb, count):
    lane = lax.broadcasted_iota(jnp.int32, kb.shape, 1)
    return kb * jnp.where(lane < count, 1.0, 0.0)


def as_column(row):
    size = row.shape[1]
    shape = (size, size)
    eye = lax.broadcasted_iota(jnp.int32, shape, 0) == lax.broadcasted_iota(jnp.int32, shape, 1)
    return jnp.sum(jnp.where(eye, jnp.broadcast_to(row, shape), 0.0), axis=1, keepdims=True)


def split_element(column):
    return column // 2, column % 2


def outgoing(g, acol, ucol, scale, slab, x, kface, both_t, face_sums, up, down, own_out, held_out):
    d, ch = g.d, g.ch
    half = 4 * LANES
    own = dot(both_t[ch:, :], x[:, pl.ds(pl.multiple_of(half + acol * LANES, LANES), LANES)])
    held = dot(both_t[:ch, :], x[:, pl.ds(pl.multiple_of(ucol * LANES, LANES), LANES)])
    own_out[...] = own
    held_out[...] = held
    sums = dot(kface, x[:, half:])
    face_sums[...] = jnp.zeros_like(face_sums)
    for a in range(2):
        for b in range(2):
            lane = (a * 2 + b) * LANES
            part = sums[:, lane : lane + LANES] * scale[4 + a * 2 + b : 5 + a * 2 + b, :]
            g.add_face(face_sums, 0, a, b, lambda k: part[k * d : (k + 1) * d])
    up[: g.plane, :] = face_sums[...].astype(bf16)
    up[g.plane : g.plane + ch, :] = own.astype(bf16)
    down[: g.plane, :] = slab[: g.plane, :].astype(bf16)
    down[g.plane :, :] = held.astype(bf16)


def gather_all(g, slab, x):
    for a in range(2):
        for b in range(2):
            lane = (a * 2 + b) * LANES
            g.gather_element(slab, x, lane, 0, a, b, True)
            g.gather_element(slab, x, 4 * LANES + lane, g.d * g.plane, a, b, False)


def start_kernel(
    g, acol, ucol, count, wave_hbm, mass_hbm, scale_hbm, stiff_hbm, low_hbm, up_hbm, kb_hbm, perm_hbm, pot_hbm,
    slab, x, mass_wide, wave, stiff, scale, perm, pot, kb, both, both_t, own_out, held_out, inner, outer,
    face_sums, up, down, mass, scale_in, proj, sems,
):
    ch = g.ch
    copies = [
        pltpu.make_async_copy(source, target, sems.at[k])
        for k, (source, target) in enumerate((
            (mass_hbm, mass), (wave_hbm, wave), (up_hbm.at[0], proj.at[:ch]), (low_hbm.at[0], proj.at[ch:]),
            (perm_hbm, perm), (stiff_hbm, stiff), (scale_hbm, scale_in), (kb_hbm, kb), (pot_hbm, pot),
        ))
    ]
    for copy in copies:
        copy.start()
    copies[0].wait()
    copies[1].wait()
    mass_t = mass[...].T
    for p in range(g.e):
        wide = jnp.broadcast_to(mass_t[:, p : p + 1], (g.plane, LANES))
        rows = pl.ds(p * g.plane, g.plane)
        mass_wide[rows, :] = wide
        start = wave[p].astype(f32).reshape(g.plane, LANES)
        slab[rows, :] = (wide * start).astype(bf16).astype(f32)
    gather_all(g, slab, x)
    for copy in copies[2:]:
        copy.wait()
    for k in range(8):
        one = scale_in[k // 4, k % 4 // 2 : k % 4 // 2 + 1, k % 2 : k % 2 + 1]
        scale[k : k + 1, :] = jnp.broadcast_to(one, (1, LANES))
    pick = onehot_rows(perm[...], stiff.shape[0])
    ordered = dot_nt(proj[...], pick)
    both_t[...] = ordered.astype(bf16)
    ordered = ordered.T.astype(bf16)
    both[...] = ordered
    kface = dot_nt(dot(pick[:FACE], stiff[...]).astype(bf16), pick).astype(bf16)
    outgoing(g, acol[0], ucol[0], scale, slab, x, kface, both_t, face_sums, up, down, own_out, held_out)
    at = g.plane + ch
    up[at : at + FACE, :] = jnp.zeros((FACE, LANES), bf16)
    up[at : at + FACE, :ch] = ordered[:FACE, ch:]
    shape = (CONST_ROWS, LANES)
    row = lax.broadcasted_iota(jnp.int32, shape, 0)
    values = jnp.zeros(shape, f32)
    for k in range(4):
        chosen = jnp.where(acol[0] == k, 1.0, 0.0)
        values = jnp.where(row == k, chosen, values)
        full = jnp.broadcast_to(scale[4 + k : 5 + k, :], shape)
        high = full.astype(bf16).astype(f32)
        values = jnp.where(row == 4 + k, high, values)
        values = jnp.where(row == 8 + k, full - high, values)
    weights = live_weights(kb[...], count[0])
    weights = jnp.concatenate([weights, jnp.zeros((1, LANES - ch), f32)], axis=1)
    full = jnp.broadcast_to(weights, shape)
    high = full.astype(bf16).astype(f32)
    values = jnp.where(row == 12, high, values)
    values = jnp.where(row == 13, full - high, values)
    up[at + FACE :, :] = values.astype(bf16)
    post(up, down, inner, outer)


def order_kernel(stiff, perm, ordered):
    pick = onehot_rows(perm[...], stiff.shape[0])
    part = perm.shape[1] // 3
    for k in range(3):
        rows = slice(k * part, (k + 1) * part)
        half = dot(pick[rows], stiff[...]).astype(bf16)
        ordered[rows, :] = dot_nt(half, pick).astype(bf16)


def bulk_kernel(g, scale, ordered, x, slab, potential, total, face_own, x_face, z):
    d = g.d
    pot_t = potential[...].T
    for p in range(g.e):
        wide = jnp.broadcast_to(pot_t[:, p : p + 1], (g.plane, LANES))
        rows = pl.ds(p * g.plane, g.plane)
        total[rows, :] = wide * slab[rows, :]
    for layer in range(2):
        for a in range(2):
            lane = (layer * 2 + a) * 2 * LANES
            z[...] = dot(ordered[: g.used, :], x[:, lane : lane + 2 * LANES])
            for b in range(2):
                factor = scale[layer * 4 + a * 2 + b : layer * 4 + a * 2 + b + 1, :]

                def load(k):
                    return z[k * d : (k + 1) * d, b * LANES : (b + 1) * LANES] * factor

                base = layer * d * g.plane
                if layer == 0:
                    g.add_face(total, d * g.plane, a, b, load)
                g.add_layer(total, base, a, b, load)
    for a in range(2):
        for b in range(2):
            g.gather_face(slab, x_face, (a * 2 + b) * LANES, 0, a, b)
    face_own[...] = dot(ordered[:FACE, :LANES], x_face[...])


def complete(
    g, acol, ucol, count, scale, total, face_own, x_face, ordered, both, both_t, own, held, kb,
    face_low, consts, up, down, sums, next_plane, x_next,
):
    d, ch = g.d, g.ch
    next_plane[...] = down[: g.plane, :].astype(f32)
    for a in range(2):
        for b in range(2):
            g.gather_face(next_plane, x_next, (a * 2 + b) * LANES, 0, a, b)
    mine = own[...] + down[g.plane :, :].astype(f32)
    column = pl.ds(pl.multiple_of(acol * LANES, LANES), LANES)
    mine = mine + dot(both_t[ch:, :LANES], x_next[:, column])
    mine = (as_column(live_weights(kb[...], count)) * mine).astype(bf16)
    const = consts.astype(f32)
    one_hot = [const[k : k + 1, :] for k in range(4)]
    scale_low = [const[4 + k : 5 + k, :] + const[8 + k : 9 + k, :] for k in range(4)]
    weights_low = as_column(const[12:13, :ch] + const[13:14, :ch])
    low = up[g.plane : g.plane + ch, :].astype(f32) + held[...]
    low = low + dot_chosen(face_low, x_face, one_hot)
    low = (weights_low * low).astype(bf16)
    lifted_low = dot(face_low, low)
    upper = dot(ordered[: g.used, :LANES], x_next[...])
    lifted = dot(both[: g.used, ch:], mine)
    half = d * g.plane
    sums[:half, :] = total[:half, :]
    for a in range(2):
        for b in range(2):
            lane = (a * 2 + b) * LANES
            here = jnp.where(acol == a * 2 + b, 1.0, 0.0)
            factor = scale[4 + a * 2 + b : 5 + a * 2 + b, :]

            def load(k):
                rows = slice(k * d, (k + 1) * d)
                return upper[rows, lane : lane + LANES] * factor + lifted[rows] * here

            near = half + a * d * g.e + b * d
            for i in range(d):
                for j in range(d):
                    rows = pl.ds(near + i * g.plane + j * g.e, d)
                    sums[rows, :] = total[rows, :] + load(g.face_groups + i * d + j)
    for a in range(2):
        for b in range(2):
            lane = (a * 2 + b) * LANES
            here = jnp.where(acol == a * 2 + b, 1.0, 0.0)
            factor = scale[4 + a * 2 + b : 5 + a * 2 + b, :]

            def load(k):
                rows = slice(k * d, (k + 1) * d)
                return upper[rows, lane : lane + LANES] * factor + lifted[rows] * here

            g.add_layer(sums, half, a, b, load, start=d * d)
    sums[: g.plane, :] = sums[: g.plane, :] + up[: g.plane, :].astype(f32)
    for a in range(2):
        for b in range(2):
            k4 = a * 2 + b
            part = face_own[:, k4 * LANES : (k4 + 1) * LANES] * scale_low[k4]
            part = part + lifted_low * one_hot[k4]
            g.add_face(sums, 0, a, b, lambda k: part[k * d : (k + 1) * d])
    lifted_up = dot(both[: g.used, :ch], low)
    a, b = split_element(ucol)

    def load_up(k):
        return lifted_up[k * d : (k + 1) * d]

    g.add_face(sums, half, a, b, load_up)
    g.add_layer(sums, 0, a, b, load_up)


def dot_chosen(face, x_face, one_hot):
    rows = face.shape[0]
    chosen = jnp.zeros((rows, LANES), f32)
    for k in range(4):
        chosen = chosen + x_face[:rows, k * LANES : (k + 1) * LANES].astype(f32) * one_hot[k]
    face_t = face.astype(f32).T.astype(bf16)
    return dot(face_t, chosen.astype(bf16))


def middle_kernel(
    g, acol, ucol, count, scale, wave, mass_wide, total, face_own, x_face, ordered, both, both_t,
    own, held, kb, inner, outer,
    slab, x, step, own_out, held_out, inner_out, outer_out, kept,
    sums, next_plane, x_next, face_sums, up, down, up_out, down_out,
):
    at = g.plane + g.ch
    collect(inner, outer, up, down)
    kept[...] = up[at:, :]
    complete(
        g, acol[0], ucol[0], count[0], scale, total, face_own, x_face, ordered, both, both_t, own, held, kb,
        up[at : at + FACE, : g.ch], up[at + FACE :, :], up, down, sums, next_plane, x_next,
    )
    for p in range(g.e):
        rows = pl.ds(p * g.plane, g.plane)
        wide = mass_wide[rows, :]
        before = wave[p].astype(f32).reshape(g.plane, LANES)
        image = wide * sums[rows, :]
        one = ((image - spectrum_center * before) * (1.0 / spectrum_half)).astype(bf16)
        step[rows, :] = one
        slab[rows, :] = (wide * one.astype(f32)).astype(bf16).astype(f32)
    gather_all(g, slab, x)
    outgoing(
        g, acol[0], ucol[0], scale, slab, x, ordered[:FACE, :], both_t, face_sums, up_out, down_out,
        own_out, held_out,
    )
    post(up_out, down_out, inner_out, outer_out)


def last_kernel(
    g, acol, ucol, count, scale, wave, mass_wide, total, face_own, x_face, ordered, both, both_t,
    own, held, kb, kept, inner, outer, step,
    filtered, own_out, held_out,
    sums, next_plane, x_next, x_pair, up, down,
):
    d, ch = g.d, g.ch
    collect(inner, outer, up, down)
    face_low = kept[:FACE, :ch]
    consts = kept[FACE:, :]
    complete(
        g, acol[0], ucol[0], count[0], scale, total, face_own, x_face, ordered, both, both_t, own, held, kb,
        face_low, consts, up, down, sums, next_plane, x_next,
    )
    for p in range(g.e):
        rows = pl.ds(p * g.plane, g.plane)
        before = wave[p].astype(f32).reshape(g.plane, LANES)
        image = mass_wide[rows, :] * sums[rows, :]
        one = step[rows, :].astype(f32)
        new = (image - spectrum_center * one) * (2.0 / spectrum_half) - before
        new = new.astype(bf16)
        filtered[p] = new.reshape(g.e, g.e, LANES)
        sums[rows, :] = new.astype(f32)
    a, b = split_element(acol[0])
    g.gather_element(sums, x_pair, 0, d * g.plane, a, b, False)
    own_out[...] = dot(both_t[ch:, :], x_pair[:, :LANES])
    a, b = split_element(ucol[0])
    g.gather_element(sums, x_pair, LANES, 0, a, b, True)
    for a in range(2):
        for b in range(2):
            g.gather_face(sums, x_next, (a * 2 + b) * LANES, 0, a, b)
    const = consts.astype(f32)
    one_hot = [const[k : k + 1, :] for k in range(4)]
    held_out[...] = dot(both_t[:ch, :], x_pair[:, LANES:]) + dot_chosen(face_low, x_next, one_hot)


def call(kernel, name, scalars, operands, outs, scratch, flops, limit=24 << 20, hbm=False):
    smem = pl.BlockSpec(memory_space=pltpu.SMEM)
    vmem = pl.BlockSpec(memory_space=pltpu.VMEM)
    far = pl.BlockSpec(memory_space=pltpu.MemorySpace.HBM)
    moved = sum(v.size * v.dtype.itemsize for v in operands)
    if hbm:
        operands = [pltpu.with_memory_space_constraint(v, pltpu.MemorySpace.HBM) for v in operands]
    return pl.pallas_call(
        kernel,
        name=name,
        out_shape=[jax.ShapeDtypeStruct(s, t) for s, t in outs],
        in_specs=[smem] * len(scalars) + [far if hbm else vmem] * len(operands),
        out_specs=[vmem] * len(outs),
        scratch_shapes=[s if isinstance(s, pltpu.SemaphoreType) or not isinstance(s, tuple) else pltpu.VMEM(*s) for s in scratch],
        compiler_params=pltpu.CompilerParams(vmem_limit_bytes=limit),
        cost_estimate=pl.CostEstimate(flops=flops, bytes_accessed=moved, transcendentals=0),
    )(*scalars, *operands)


def per_device(
    wave_in, mass_scale, potential, elem_scale, stiffness, proj_lower, proj_upper, kb_coef,
    atom_column, chan_count, upper_column,
):
    extent = wave_in.shape[0]
    degree = extent // 2
    ch = kb_coef.shape[-1]
    order, used = row_order(degree)
    padded = order.shape[0]
    perm = jnp.asarray(order, f32)[None, :]
    g = Mesh1(degree, ch, used, padded)
    plane, nodes = g.plane, g.nodes
    scalars = (atom_column, upper_column, chan_count)
    part = ((ch, LANES), f32)
    slab_s, x_s = ((nodes, LANES), f32), ((padded, 8 * LANES), bf16)
    wire_s = ((plane + ch, LANES), bf16)
    wire_first_s = ((plane + ch + FACE + CONST_ROWS, LANES), bf16)
    plane_s, face_s = ((plane, LANES), f32), ((LANES, 4 * LANES), bf16)

    slab, x, mass_wide, wave, stiff, scale, order_row, pot, kb, both, both_t, own, held, inner, outer = call(
        functools.partial(start_kernel, g), "start", scalars,
        (wave_in, mass_scale, elem_scale, stiffness, jnp.swapaxes(proj_lower, 1, 2), jnp.swapaxes(proj_upper, 1, 2),
         kb_coef, perm, potential),
        [slab_s, x_s, slab_s, (wave_in.shape, bf16), (stiffness.shape, bf16), ((8, LANES), f32), (perm.shape, f32),
         (potential.shape, f32), (kb_coef.shape, f32), ((padded, 2 * ch), bf16), ((2 * ch, padded), bf16), part, part,
         wire_first_s, wire_first_s],
        [plane_s, wire_first_s, wire_s, (mass_scale.shape, f32), (elem_scale.shape, f32),
         ((2 * ch, stiffness.shape[0]), bf16), pltpu.SemaphoreType.DMA((9,))], 10**8, hbm=True,
    )
    inner, outer = swapped(inner, outer, "space")
    (ordered,) = call(order_kernel, "order", (), (stiff, order_row), [((padded, padded), bf16)], [], 2 * 10**9)

    def bulk(slab, x):
        return call(
            functools.partial(bulk_kernel, g), "bulk", (), (scale, ordered, x, slab, pot),
            [slab_s, ((FACE, 4 * LANES), f32), face_s], [((used, 2 * LANES), f32)], 2 * 10**9,
        )

    total, face_own, x_face = bulk(slab, x)
    shared = (ordered, both, both_t)
    slab, x, step, own, held, inner, outer, kept = call(
        functools.partial(middle_kernel, g), "middle", scalars,
        (scale, wave, mass_wide, total, face_own, x_face, *shared, own, held, kb, inner, outer),
        [slab_s, x_s, ((nodes, LANES), bf16), part, part, wire_s, wire_s, ((FACE + CONST_ROWS, LANES), bf16)],
        [slab_s, plane_s, face_s, plane_s, wire_first_s, wire_s, wire_s, wire_s], 10**8,
    )
    inner, outer = swapped(inner, outer, "space")
    total, face_own, x_face = bulk(slab, x)
    filtered, own, held = call(
        functools.partial(last_kernel, g), "last", scalars,
        (scale, wave, mass_wide, total, face_own, x_face, *shared, own, held, kb, kept, inner, outer, step),
        [(wave_in.shape, bf16), part, part],
        [slab_s, plane_s, face_s, ((padded, 2 * LANES), bf16), wire_s, wire_s], 10**8,
    )
    return filtered, (own + shifted(held, "space", -1))[None]


def solution(mesh):
    in_specs = (
        P("space", None, None, "band"),
        P("space", None),
        P("space", None),
        P("space", None, None),
        P(),
        P("space", None, None),
        P("space", None, None),
        P("space", None),
        P("space"),
        P("space"),
        P("space"),
    )
    out_specs = (P("space", None, None, "band"), P("space", None, "band"))
    return jax.shard_map(
        per_device, mesh=mesh, in_specs=in_specs, out_specs=out_specs, check_vma=False
    )
```

```python
import functools

import jax
import jax.numpy as jnp
import numpy as np
from jax import lax
from jax.experimental import pallas as pl
from jax.experimental.pallas import tpu as pltpu
from jax.sharding import PartitionSpec as P

spectrum_center = 1.0
spectrum_half = 6.0
f32 = jnp.float32
bf16 = jnp.bfloat16
LANES = 128
FACE = 96
CONST_ROWS = 16


def shifted(value, axis, steps):
    count = lax.axis_size(axis)
    pairs = [(source, (source + steps) % count) for source in range(count)]
    return lax.ppermute(value, axis, pairs)


def swapped(inner, outer, axis):
    count = lax.axis_size(axis)
    within = [(source, source ^ 1) for source in range(count)]
    across = [(source, (source + (1 if source % 2 else -1)) % count) for source in range(count)]
    return lax.ppermute(inner, axis, within), lax.ppermute(outer, axis, across)


def is_odd():
    return lax.rem(lax.axis_index("space"), 2) == 1


def post(up, down, inner, outer):
    @pl.when(is_odd())
    def _():
        inner[: down.shape[0], :] = down[...]
        outer[: up.shape[0], :] = up[...]

    @pl.when(jnp.logical_not(is_odd()))
    def _():
        inner[: up.shape[0], :] = up[...]
        outer[: down.shape[0], :] = down[...]


def collect(inner, outer, up, down):
    @pl.when(is_odd())
    def _():
        up[...] = inner[: up.shape[0], :]
        down[...] = outer[: down.shape[0], :]

    @pl.when(jnp.logical_not(is_odd()))
    def _():
        up[...] = outer[: up.shape[0], :]
        down[...] = inner[: down.shape[0], :]


def row_order(degree):
    points = degree + 1

    def natural(i, j, l):
        return (i * points + j) * points + l

    inner = range(degree)
    order = [natural(degree, j, l) for j in inner for l in inner]
    order += [natural(degree, degree, l) for l in inner]
    order += [natural(degree, j, degree) for j in inner]
    order += [natural(degree, degree, degree)] + [-1] * (degree - 1)
    order += [natural(i, j, l) for i in inner for j in inner for l in inner]
    order += [natural(i, degree, l) for i in inner for l in inner]
    order += [natural(i, j, degree) for i in inner for j in inner]
    order += [natural(i, degree, degree) for i in inner]
    used = len(order)
    order += [-1] * (-used % 256)
    return np.asarray(order, np.int32), used


def dot(a, b):
    return jnp.dot(a, b, preferred_element_type=f32)


def dot_nt(a, b):
    return lax.dot_general(a, b, (((1,), (1,)), ((), ())), preferred_element_type=f32)


def onehot_rows(perm, count):
    rows = perm.shape[1]
    column = jnp.broadcast_to(perm, (8, rows)).T[:, :1]
    lane = lax.broadcasted_iota(jnp.int32, (rows, count), 1).astype(f32)
    return (column == lane).astype(bf16)


class Mesh1:
    def __init__(self, degree, channels, used, padded):
        self.d = degree
        self.e = 2 * degree
        self.plane = self.e * self.e
        self.nodes = self.e * self.plane
        self.ch = channels
        self.face_groups = degree + 3
        self.used = used
        self.padded = padded
        self.columns = [(a, b) for a in range(2) for b in range(2)]
        self.face_rows = degree * (degree + 1) ** 2
        rest = self.face_groups * degree
        lines = rest + degree**3
        self.lower_face_rows = [rest + j * degree for j in range(degree)]
        self.lower_face_rows += [lines, lines + degree**2, lines + 2 * degree**2]

    def far(self, index):
        return (1 - index) * self.d

    def aligned(self, value):
        return value if isinstance(value, int) else pl.multiple_of(value, self.d)

    def face_places(self, base, a, b):
        d, e = self.d, self.e
        near = base + a * d * e + b * d
        places = [(self.aligned(near + j * e), 1) for j in range(d)]
        places.append((self.aligned(base + self.far(a) * e + b * d), 1))
        places.append((base + a * d * e + self.far(b), e))
        places.append((self.aligned(base + self.far(a) * e + self.far(b)), 0))
        return places

    def layer_places(self, base, a, b):
        d, e, plane = self.d, self.e, self.plane
        near = base + a * d * e + b * d
        places = [(self.aligned(near + i * plane + j * e), 1) for i in range(d) for j in range(d)]
        places += [
            (self.aligned(base + i * plane + self.far(a) * e + b * d), 1) for i in range(d)
        ]
        places += [(base + i * plane + a * d * e + self.far(b), e) for i in range(d)]
        places.append((base + self.far(a) * e + self.far(b), plane))
        return places

    def take(self, ref, place):
        start, stride = place
        if stride > 1:
            return ref[pl.ds(start, self.d, stride=stride), :]
        value = ref[pl.ds(start, self.d), :]
        if stride == 0:
            first = lax.broadcasted_iota(jnp.int32, value.shape, 0) == 0
            value = jnp.where(first, value, 0.0)
        return value

    def put_add(self, ref, place, value):
        start, stride = place
        if stride > 1:
            rows = pl.ds(start, self.d, stride=stride)
        else:
            rows = pl.ds(start, self.d)
            if stride == 0:
                first = lax.broadcasted_iota(jnp.int32, value.shape, 0) == 0
                value = jnp.where(first, value, 0.0)
        ref[rows, :] = ref[rows, :] + value

    def pack(self, ref, lane, groups, first_row=0):
        lanes = pl.ds(lane, LANES)
        for at in range(0, len(groups), 2):
            pair = jnp.concatenate([groups[at], groups[at + 1]], axis=0).astype(bf16)
            ref[pl.ds(first_row + at * self.d, 2 * self.d), lanes] = pair

    def gather_element(self, slab, ref, lane, base, a, b, with_face):
        d = self.d
        zero = jnp.zeros((d, LANES), f32)
        if with_face:
            groups = [self.take(slab, p) for p in self.face_places(base + d * self.plane, a, b)]
        else:
            groups = [zero] * self.face_groups
        groups += [self.take(slab, p) for p in self.layer_places(base, a, b)]
        groups += [zero] * ((self.padded - self.used) // d)
        self.pack(ref, lane, groups)

    def gather_face(self, slab, ref, lane, base, a, b):
        zero = jnp.zeros((self.d, LANES), f32)
        groups = [self.take(slab, p) for p in self.face_places(base, a, b)]
        groups += [zero] * (LANES // self.d - len(groups))
        self.pack(ref, lane, groups)

    def add_face(self, ref, base, a, b, load):
        for g, place in enumerate(self.face_places(base, a, b)):
            self.put_add(ref, place, load(g))

    def add_layer(self, ref, base, a, b, load, start=0):
        for g, place in enumerate(self.layer_places(base, a, b)):
            if g >= start:
                self.put_add(ref, place, load(self.face_groups + g))


def live_weights(kb, count):
    lane = lax.broadcasted_iota(jnp.int32, kb.shape, 1)
    return kb * jnp.where(lane < count, 1.0, 0.0)


def as_column(row):
    size = row.shape[1]
    shape = (size, size)
    eye = lax.broadcasted_iota(jnp.int32, shape, 0) == lax.broadcasted_iota(jnp.int32, shape, 1)
    return jnp.sum(jnp.where(eye, jnp.broadcast_to(row, shape), 0.0), axis=1, keepdims=True)


def split_element(column):
    return column // 2, column % 2


def outgoing(g, acol, scale, slab, x_top, x_held, kface, both_t, face_sums, up, down, own_out, held_out):
    d, ch = g.d, g.ch
    own = dot(both_t[ch:, :], x_top[:, pl.ds(pl.multiple_of(acol * LANES, LANES), LANES)])
    held = dot(both_t[:ch, :], x_held[...])
    own_out[...] = own
    held_out[...] = held
    sums = dot(kface, x_top[...])
    face_sums[...] = jnp.zeros_like(face_sums)
    for k, (a, b) in enumerate(g.columns):
        part = sums[:, k * LANES : (k + 1) * LANES] * scale[4 + k : 5 + k, :]
        g.add_face(face_sums, 0, a, b, lambda n: part[n * d : (n + 1) * d])
    up[: g.plane, :] = face_sums[...].astype(bf16)
    up[g.plane : g.plane + ch, :] = own.astype(bf16)
    down[: g.plane, :] = slab[: g.plane, :].astype(bf16)
    down[g.plane :, :] = held.astype(bf16)


def gather_out(g, slab, x_top, x_held, ucol):
    for k, (a, b) in enumerate(g.columns):
        g.gather_element(slab, x_top, k * LANES, g.d * g.plane, a, b, False)
    a, b = split_element(ucol)
    g.gather_element(slab, x_held, 0, 0, a, b, True)


def widen(g, source, target):
    value = source[...]
    high = value.astype(bf16).astype(f32)
    middle = (value - high).astype(bf16).astype(f32)
    parts = jnp.concatenate([high, middle, value - high - middle], axis=0).T.astype(bf16)
    shape = (3 * g.e, 2 * LANES)
    row = lax.rem(lax.broadcasted_iota(jnp.int32, shape, 0), g.e)
    second = (lax.broadcasted_iota(jnp.int32, shape, 1) >= LANES).astype(jnp.int32)
    for p in range(0, g.e, 2):
        wide = dot(parts, (row == p + second).astype(f32).astype(bf16))
        target[p * g.plane : (p + 1) * g.plane, :] = wide[:, :LANES]
        target[(p + 1) * g.plane : (p + 2) * g.plane, :] = wide[:, LANES:]


def start_kernel(
    g, acol, ucol, count, wave_hbm, mass_hbm, scale_hbm, stiff_hbm, low_hbm, up_hbm, kb_hbm, perm_hbm, pot_hbm,
    slab, x_top, mass_wide, wave, stiff, scale, perm, pot, kb, both, both_t, own_out, held_out, inner, outer,
    face_sums, up, down, mass, scale_in, proj, x_held, sems,
):
    ch = g.ch
    copies = [
        pltpu.make_async_copy(source, target, sems.at[k])
        for k, (source, target) in enumerate((
            (mass_hbm, mass), (wave_hbm, wave), (perm_hbm, perm), (up_hbm.at[0], proj.at[:ch]),
            (low_hbm.at[0], proj.at[ch:]), (stiff_hbm, stiff), (scale_hbm, scale_in), (kb_hbm, kb), (pot_hbm, pot),
        ))
    ]
    for copy in copies:
        copy.start()
    copies[0].wait()
    widen(g, mass, mass_wide)
    copies[1].wait()
    for p in range(g.e):
        rows = pl.ds(p * g.plane, g.plane)
        start = wave[p].astype(f32).reshape(g.plane, LANES)
        slab[rows, :] = (mass_wide[rows, :] * start).astype(bf16).astype(f32)
    gather_out(g, slab, x_top, x_held, ucol[0])
    for copy in copies[2:]:
        copy.wait()
    for k in range(8):
        one = scale_in[k // 4, k % 4 // 2 : k % 4 // 2 + 1, k % 2 : k % 2 + 1]
        scale[k : k + 1, :] = jnp.broadcast_to(one, (1, LANES))
    count_rows = stiff.shape[0]
    sublane = lax.broadcasted_iota(jnp.int32, (count_rows, g.padded), 0).astype(f32)
    pick_t = (perm[...] == sublane).astype(f32).astype(bf16)
    first = g.face_rows // 16 * 16
    left = jnp.concatenate([proj[...], stiff[first:, :]], axis=0)
    ordered = dot(left, pick_t)
    both_t[...] = ordered[: 2 * ch].astype(bf16)
    kface = dot(onehot_rows(perm[:, :LANES] - first, count_rows - first)[:FACE], ordered[2 * ch :].astype(bf16))
    kface = kface.astype(bf16)
    turned = ordered[: 2 * ch].T.astype(bf16)
    both[...] = turned
    outgoing(g, acol[0], scale, slab, x_top, x_held, kface, both_t, face_sums, up, down, own_out, held_out)
    at = g.plane + ch
    up[at : at + FACE, :] = jnp.zeros((FACE, LANES), bf16)
    up[at : at + FACE, :ch] = turned[:FACE, ch:]
    shape = (CONST_ROWS, LANES)
    row = lax.broadcasted_iota(jnp.int32, shape, 0)
    values = jnp.zeros(shape, f32)
    for k in range(4):
        chosen = jnp.where(acol[0] == k, 1.0, 0.0)
        values = jnp.where(row == k, chosen, values)
        full = jnp.broadcast_to(scale[4 + k : 5 + k, :], shape)
        high = full.astype(bf16).astype(f32)
        values = jnp.where(row == 4 + k, high, values)
        values = jnp.where(row == 8 + k, full - high, values)
    weights = live_weights(kb[...], count[0])
    weights = jnp.concatenate([weights, jnp.zeros((1, LANES - ch), f32)], axis=1)
    full = jnp.broadcast_to(weights, shape)
    high = full.astype(bf16).astype(f32)
    values = jnp.where(row == 12, high, values)
    values = jnp.where(row == 13, full - high, values)
    up[at + FACE :, :] = values.astype(bf16)
    post(up, down, inner, outer)


def order_kernel(g, stiff, perm, pot, ordered, pot_wide):
    widen(g, pot, pot_wide)
    pick = onehot_rows(perm[...], stiff.shape[0])
    part = perm.shape[1] // 3
    for k in range(3):
        rows = slice(k * part, (k + 1) * part)
        half = dot(pick[rows], stiff[...]).astype(bf16)
        ordered[rows, :] = dot_nt(half, pick).astype(bf16)


def bulk_sums(g, scale, ordered, x_top, slab, pot_wide, face_own, x_face, total, z, x_low):
    d = g.d
    for p in range(g.e):
        rows = pl.ds(p * g.plane, g.plane)
        total[rows, :] = pot_wide[rows, :] * slab[rows, :]
    for k, (a, b) in enumerate(g.columns):
        g.gather_element(slab, x_low, k * LANES, 0, a, b, True)
        g.gather_face(slab, x_face, k * LANES, 0, a, b)
    for layer, x in enumerate((x_low, x_top)):
        for a in range(2):
            lane = a * 2 * LANES
            z[...] = dot(ordered[: g.used, :], x[:, lane : lane + 2 * LANES])
            for b in range(2):
                k = layer * 4 + a * 2 + b
                factor = scale[k : k + 1, :]

                def load(n):
                    return z[n * d : (n + 1) * d, b * LANES : (b + 1) * LANES] * factor

                if layer == 0:
                    g.add_face(total, d * g.plane, a, b, load)
                g.add_layer(total, layer * d * g.plane, a, b, load)
    face_own[...] = dot(ordered[:FACE, :LANES], x_face[...])


def bulk_kernel(
    g, scale, ordered, x_top, slab, pot_wide, mass_wide, wave,
    before, low_step, low_slab, face_own, x_face, total, z, x_low,
):
    bulk_sums(g, scale, ordered, x_top, slab, pot_wide, face_own, x_face, total, z, x_low)
    for p in range(g.e):
        rows = pl.ds(p * g.plane, g.plane)
        wide = mass_wide[rows, :]
        base = wave[p].astype(f32).reshape(g.plane, LANES)
        value = (wide * total[rows, :] - spectrum_center * base) * (1.0 / spectrum_half)
        before[rows, :] = value
        if p < g.d:
            one = value.astype(bf16).astype(f32)
            low_step[rows, :] = one
            low_slab[rows, :] = (wide * one).astype(bf16).astype(f32)


def bulk_last_kernel(
    g, scale, ordered, x_top, slab, pot_wide, mass_wide, wave, step,
    before, low_new, face_own, x_face, total, z, x_low,
):
    bulk_sums(g, scale, ordered, x_top, slab, pot_wide, face_own, x_face, total, z, x_low)
    for p in range(g.e):
        rows = pl.ds(p * g.plane, g.plane)
        base = wave[p].astype(f32).reshape(g.plane, LANES)
        image = mass_wide[rows, :] * total[rows, :]
        value = (image - spectrum_center * step[rows, :]) * (2.0 / spectrum_half) - base
        before[rows, :] = value
        if p < g.d:
            low_new[rows, :] = value.astype(bf16).astype(f32)


def neighbour_terms(
    g, acol, count, both, both_t, own, held, kb, face_low, const, up, down, x_face, next_plane, x_next,
):
    ch = g.ch
    next_plane[...] = down[: g.plane, :].astype(f32)
    for k, (a, b) in enumerate(g.columns):
        g.gather_face(next_plane, x_next, k * LANES, 0, a, b)
    mine = own[...] + down[g.plane :, :].astype(f32)
    column = pl.ds(pl.multiple_of(acol * LANES, LANES), LANES)
    mine = mine + dot(both_t[ch:, :LANES], x_next[:, column])
    mine = (as_column(live_weights(kb[...], count)) * mine).astype(bf16)
    weights_low = as_column(const[12:13, :ch] + const[13:14, :ch])
    low = up[g.plane : g.plane + ch, :].astype(f32) + held[...]
    low = low + dot_chosen(face_low, x_face, const)
    low = (weights_low * low).astype(bf16)
    return mine, low


def dot_chosen(face, x_face, const):
    rows = face.shape[0]
    chosen = jnp.zeros((rows, LANES), f32)
    for k in range(4):
        chosen = chosen + x_face[:rows, k * LANES : (k + 1) * LANES].astype(f32) * const[k : k + 1, :]
    face_t = face.astype(f32).T.astype(bf16)
    return dot(face_t, chosen.astype(bf16))


def rim_sums(g, ucol, const, face_own, face_low, low, lifted_up, up, rim):
    d = g.d
    lifted_low = dot(face_low, low)
    rim[...] = up[: g.plane, :].astype(f32)
    for k, (a, b) in enumerate(g.columns):
        part = face_own[:, k * LANES : (k + 1) * LANES] * (const[4 + k : 5 + k, :] + const[8 + k : 9 + k, :])
        part = part + lifted_low * const[k : k + 1, :]
        g.add_face(rim, 0, a, b, lambda n: part[n * d : (n + 1) * d])
    a, b = split_element(ucol)
    for start, place in zip(g.lower_face_rows, g.face_places(0, a, b)):
        g.put_add(rim, place, lifted_up[start : start + d])


def upper_sums(g, acol, scale, ordered, both, x_next, mine, sums):
    d = g.d
    upper = dot(ordered[: g.used, :LANES], x_next[...])
    lifted = dot(both[: g.used, g.ch :], mine)

    def loader(k):
        here = jnp.where(acol == k, 1.0, 0.0)
        factor = scale[4 + k : 5 + k, :]
        lane = k * LANES

        def load(n):
            rows = slice(n * d, (n + 1) * d)
            return upper[rows, lane : lane + LANES] * factor + lifted[rows] * here

        return load

    for k, (a, b) in enumerate(g.columns):
        load = loader(k)
        near = a * d * g.e + b * d
        for i in range(d):
            for j in range(d):
                sums[pl.ds(near + i * g.plane + j * g.e, d), :] = load(g.face_groups + i * d + j)
    for k, (a, b) in enumerate(g.columns):
        g.add_layer(sums, 0, a, b, loader(k), start=d * d)


def held_places(g, ucol, lifted_up):
    d = g.d
    a, b = split_element(ucol)
    for n, place in enumerate(g.layer_places(0, a, b)):
        row = (g.face_groups + n) * d
        if row not in g.lower_face_rows[:-1]:
            start, stride = place
            rows = pl.ds(start, d, stride=stride) if stride > 1 else pl.ds(start, d)
            yield rows, None if lifted_up is None else lifted_up[row : row + d]


def middle_kernel(
    g, acol, ucol, count, scale, mass_wide, before, low_step, low_slab, face_own, x_face, ordered, both, both_t,
    own, held, kb, inner, outer,
    slab, x_top, step, own_out, held_out, inner_out, outer_out, kept,
    sums, next_plane, x_next, face_sums, up, down, up_out, down_out, rim, x_held,
):
    at = g.plane + g.ch
    d = g.d
    half = d * g.plane
    collect(inner, outer, up, down)
    kept[...] = up[at:, :]
    face_low = up[at : at + FACE, : g.ch]
    const = up[at + FACE :, :].astype(f32)
    mine, low = neighbour_terms(
        g, acol[0], count[0], both, both_t, own, held, kb, face_low, const, up, down, x_face, next_plane, x_next
    )
    lifted_up = dot(both[: g.used, : g.ch], low)
    upper_sums(g, acol[0], scale, ordered, both, x_next, mine, sums)
    a, b = split_element(ucol[0])
    g.add_face(sums, 0, a, b, lambda n: lifted_up[n * d : (n + 1) * d])
    rim_sums(g, ucol[0], const, face_own, face_low, low, lifted_up, up, rim)
    step[:half, :] = low_step[...]
    slab[:half, :] = low_slab[...]

    def finish(rows, added):
        wide = mass_wide[rows, :]
        one = (before[rows, :] + wide * (added * (1.0 / spectrum_half))).astype(bf16).astype(f32)
        step[rows, :] = one
        slab[rows, :] = (wide * one).astype(bf16).astype(f32)

    for rows, added in held_places(g, ucol[0], lifted_up):
        finish(rows, added)
    finish(pl.ds(0, g.plane), rim[...])
    for p in range(d):
        finish(pl.ds(half + p * g.plane, g.plane), sums[p * g.plane : (p + 1) * g.plane, :])
    gather_out(g, slab, x_top, x_held, ucol[0])
    outgoing(
        g, acol[0], scale, slab, x_top, x_held, ordered[:FACE, :], both_t, face_sums, up_out, down_out,
        own_out, held_out,
    )
    post(up_out, down_out, inner_out, outer_out)


def last_low_kernel(
    g, acol, ucol, count, scale, mass_wide, before, face_own, x_face, ordered, both, both_t,
    own, held, kb, kept, inner, outer,
    held_out, new, mine_out, x_next,
    sums, next_plane, x_held, x_rim, up, down, rim,
):
    d, ch = g.d, g.ch
    half = d * g.plane
    collect(inner, outer, up, down)
    face_low = kept[:FACE, :ch]
    const = kept[FACE:, :].astype(f32)
    mine, low = neighbour_terms(
        g, acol[0], count[0], both, both_t, own, held, kb, face_low, const, up, down, x_face, next_plane, x_next
    )
    mine_out[...] = mine
    lifted_up = dot(both[: g.used, :ch], low)
    starts = g.lower_face_rows
    pieces = [slice(starts[0] - d, starts[0] + (d + 1) * d)] + [slice(s - d, s + d) for s in starts[d:]]
    offsets = [d + n * d for n in range(d)] + [(d + 2) * d + n * 2 * d + d for n in range(3)]
    upper = dot(jnp.concatenate([ordered[p, :LANES] for p in pieces], axis=0), x_next[...])
    lifted = dot(jnp.concatenate([both[p, ch:] for p in pieces], axis=0), mine)
    sums[...] = jnp.zeros_like(sums)
    for k, (a, b) in enumerate(g.columns):
        here = jnp.where(acol[0] == k, 1.0, 0.0)
        factor = scale[4 + k : 5 + k, :]
        part = upper[:, k * LANES : (k + 1) * LANES] * factor + lifted * here
        g.add_face(sums, 0, a, b, lambda n: part[offsets[n] : offsets[n] + d])
    a, b = split_element(ucol[0])
    g.add_face(sums, 0, a, b, lambda n: lifted_up[n * d : (n + 1) * d])
    rim_sums(g, ucol[0], const, face_own, face_low, low, lifted_up, up, rim)

    def finish(rows, added):
        value = before[rows, :] + mass_wide[rows, :] * (added * (2.0 / spectrum_half))
        new[rows, :] = value.astype(bf16).astype(f32)

    for rows, added in held_places(g, ucol[0], lifted_up):
        finish(rows, added)
    finish(pl.ds(0, g.plane), rim[...])
    finish(pl.ds(half, g.plane), sums[...])
    g.gather_element(new, x_held, 0, 0, a, b, True)
    for k, (a, b) in enumerate(g.columns):
        g.gather_face(new, x_rim, k * LANES, 0, a, b)
    held_out[...] = dot(both_t[:ch, :], x_held[...]) + dot_chosen(face_low, x_rim, const)


def last_high_kernel(
    g, acol, ucol, count, scale, mass_wide, before, low_new, ordered, both, both_t, new, mine, x_next,
    filtered, own_out, sums, field, x_own,
):
    d = g.d
    half = d * g.plane
    field[:half, :] = low_new[...]
    for rows, _ in held_places(g, ucol[0], None):
        field[rows, :] = new[rows, :]
    field[: g.plane, :] = new[: g.plane, :]
    field[half : half + g.plane, :] = new[half : half + g.plane, :]
    upper_sums(g, acol[0], scale, ordered, both, x_next, mine[...], sums)
    for p in range(1, d):
        rows = pl.ds(half + p * g.plane, g.plane)
        added = sums[p * g.plane : (p + 1) * g.plane, :]
        value = before[rows, :] + mass_wide[rows, :] * (added * (2.0 / spectrum_half))
        field[rows, :] = value.astype(bf16).astype(f32)
    for p in range(g.e):
        filtered[p] = field[p * g.plane : (p + 1) * g.plane, :].astype(bf16).reshape(g.e, g.e, LANES)
    a, b = split_element(acol[0])
    g.gather_element(field, x_own, 0, half, a, b, False)
    own_out[...] = dot(both_t[g.ch :, :], x_own[...])


def call(kernel, name, scalars, operands, outs, scratch, flops, limit=24 << 20, hbm=False):
    smem = pl.BlockSpec(memory_space=pltpu.SMEM)
    vmem = pl.BlockSpec(memory_space=pltpu.VMEM)
    far = pl.BlockSpec(memory_space=pltpu.MemorySpace.HBM)
    moved = sum(v.size * v.dtype.itemsize for v in operands)
    if hbm:
        operands = [pltpu.with_memory_space_constraint(v, pltpu.MemorySpace.HBM) for v in operands]
    return pl.pallas_call(
        kernel,
        name=name,
        out_shape=[jax.ShapeDtypeStruct(s, t) for s, t in outs],
        in_specs=[smem] * len(scalars) + [far if hbm else vmem] * len(operands),
        out_specs=[vmem] * len(outs),
        scratch_shapes=[pltpu.VMEM(*s) if isinstance(s, tuple) else s for s in scratch],
        compiler_params=pltpu.CompilerParams(vmem_limit_bytes=limit),
        cost_estimate=pl.CostEstimate(flops=flops, bytes_accessed=moved, transcendentals=0),
    )(*scalars, *operands)


def per_device(
    wave_in, mass_scale, potential, elem_scale, stiffness, proj_lower, proj_upper, kb_coef,
    atom_column, chan_count, upper_column,
):
    extent = wave_in.shape[0]
    degree = extent // 2
    ch = kb_coef.shape[-1]
    order, used = row_order(degree)
    padded = order.shape[0]
    perm = jnp.asarray(order, f32)[None, :]
    g = Mesh1(degree, ch, used, padded)
    plane, nodes = g.plane, g.nodes
    scalars = (atom_column, upper_column, chan_count)
    part = ((ch, LANES), f32)
    slab_s, half_s, plane_s = ((nodes, LANES), f32), ((nodes // 2, LANES), f32), ((plane, LANES), f32)
    x_s, x_one_s = ((padded, 4 * LANES), bf16), ((padded, LANES), bf16)
    wire_s = ((plane + ch, LANES), bf16)
    wire_first_s = ((plane + ch + FACE + CONST_ROWS, LANES), bf16)
    face_s = ((LANES, 4 * LANES), bf16)
    face_sum_s = ((FACE, 4 * LANES), f32)

    slab, x_top, mass_wide, wave, stiff, scale, order_row, pot, kb, both, both_t, own, held, inner, outer = call(
        functools.partial(start_kernel, g), "start", scalars,
        (wave_in, mass_scale, elem_scale, stiffness, jnp.swapaxes(proj_lower, 1, 2), jnp.swapaxes(proj_upper, 1, 2),
         kb_coef, perm, potential),
        [slab_s, x_s, slab_s, (wave_in.shape, bf16), (stiffness.shape, bf16), ((8, LANES), f32), (perm.shape, f32),
         (potential.shape, f32), (kb_coef.shape, f32), ((padded, 2 * ch), bf16), ((2 * ch, padded), bf16), part, part,
         wire_first_s, wire_first_s],
        [plane_s, wire_first_s, wire_s, (mass_scale.shape, f32), (elem_scale.shape, f32),
         ((2 * ch, stiffness.shape[0]), bf16), x_one_s, pltpu.SemaphoreType.DMA((9,))], 10**8, hbm=True,
    )
    inner, outer = swapped(inner, outer, "space")
    ordered, pot_wide = call(
        functools.partial(order_kernel, g), "order", (), (stiff, order_row, pot),
        [((padded, padded), bf16), slab_s], [], 2 * 10**9,
    )
    bulk_scratch = [slab_s, ((used, 2 * LANES), f32), x_s]
    before, low_step, low_slab, face_own, x_face = call(
        functools.partial(bulk_kernel, g), "bulk", (), (scale, ordered, x_top, slab, pot_wide, mass_wide, wave),
        [slab_s, half_s, half_s, face_sum_s, face_s], bulk_scratch, 2 * 10**9,
    )
    shared = (ordered, both, both_t)
    slab, x_top, step, own, held, inner, outer, kept = call(
        functools.partial(middle_kernel, g), "middle", scalars,
        (scale, mass_wide, before, low_step, low_slab, face_own, x_face, *shared, own, held, kb, inner, outer),
        [slab_s, x_s, slab_s, part, part, wire_s, wire_s, ((FACE + CONST_ROWS, LANES), bf16)],
        [half_s, plane_s, face_s, plane_s, wire_first_s, wire_s, wire_s, wire_s, plane_s, x_one_s], 10**8,
    )
    inner, outer = swapped(inner, outer, "space")
    before, low_new, face_own, x_face = call(
        functools.partial(bulk_last_kernel, g), "bulk_last", (),
        (scale, ordered, x_top, slab, pot_wide, mass_wide, wave, step),
        [slab_s, half_s, face_sum_s, face_s], bulk_scratch, 2 * 10**9,
    )
    held, new, mine, x_next = call(
        functools.partial(last_low_kernel, g), "last_low", scalars,
        (scale, mass_wide, before, face_own, x_face, *shared, own, held, kb, kept, inner, outer),
        [part, ((nodes // 2 + plane, LANES), f32), ((ch, LANES), bf16), face_s],
        [plane_s, plane_s, x_one_s, face_s, wire_s, wire_s, plane_s], 10**8,
    )
    held = shifted(held, "space", -1)
    filtered, own = call(
        functools.partial(last_high_kernel, g), "last_high", scalars,
        (scale, mass_wide, before, low_new, *shared, new, mine, x_next),
        [(wave_in.shape, bf16), part], [half_s, slab_s, x_one_s], 10**9,
    )
    return filtered, (own + held)[None]


def solution(mesh):
    in_specs = (
        P("space", None, None, "band"),
        P("space", None),
        P("space", None),
        P("space", None, None),
        P(),
        P("space", None, None),
        P("space", None, None),
        P("space", None),
        P("space"),
        P("space"),
        P("space"),
    )
    out_specs = (P("space", None, None, "band"), P("space", None, "band"))
    return jax.shard_map(
        per_device, mesh=mesh, in_specs=in_specs, out_specs=out_specs, check_vma=False
    )
```

```python
import functools

import jax
import jax.numpy as jnp
import numpy as np
from jax import lax
from jax.experimental import pallas as pl
from jax.experimental.pallas import tpu as pltpu
from jax.sharding import PartitionSpec as P


spectrum_center = 1.0
spectrum_half = 6.0
f32 = jnp.float32
bf16 = jnp.bfloat16
LANES = 128
FACE = 96
FOLD = 32
CONST_ROWS = 16


def shifted(value, axis, steps):
    count = lax.axis_size(axis)
    pairs = [(source, (source + steps) % count) for source in range(count)]
    return lax.ppermute(value, axis, pairs)


def swapped(inner, outer, axis):
    count = lax.axis_size(axis)
    within = [(source, source ^ 1) for source in range(count)]
    across = [(source, (source + (1 if source % 2 else -1)) % count) for source in range(count)]
    outer = lax.ppermute(outer, axis, across)
    inner = lax.ppermute(inner, axis, within)
    return inner, outer


def is_odd():
    return lax.rem(lax.axis_index("space"), 2) == 1


def post(up, down, inner, outer):
    @pl.when(is_odd())
    def _():
        inner[: down.shape[0], :] = down[...]
        outer[: up.shape[0], :] = up[...]

    @pl.when(jnp.logical_not(is_odd()))
    def _():
        inner[: up.shape[0], :] = up[...]
        outer[: down.shape[0], :] = down[...]


def collect(inner, outer, up, down):
    @pl.when(is_odd())
    def _():
        up[...] = inner[: up.shape[0], :]
        down[...] = outer[: down.shape[0], :]

    @pl.when(jnp.logical_not(is_odd()))
    def _():
        up[...] = outer[: up.shape[0], :]
        down[...] = inner[: down.shape[0], :]


def row_order(degree):
    points = degree + 1

    def natural(i, j, l):
        return (i * points + j) * points + l

    inner = range(degree)
    order = [natural(degree, j, l) for j in inner for l in inner]
    order += [natural(degree, degree, l) for l in inner]
    order += [natural(degree, j, degree) for j in inner]
    order += [natural(degree, degree, degree)] + [-1] * (degree - 1)
    order += [natural(i, j, l) for i in inner for j in inner for l in inner]
    order += [natural(i, degree, l) for i in inner for l in inner]
    order += [natural(i, j, degree) for i in inner for j in inner]
    order += [natural(i, degree, degree) for i in inner]
    used = len(order)
    order += [-1] * (-used % 256)
    return np.asarray(order, np.int32), used


def dot(a, b):
    return jnp.dot(a, b, preferred_element_type=f32)


def dot_nt(a, b):
    return lax.dot_general(a, b, (((1,), (1,)), ((), ())), preferred_element_type=f32)


def onehot_rows(perm, count):
    rows = perm.shape[1]
    column = jnp.broadcast_to(perm, (8, rows)).T[:, :1]
    lane = lax.broadcasted_iota(jnp.int32, (rows, count), 1).astype(f32)
    return (column == lane).astype(bf16)


class Mesh1:
    def __init__(self, degree, channels, used, padded):
        self.d = degree
        self.e = 2 * degree
        self.plane = self.e * self.e
        self.nodes = self.e * self.plane
        self.ch = channels
        self.face_groups = degree + 3
        self.used = used
        self.padded = padded
        self.columns = [(a, b) for a in range(2) for b in range(2)]
        self.face_rows = degree * (degree + 1) ** 2
        rest = self.face_groups * degree
        lines = rest + degree**3
        self.lower_face_rows = [rest + j * degree for j in range(degree)]
        self.lower_face_rows += [lines, lines + degree**2, lines + 2 * degree**2]

    def far(self, index):
        return (1 - index) * self.d

    def aligned(self, value):
        return value if isinstance(value, int) else pl.multiple_of(value, self.d)

    def face_places(self, base, a, b):
        d, e = self.d, self.e
        near = base + a * d * e + b * d
        places = [(self.aligned(near + j * e), 1) for j in range(d)]
        places.append((self.aligned(base + self.far(a) * e + b * d), 1))
        places.append((base + a * d * e + self.far(b), e))
        places.append((self.aligned(base + self.far(a) * e + self.far(b)), 0))
        return places

    def layer_places(self, base, a, b):
        d, e, plane = self.d, self.e, self.plane
        near = base + a * d * e + b * d
        places = [(self.aligned(near + i * plane + j * e), 1) for i in range(d) for j in range(d)]
        places += [
            (self.aligned(base + i * plane + self.far(a) * e + b * d), 1) for i in range(d)
        ]
        places += [(base + i * plane + a * d * e + self.far(b), e) for i in range(d)]
        places.append((base + self.far(a) * e + self.far(b), plane))
        return places

    def take(self, ref, place):
        start, stride = place
        if stride > 1:
            return ref[pl.ds(start, self.d, stride=stride), :]
        value = ref[pl.ds(start, self.d), :]
        if stride == 0:
            first = lax.broadcasted_iota(jnp.int32, value.shape, 0) == 0
            value = jnp.where(first, value, 0.0)
        return value

    def put_add(self, ref, place, value):
        start, stride = place
        if stride > 1:
            rows = pl.ds(start, self.d, stride=stride)
        else:
            rows = pl.ds(start, self.d)
            if stride == 0:
                first = lax.broadcasted_iota(jnp.int32, value.shape, 0) == 0
                value = jnp.where(first, value, 0.0)
        ref[rows, :] = ref[rows, :] + value

    def pack(self, ref, lane, groups, first_row=0):
        lanes = pl.ds(lane, LANES)
        for at in range(0, len(groups), 2):
            pair = jnp.concatenate([groups[at], groups[at + 1]], axis=0).astype(bf16)
            ref[pl.ds(first_row + at * self.d, 2 * self.d), lanes] = pair

    def gather_element(self, slab, ref, lane, base, a, b, with_face):
        d = self.d
        zero = jnp.zeros((d, LANES), f32)
        if with_face:
            groups = [self.take(slab, p) for p in self.face_places(base + d * self.plane, a, b)]
        else:
            groups = [zero] * self.face_groups
        groups += [self.take(slab, p) for p in self.layer_places(base, a, b)]
        groups += [zero] * ((self.padded - self.used) // d)
        self.pack(ref, lane, groups)

    def gather_face(self, slab, ref, lane, base, a, b):
        zero = jnp.zeros((self.d, LANES), f32)
        groups = [self.take(slab, p) for p in self.face_places(base, a, b)]
        groups += [zero] * (LANES // self.d - len(groups))
        self.pack(ref, lane, groups)

    def add_face(self, ref, base, a, b, load):
        for g, place in enumerate(self.face_places(base, a, b)):
            self.put_add(ref, place, load(g))

    def add_layer(self, ref, base, a, b, load, start=0):
        for g, place in enumerate(self.layer_places(base, a, b)):
            if g >= start:
                self.put_add(ref, place, load(self.face_groups + g))


def live_weights(kb, count):
    lane = lax.broadcasted_iota(jnp.int32, kb.shape, 1)
    return kb * jnp.where(lane < count, 1.0, 0.0)


def as_column(row):
    size = row.shape[1]
    shape = (size, size)
    eye = lax.broadcasted_iota(jnp.int32, shape, 0) == lax.broadcasted_iota(jnp.int32, shape, 1)
    return jnp.sum(jnp.where(eye, jnp.broadcast_to(row, shape), 0.0), axis=1, keepdims=True)


def split_element(column):
    return column // 2, column % 2


def outgoing(g, acol, scale, slab, x_top, x_held, kface, both_t, face_sums, up, down, own_out, held_out):
    d, ch = g.d, g.ch
    own = dot(both_t[ch:, :], x_top[:, pl.ds(pl.multiple_of(acol * LANES, LANES), LANES)])
    held = dot(both_t[:ch, :], x_held[...])
    own_out[...] = own
    held_out[...] = held
    sums = dot(kface, x_top[...])
    face_sums[...] = jnp.zeros_like(face_sums)
    for k, (a, b) in enumerate(g.columns):
        part = sums[:, k * LANES : (k + 1) * LANES] * scale[4 + k : 5 + k, :]
        g.add_face(face_sums, 0, a, b, lambda n: part[n * d : (n + 1) * d])
    up[: g.plane, :] = face_sums[...].astype(bf16)
    up[g.plane : g.plane + ch, :] = own.astype(bf16)
    down[: g.plane, :] = slab[: g.plane, :].astype(bf16)
    down[g.plane :, :] = held.astype(bf16)


def gather_out(g, slab, x_top, x_held, ucol):
    for k, (a, b) in enumerate(g.columns):
        g.gather_element(slab, x_top, k * LANES, g.d * g.plane, a, b, False)
    a, b = split_element(ucol)
    g.gather_element(slab, x_held, 0, 0, a, b, True)


def widen(g, source, target):
    value = source[...]
    high = value.astype(bf16).astype(f32)
    middle = (value - high).astype(bf16).astype(f32)
    parts = jnp.concatenate([high, middle, value - high - middle], axis=0).T.astype(bf16)
    shape = (3 * g.e, 2 * LANES)
    row = lax.rem(lax.broadcasted_iota(jnp.int32, shape, 0), g.e)
    second = (lax.broadcasted_iota(jnp.int32, shape, 1) >= LANES).astype(jnp.int32)
    for p in range(0, g.e, 2):
        wide = dot(parts, (row == p + second).astype(f32).astype(bf16))
        target[p * g.plane : (p + 1) * g.plane, :] = wide[:, :LANES]
        target[(p + 1) * g.plane : (p + 2) * g.plane, :] = wide[:, LANES:]


def start_kernel(
    g, acol, ucol, count, wave_hbm, mass_hbm, scale_hbm, stiff_hbm, low_hbm, up_hbm, kb_hbm, perm_hbm, pot_hbm,
    slab, x_top, mass_wide, wave, stiff, scale, perm, pot, kb, both, both_t, own_out, held_out, inner, outer,
    face_sums, up, down, mass, scale_in, proj, x_held, sems,
):
    ch = g.ch
    copies = [
        pltpu.make_async_copy(source, target, sems.at[k])
        for k, (source, target) in enumerate((
            (mass_hbm, mass), (perm_hbm, perm), (wave_hbm, wave), (up_hbm.at[0], proj.at[:ch]),
            (low_hbm.at[0], proj.at[ch:]), (stiff_hbm, stiff), (scale_hbm, scale_in), (kb_hbm, kb), (pot_hbm, pot),
        ))
    ]
    for copy in copies:
        copy.start()
    count_rows = stiff.shape[0]
    copies[0].wait()
    widen(g, mass, mass_wide)
    copies[1].wait()
    sublane = lax.broadcasted_iota(jnp.int32, (count_rows, g.padded), 0).astype(f32)
    pick_t = (perm[...] == sublane).astype(f32).astype(bf16)
    copies[2].wait()
    for p in range(g.e):
        rows = pl.ds(p * g.plane, g.plane)
        start = wave[p].astype(f32).reshape(g.plane, LANES)
        slab[rows, :] = (mass_wide[rows, :] * start).astype(bf16).astype(f32)
    gather_out(g, slab, x_top, x_held, ucol[0])
    for copy in copies[3:]:
        copy.wait()
    for k in range(8):
        one = scale_in[k // 4, k % 4 // 2 : k % 4 // 2 + 1, k % 2 : k % 2 + 1]
        scale[k : k + 1, :] = jnp.broadcast_to(one, (1, LANES))
    first = g.face_rows // 16 * 16
    left = jnp.concatenate([proj[...], stiff[first:, :]], axis=0)
    ordered = dot(left, pick_t)
    both_t[...] = ordered[: 2 * ch].astype(bf16)
    kface = dot(onehot_rows(perm[:, :LANES] - first, count_rows - first)[:FACE], ordered[2 * ch :].astype(bf16))
    kface = kface.astype(bf16)
    turned = ordered[: 2 * ch].T.astype(bf16)
    both[...] = turned
    outgoing(g, acol[0], scale, slab, x_top, x_held, kface, both_t, face_sums, up, down, own_out, held_out)
    at = g.plane + ch
    folded = [turned[k : k + FOLD, ch:] for k in range(0, FACE, FOLD)]
    rest = LANES - len(folded) * ch
    if rest:
        folded.append(jnp.zeros((FOLD, rest), bf16))
    up[at : at + FOLD, :] = jnp.concatenate(folded, axis=1)
    shape = (CONST_ROWS, LANES)
    row = lax.broadcasted_iota(jnp.int32, shape, 0)
    values = jnp.zeros(shape, f32)
    for k in range(4):
        chosen = jnp.where(acol[0] == k, 1.0, 0.0)
        values = jnp.where(row == k, chosen, values)
        full = jnp.broadcast_to(scale[4 + k : 5 + k, :], shape)
        high = full.astype(bf16).astype(f32)
        values = jnp.where(row == 4 + k, high, values)
        values = jnp.where(row == 8 + k, full - high, values)
    weights = live_weights(kb[...], count[0])
    weights = jnp.concatenate([weights, jnp.zeros((1, LANES - ch), f32)], axis=1)
    full = jnp.broadcast_to(weights, shape)
    high = full.astype(bf16).astype(f32)
    values = jnp.where(row == 12, high, values)
    values = jnp.where(row == 13, full - high, values)
    up[at + FOLD :, :] = values.astype(bf16)
    post(up, down, inner, outer)


def order_kernel(g, stiff, perm, pot, ordered, pot_wide):
    widen(g, pot, pot_wide)
    pick = onehot_rows(perm[...], stiff.shape[0])
    part = perm.shape[1] // 3
    for k in range(3):
        rows = slice(k * part, (k + 1) * part)
        half = dot(pick[rows], stiff[...]).astype(bf16)
        ordered[rows, :] = dot_nt(half, pick).astype(bf16)


def bulk_sums(g, scale, ordered, x_top, slab, pot_wide, face_own, x_face, total, z, x_low):
    d = g.d
    for p in range(g.e):
        rows = pl.ds(p * g.plane, g.plane)
        total[rows, :] = pot_wide[rows, :] * slab[rows, :]
    for k, (a, b) in enumerate(g.columns):
        g.gather_element(slab, x_low, k * LANES, 0, a, b, True)
        g.gather_face(slab, x_face, k * LANES, 0, a, b)
    for layer, x in enumerate((x_low, x_top)):
        for a in range(2):
            lane = a * 2 * LANES
            z[...] = dot(ordered[: g.used, :], x[:, lane : lane + 2 * LANES])
            for b in range(2):
                k = layer * 4 + a * 2 + b
                factor = scale[k : k + 1, :]

                def load(n):
                    return z[n * d : (n + 1) * d, b * LANES : (b + 1) * LANES] * factor

                if layer == 0:
                    g.add_face(total, d * g.plane, a, b, load)
                g.add_layer(total, layer * d * g.plane, a, b, load)
    face_own[...] = dot(ordered[:FACE, :LANES], x_face[...])


def bulk_kernel(
    g, scale, ordered, x_top, slab, pot_wide, mass_wide, wave,
    before, low_step, low_slab, face_own, x_face, total, z, x_low,
):
    bulk_sums(g, scale, ordered, x_top, slab, pot_wide, face_own, x_face, total, z, x_low)
    for p in range(g.e):
        rows = pl.ds(p * g.plane, g.plane)
        wide = mass_wide[rows, :]
        base = wave[p].astype(f32).reshape(g.plane, LANES)
        value = (wide * total[rows, :] - spectrum_center * base) * (1.0 / spectrum_half)
        before[rows, :] = value
        if p < g.d:
            one = value.astype(bf16).astype(f32)
            low_step[rows, :] = one
            low_slab[rows, :] = (wide * one).astype(bf16).astype(f32)


def bulk_last_kernel(
    g, scale, ordered, x_top, slab, pot_wide, mass_wide, wave, step,
    before, low_new, face_own, x_face, total, z, x_low,
):
    bulk_sums(g, scale, ordered, x_top, slab, pot_wide, face_own, x_face, total, z, x_low)
    for p in range(g.e):
        rows = pl.ds(p * g.plane, g.plane)
        base = wave[p].astype(f32).reshape(g.plane, LANES)
        image = mass_wide[rows, :] * total[rows, :]
        value = (image - spectrum_center * step[rows, :]) * (2.0 / spectrum_half) - base
        before[rows, :] = value
        if p < g.d:
            low_new[rows, :] = value.astype(bf16).astype(f32)


def neighbour_terms(g, acol, count, both_t, own, held, kb, face_low, const, up, down, x_face, next_plane, x_next):
    ch = g.ch
    next_plane[...] = down[: g.plane, :].astype(f32)
    for k, (a, b) in enumerate(g.columns):
        g.gather_face(next_plane, x_next, k * LANES, 0, a, b)
    mine = own[...] + down[g.plane :, :].astype(f32)
    column = pl.ds(pl.multiple_of(acol * LANES, LANES), LANES)
    mine = mine + dot(both_t[ch:, :LANES], x_next[:, column])
    mine = (as_column(live_weights(kb[...], count)) * mine).astype(bf16)
    weights_low = as_column(const[12:13, :ch] + const[13:14, :ch])
    low = up[g.plane : g.plane + ch, :].astype(f32) + held[...]
    low = low + dot_chosen(face_low, x_face, const)
    low = (weights_low * low).astype(bf16)
    return mine, low


def dot_chosen(face, x_face, const):
    rows = face.shape[0]
    chosen = jnp.zeros((rows, LANES), f32)
    for k in range(4):
        chosen = chosen + x_face[:rows, k * LANES : (k + 1) * LANES].astype(f32) * const[k : k + 1, :]
    face_t = face.astype(f32).T.astype(bf16)
    return dot(face_t, chosen.astype(bf16))


def rim_sums(g, ucol, const, face_own, face_low, low, lifted_up, up, rim):
    d = g.d
    lifted_low = dot(face_low, low)
    rim[...] = up[: g.plane, :].astype(f32)
    for k, (a, b) in enumerate(g.columns):
        part = face_own[:, k * LANES : (k + 1) * LANES] * (const[4 + k : 5 + k, :] + const[8 + k : 9 + k, :])
        part = part + lifted_low * const[k : k + 1, :]
        g.add_face(rim, 0, a, b, lambda n: part[n * d : (n + 1) * d])
    a, b = split_element(ucol)
    for start, place in zip(g.lower_face_rows, g.face_places(0, a, b)):
        g.put_add(rim, place, lifted_up[start : start + d])


def upper_sums(g, acol, scale, ordered, both, x_next, mine, sums):
    d = g.d
    upper = dot(ordered[: g.used, :LANES], x_next[...])
    lifted = dot(both[: g.used, g.ch :], mine)

    def loader(k):
        here = jnp.where(acol == k, 1.0, 0.0)
        factor = scale[4 + k : 5 + k, :]
        lane = k * LANES

        def load(n):
            rows = slice(n * d, (n + 1) * d)
            return upper[rows, lane : lane + LANES] * factor + lifted[rows] * here

        return load

    for k, (a, b) in enumerate(g.columns):
        load = loader(k)
        near = a * d * g.e + b * d
        for i in range(d):
            for j in range(d):
                sums[pl.ds(near + i * g.plane + j * g.e, d), :] = load(g.face_groups + i * d + j)
    for k, (a, b) in enumerate(g.columns):
        g.add_layer(sums, 0, a, b, loader(k), start=d * d)


def held_places(g, ucol, lifted_up):
    d = g.d
    a, b = split_element(ucol)
    for n, place in enumerate(g.layer_places(0, a, b)):
        row = (g.face_groups + n) * d
        if row not in g.lower_face_rows[:-1]:
            start, stride = place
            rows = pl.ds(start, d, stride=stride) if stride > 1 else pl.ds(start, d)
            yield rows, None if lifted_up is None else lifted_up[row : row + d]


def middle_kernel(
    g, acol, ucol, count, scale, mass_wide, before, low_step, low_slab, face_own, x_face, ordered, both, both_t,
    own, held, kb, inner, outer,
    slab, x_top, step, own_out, held_out, inner_out, outer_out, kept,
    sums, next_plane, x_next, face_sums, up, down, up_out, down_out, rim, x_held,
):
    at = g.plane + g.ch
    d = g.d
    half = d * g.plane
    collect(inner, outer, up, down)
    for k in range(FACE // FOLD):
        kept[k * FOLD : (k + 1) * FOLD, : g.ch] = up[at : at + FOLD, k * g.ch : (k + 1) * g.ch]
    kept[FACE:, :] = up[at + FOLD :, :]
    face_low = kept[:FACE, : g.ch]
    const = kept[FACE:, :].astype(f32)
    mine, low = neighbour_terms(
        g, acol[0], count[0], both_t, own, held, kb, face_low, const, up, down, x_face, next_plane, x_next
    )
    lifted_up = dot(both[: g.used, : g.ch], low)
    upper_sums(g, acol[0], scale, ordered, both, x_next, mine, sums)
    a, b = split_element(ucol[0])
    g.add_face(sums, 0, a, b, lambda n: lifted_up[n * d : (n + 1) * d])
    rim_sums(g, ucol[0], const, face_own, face_low, low, lifted_up, up, rim)
    step[:half, :] = low_step[...]
    slab[:half, :] = low_slab[...]

    def finish(rows, added):
        wide = mass_wide[rows, :]
        one = (before[rows, :] + wide * (added * (1.0 / spectrum_half))).astype(bf16).astype(f32)
        step[rows, :] = one
        slab[rows, :] = (wide * one).astype(bf16).astype(f32)

    for rows, added in held_places(g, ucol[0], lifted_up):
        finish(rows, added)
    finish(pl.ds(0, g.plane), rim[...])
    for p in range(d):
        finish(pl.ds(half + p * g.plane, g.plane), sums[p * g.plane : (p + 1) * g.plane, :])
    gather_out(g, slab, x_top, x_held, ucol[0])
    outgoing(
        g, acol[0], scale, slab, x_top, x_held, ordered[:FACE, :], both_t, face_sums, up_out, down_out,
        own_out, held_out,
    )
    post(up_out, down_out, inner_out, outer_out)


def last_low_kernel(
    g, acol, ucol, count, scale, mass_wide, before, face_own, x_face, ordered, both, both_t,
    own, held, kb, kept, inner, outer,
    held_out, new, mine_out, x_next,
    sums, next_plane, x_held, x_rim, up, down, rim,
):
    d, ch = g.d, g.ch
    half = d * g.plane
    collect(inner, outer, up, down)
    face_low = kept[:FACE, :ch]
    const = kept[FACE:, :].astype(f32)
    mine, low = neighbour_terms(
        g, acol[0], count[0], both_t, own, held, kb, face_low, const, up, down, x_face, next_plane, x_next
    )
    mine_out[...] = mine
    lifted_up = dot(both[: g.used, :ch], low)
    starts = g.lower_face_rows
    pieces = [slice(starts[0] - d, starts[0] + (d + 1) * d)] + [slice(s - d, s + d) for s in starts[d:]]
    offsets = [d + n * d for n in range(d)] + [(d + 2) * d + n * 2 * d + d for n in range(3)]
    upper = dot(jnp.concatenate([ordered[p, :LANES] for p in pieces], axis=0), x_next[...])
    lifted = dot(jnp.concatenate([both[p, ch:] for p in pieces], axis=0), mine)
    sums[...] = jnp.zeros_like(sums)
    for k, (a, b) in enumerate(g.columns):
        here = jnp.where(acol[0] == k, 1.0, 0.0)
        factor = scale[4 + k : 5 + k, :]
        part = upper[:, k * LANES : (k + 1) * LANES] * factor + lifted * here
        g.add_face(sums, 0, a, b, lambda n: part[offsets[n] : offsets[n] + d])
    a, b = split_element(ucol[0])
    g.add_face(sums, 0, a, b, lambda n: lifted_up[n * d : (n + 1) * d])
    rim_sums(g, ucol[0], const, face_own, face_low, low, lifted_up, up, rim)

    def finish(rows, added):
        value = before[rows, :] + mass_wide[rows, :] * (added * (2.0 / spectrum_half))
        new[rows, :] = value.astype(bf16).astype(f32)

    for rows, added in held_places(g, ucol[0], lifted_up):
        finish(rows, added)
    finish(pl.ds(0, g.plane), rim[...])
    finish(pl.ds(half, g.plane), sums[...])
    g.gather_element(new, x_held, 0, 0, a, b, True)
    for k, (a, b) in enumerate(g.columns):
        g.gather_face(new, x_rim, k * LANES, 0, a, b)
    held_out[...] = dot(both_t[:ch, :], x_held[...]) + dot_chosen(face_low, x_rim, const)


def last_high_kernel(
    g, acol, ucol, count, scale, mass_wide, before, low_new, ordered, both, both_t, new, mine, x_next,
    filtered, own_out, sums, field, x_own, done, sems,
):
    d = g.d
    half = d * g.plane
    copies = [
        pltpu.make_async_copy(done.at[pl.ds(p, n)], filtered.at[pl.ds(p, n)], sems.at[k])
        for k, (p, n) in enumerate(((0, d), (d, d)))
    ]

    def give(planes):
        for p in planes:
            done[p] = field[p * g.plane : (p + 1) * g.plane, :].astype(bf16).reshape(g.e, g.e, LANES)

    field[:half, :] = low_new[...]
    for rows, _ in held_places(g, ucol[0], None):
        field[rows, :] = new[rows, :]
    field[: g.plane, :] = new[: g.plane, :]
    give(range(d))
    copies[0].start()
    field[half : half + g.plane, :] = new[half : half + g.plane, :]
    upper_sums(g, acol[0], scale, ordered, both, x_next, mine[...], sums)
    for p in range(1, d):
        rows = pl.ds(half + p * g.plane, g.plane)
        added = sums[p * g.plane : (p + 1) * g.plane, :]
        value = before[rows, :] + mass_wide[rows, :] * (added * (2.0 / spectrum_half))
        field[rows, :] = value.astype(bf16).astype(f32)
    give(range(d, g.e))
    copies[1].start()
    a, b = split_element(acol[0])
    g.gather_element(field, x_own, 0, half, a, b, False)
    own_out[...] = dot(both_t[g.ch :, :], x_own[...])
    for copy in copies:
        copy.wait()


def call(kernel, scalars, operands, outs, scratch, flops, limit=24 << 20, hbm=False, far_outs=0):
    smem = pl.BlockSpec(memory_space=pltpu.SMEM)
    vmem = pl.BlockSpec(memory_space=pltpu.VMEM)
    far = pl.BlockSpec(memory_space=pltpu.MemorySpace.HBM)
    moved = sum(v.size * v.dtype.itemsize for v in operands)
    if hbm:
        operands = [pltpu.with_memory_space_constraint(v, pltpu.MemorySpace.HBM) for v in operands]
    return pl.pallas_call(
        kernel,
        out_shape=[jax.ShapeDtypeStruct(s, t) for s, t in outs],
        in_specs=[smem] * len(scalars) + [far if hbm else vmem] * len(operands),
        out_specs=[far] * far_outs + [vmem] * (len(outs) - far_outs),
        scratch_shapes=[pltpu.VMEM(*s) if isinstance(s, tuple) else s for s in scratch],
        compiler_params=pltpu.CompilerParams(vmem_limit_bytes=limit),
        cost_estimate=pl.CostEstimate(flops=flops, bytes_accessed=moved, transcendentals=0),
    )(*scalars, *operands)


def per_device(
    wave_in, mass_scale, potential, elem_scale, stiffness, proj_lower, proj_upper, kb_coef,
    atom_column, chan_count, upper_column,
):
    extent = wave_in.shape[0]
    degree = extent // 2
    ch = kb_coef.shape[-1]
    order, used = row_order(degree)
    padded = order.shape[0]
    perm = jnp.asarray(order, f32)[None, :]
    g = Mesh1(degree, ch, used, padded)
    plane, nodes = g.plane, g.nodes
    scalars = (atom_column, upper_column, chan_count)
    part = ((ch, LANES), f32)
    slab_s, half_s, plane_s = ((nodes, LANES), f32), ((nodes // 2, LANES), f32), ((plane, LANES), f32)
    x_s, x_one_s = ((padded, 4 * LANES), bf16), ((padded, LANES), bf16)
    wire_s = ((plane + ch, LANES), bf16)
    wire_first_s = ((plane + ch + FOLD + CONST_ROWS, LANES), bf16)
    face_s = ((LANES, 4 * LANES), bf16)
    face_sum_s = ((FACE, 4 * LANES), f32)

    slab, x_top, mass_wide, wave, stiff, scale, order_row, pot, kb, both, both_t, own, held, inner, outer = call(
        functools.partial(start_kernel, g), scalars,
        (wave_in, mass_scale, elem_scale, stiffness, jnp.swapaxes(proj_lower, 1, 2), jnp.swapaxes(proj_upper, 1, 2),
         kb_coef, perm, potential),
        [slab_s, x_s, slab_s, (wave_in.shape, bf16), (stiffness.shape, bf16), ((8, LANES), f32), (perm.shape, f32),
         (potential.shape, f32), (kb_coef.shape, f32), ((padded, 2 * ch), bf16), ((2 * ch, padded), bf16), part, part,
         wire_first_s, wire_first_s],
        [plane_s, wire_first_s, wire_s, (mass_scale.shape, f32), (elem_scale.shape, f32),
         ((2 * ch, stiffness.shape[0]), bf16), x_one_s, pltpu.SemaphoreType.DMA((9,))], 10**8, hbm=True,
    )
    inner, outer = swapped(inner, outer, "space")
    ordered, pot_wide = call(
        functools.partial(order_kernel, g), (), (stiff, order_row, pot),
        [((padded, padded), bf16), slab_s], [], 2 * 10**9,
    )
    bulk_scratch = [slab_s, ((used, 2 * LANES), f32), x_s]
    before, low_step, low_slab, face_own, x_face = call(
        functools.partial(bulk_kernel, g), (), (scale, ordered, x_top, slab, pot_wide, mass_wide, wave),
        [slab_s, half_s, half_s, face_sum_s, face_s], bulk_scratch, 2 * 10**9,
    )
    shared = (ordered, both, both_t)
    slab, x_top, step, own, held, inner, outer, kept = call(
        functools.partial(middle_kernel, g), scalars,
        (scale, mass_wide, before, low_step, low_slab, face_own, x_face, *shared, own, held, kb, inner, outer),
        [slab_s, x_s, slab_s, part, part, wire_s, wire_s, ((FACE + CONST_ROWS, LANES), bf16)],
        [half_s, plane_s, face_s, plane_s, wire_first_s, wire_s, wire_s, wire_s, plane_s, x_one_s], 10**8,
    )
    inner, outer = swapped(inner, outer, "space")
    before, low_new, face_own, x_face = call(
        functools.partial(bulk_last_kernel, g), (),
        (scale, ordered, x_top, slab, pot_wide, mass_wide, wave, step),
        [slab_s, half_s, face_sum_s, face_s], bulk_scratch, 2 * 10**9,
    )
    held, new, mine, x_next = call(
        functools.partial(last_low_kernel, g), scalars,
        (scale, mass_wide, before, face_own, x_face, *shared, own, held, kb, kept, inner, outer),
        [part, ((nodes // 2 + plane, LANES), f32), ((ch, LANES), bf16), face_s],
        [plane_s, plane_s, x_one_s, face_s, wire_s, wire_s, plane_s], 10**8,
    )
    held = shifted(held, "space", -1)
    filtered, own = call(
        functools.partial(last_high_kernel, g), scalars,
        (scale, mass_wide, before, low_new, *shared, new, mine, x_next),
        [(wave_in.shape, bf16), part],
        [half_s, slab_s, x_one_s, (wave_in.shape, bf16), pltpu.SemaphoreType.DMA((2,))], 10**9, far_outs=1,
    )
    return filtered, (own + held)[None]


def solution(mesh):
    in_specs = (
        P("space", None, None, "band"),
        P("space", None),
        P("space", None),
        P("space", None, None),
        P(),
        P("space", None, None),
        P("space", None, None),
        P("space", None),
        P("space"),
        P("space"),
        P("space"),
    )
    out_specs = (P("space", None, None, "band"), P("space", None, "band"))
    return jax.shard_map(
        per_device, mesh=mesh, in_specs=in_specs, out_specs=out_specs, check_vma=False
    )
```

```python
import functools

import jax
import jax.numpy as jnp
import numpy as np
from jax import lax
from jax.experimental import pallas as pl
from jax.experimental.pallas import tpu as pltpu
from jax.sharding import PartitionSpec as P


spectrum_center = 1.0
spectrum_half = 6.0
f32 = jnp.float32
bf16 = jnp.bfloat16
LANES = 128
FACE = 96
FOLD = 32
CONST_ROWS = 16


def shifted(value, axis, steps):
    count = lax.axis_size(axis)
    pairs = [(source, (source + steps) % count) for source in range(count)]
    return lax.ppermute(value, axis, pairs)


def swapped(inner, outer, axis):
    count = lax.axis_size(axis)
    within = [(source, source ^ 1) for source in range(count)]
    across = [(source, (source + (1 if source % 2 else -1)) % count) for source in range(count)]
    outer = lax.ppermute(outer, axis, across)
    inner = lax.ppermute(inner, axis, within)
    return inner, outer


def is_odd():
    return lax.rem(lax.axis_index("space"), 2) == 1


def post(up, down, inner, outer):
    @pl.when(is_odd())
    def _():
        inner[: down.shape[0], :] = down[...]
        outer[: up.shape[0], :] = up[...]

    @pl.when(jnp.logical_not(is_odd()))
    def _():
        inner[: up.shape[0], :] = up[...]
        outer[: down.shape[0], :] = down[...]


def collect(inner, outer, up, down):
    @pl.when(is_odd())
    def _():
        up[...] = inner[: up.shape[0], :]
        down[...] = outer[: down.shape[0], :]

    @pl.when(jnp.logical_not(is_odd()))
    def _():
        up[...] = outer[: up.shape[0], :]
        down[...] = inner[: down.shape[0], :]


def row_order(degree):
    points = degree + 1

    def natural(i, j, l):
        return (i * points + j) * points + l

    inner = range(degree)
    order = [natural(degree, j, l) for j in inner for l in inner]
    order += [natural(degree, degree, l) for l in inner]
    order += [natural(degree, j, degree) for j in inner]
    order += [natural(degree, degree, degree)] + [-1] * (degree - 1)
    order += [natural(i, j, l) for i in inner for j in inner for l in inner]
    order += [natural(i, degree, l) for i in inner for l in inner]
    order += [natural(i, j, degree) for i in inner for j in inner]
    order += [natural(i, degree, degree) for i in inner]
    used = len(order)
    order += [-1] * (-used % 256)
    return np.asarray(order, np.int32), used


def dot(a, b):
    return jnp.dot(a, b, preferred_element_type=f32)


def dot_nt(a, b):
    return lax.dot_general(a, b, (((1,), (1,)), ((), ())), preferred_element_type=f32)


def onehot_rows(perm, count):
    rows = perm.shape[1]
    column = jnp.broadcast_to(perm, (8, rows)).T[:, :1]
    lane = lax.broadcasted_iota(jnp.int32, (rows, count), 1).astype(f32)
    return (column == lane).astype(bf16)


class Mesh1:
    def __init__(self, degree, channels, used, padded):
        self.d = degree
        self.e = 2 * degree
        self.plane = self.e * self.e
        self.nodes = self.e * self.plane
        self.ch = channels
        self.face_groups = degree + 3
        self.used = used
        self.padded = padded
        self.columns = [(a, b) for a in range(2) for b in range(2)]
        self.face_rows = degree * (degree + 1) ** 2
        rest = self.face_groups * degree
        lines = rest + degree**3
        self.lower_face_rows = [rest + j * degree for j in range(degree)]
        self.lower_face_rows += [lines, lines + degree**2, lines + 2 * degree**2]

    def far(self, index):
        return (1 - index) * self.d

    def aligned(self, value):
        return value if isinstance(value, int) else pl.multiple_of(value, self.d)

    def face_places(self, base, a, b):
        d, e = self.d, self.e
        near = base + a * d * e + b * d
        places = [(self.aligned(near + j * e), 1) for j in range(d)]
        places.append((self.aligned(base + self.far(a) * e + b * d), 1))
        places.append((base + a * d * e + self.far(b), e))
        places.append((self.aligned(base + self.far(a) * e + self.far(b)), 0))
        return places

    def layer_places(self, base, a, b):
        d, e, plane = self.d, self.e, self.plane
        near = base + a * d * e + b * d
        places = [(self.aligned(near + i * plane + j * e), 1) for i in range(d) for j in range(d)]
        places += [
            (self.aligned(base + i * plane + self.far(a) * e + b * d), 1) for i in range(d)
        ]
        places += [(base + i * plane + a * d * e + self.far(b), e) for i in range(d)]
        places.append((base + self.far(a) * e + self.far(b), plane))
        return places

    def take(self, ref, place):
        start, stride = place
        if stride > 1:
            return ref[pl.ds(start, self.d, stride=stride), :]
        value = ref[pl.ds(start, self.d), :]
        if stride == 0:
            first = lax.broadcasted_iota(jnp.int32, value.shape, 0) == 0
            value = jnp.where(first, value, 0.0)
        return value

    def put_add(self, ref, place, value):
        start, stride = place
        if stride > 1:
            rows = pl.ds(start, self.d, stride=stride)
        else:
            rows = pl.ds(start, self.d)
            if stride == 0:
                first = lax.broadcasted_iota(jnp.int32, value.shape, 0) == 0
                value = jnp.where(first, value, 0.0)
        ref[rows, :] = ref[rows, :] + value

    def pack(self, ref, lane, groups, first_row=0):
        lanes = pl.ds(lane, LANES)
        for at in range(0, len(groups), 2):
            pair = jnp.concatenate([groups[at], groups[at + 1]], axis=0).astype(bf16)
            ref[pl.ds(first_row + at * self.d, 2 * self.d), lanes] = pair

    def gather_element(self, slab, ref, lane, base, a, b, with_face):
        d = self.d
        zero = jnp.zeros((d, LANES), f32)
        if with_face:
            groups = [self.take(slab, p) for p in self.face_places(base + d * self.plane, a, b)]
        else:
            groups = [zero] * self.face_groups
        groups += [self.take(slab, p) for p in self.layer_places(base, a, b)]
        groups += [zero] * ((self.padded - self.used) // d)
        self.pack(ref, lane, groups)

    def gather_face(self, slab, ref, lane, base, a, b):
        zero = jnp.zeros((self.d, LANES), f32)
        groups = [self.take(slab, p) for p in self.face_places(base, a, b)]
        groups += [zero] * (LANES // self.d - len(groups))
        self.pack(ref, lane, groups)

    def add_face(self, ref, base, a, b, load):
        for g, place in enumerate(self.face_places(base, a, b)):
            self.put_add(ref, place, load(g))

    def add_layer(self, ref, base, a, b, load, start=0):
        for g, place in enumerate(self.layer_places(base, a, b)):
            if g >= start:
                self.put_add(ref, place, load(self.face_groups + g))


def live_weights(kb, count):
    lane = lax.broadcasted_iota(jnp.int32, kb.shape, 1)
    return kb * jnp.where(lane < count, 1.0, 0.0)


def as_column(row):
    size = row.shape[1]
    shape = (size, size)
    eye = lax.broadcasted_iota(jnp.int32, shape, 0) == lax.broadcasted_iota(jnp.int32, shape, 1)
    return jnp.sum(jnp.where(eye, jnp.broadcast_to(row, shape), 0.0), axis=1, keepdims=True)


def split_element(column):
    return column // 2, column % 2


def outgoing(g, acol, scale, slab, x_top, x_held, kface, both_t, face_sums, up, down, own_out, held_out):
    d, ch = g.d, g.ch
    own = dot(both_t[ch:, :], x_top[:, pl.ds(pl.multiple_of(acol * LANES, LANES), LANES)])
    held = dot(both_t[:ch, :], x_held[...])
    own_out[...] = own
    held_out[...] = held
    sums = dot(kface, x_top[...])
    face_sums[...] = jnp.zeros_like(face_sums)
    for k, (a, b) in enumerate(g.columns):
        part = sums[:, k * LANES : (k + 1) * LANES] * scale[4 + k : 5 + k, :]
        g.add_face(face_sums, 0, a, b, lambda n: part[n * d : (n + 1) * d])
    up[: g.plane, :] = face_sums[...].astype(bf16)
    up[g.plane : g.plane + ch, :] = own.astype(bf16)
    down[: g.plane, :] = slab[: g.plane, :].astype(bf16)
    down[g.plane :, :] = held.astype(bf16)


def gather_out(g, slab, x_top, x_held, ucol):
    for k, (a, b) in enumerate(g.columns):
        g.gather_element(slab, x_top, k * LANES, g.d * g.plane, a, b, False)
    a, b = split_element(ucol)
    g.gather_element(slab, x_held, 0, 0, a, b, True)


def widen(g, source, target):
    value = source[...]
    high = value.astype(bf16).astype(f32)
    middle = (value - high).astype(bf16).astype(f32)
    parts = jnp.concatenate([high, middle, value - high - middle], axis=0).T.astype(bf16)
    shape = (3 * g.e, 2 * LANES)
    row = lax.rem(lax.broadcasted_iota(jnp.int32, shape, 0), g.e)
    second = (lax.broadcasted_iota(jnp.int32, shape, 1) >= LANES).astype(jnp.int32)
    for p in range(0, g.e, 2):
        wide = dot(parts, (row == p + second).astype(f32).astype(bf16))
        target[p * g.plane : (p + 1) * g.plane, :] = wide[:, :LANES]
        target[(p + 1) * g.plane : (p + 2) * g.plane, :] = wide[:, LANES:]


def start_kernel(
    g, acol, ucol, count, wave_hbm, mass_hbm, scale_hbm, stiff_hbm, low_hbm, up_hbm, kb_hbm, perm_hbm, pot_hbm,
    slab, x_top, mass_wide, wave, stiff, scale, perm, pot, kb, both, both_t, own_out, held_out, inner, outer,
    face_sums, up, down, mass, scale_in, proj, x_held, natural, pair, sems,
):
    ch = g.ch
    copies = [
        pltpu.make_async_copy(source, target, sems.at[k])
        for k, (source, target) in enumerate((
            (mass_hbm, mass), (perm_hbm, perm), (wave_hbm, wave), (up_hbm.at[0], proj.at[:ch]),
            (low_hbm.at[0], proj.at[ch:]), (stiff_hbm, stiff), (scale_hbm, scale_in), (kb_hbm, kb), (pot_hbm, pot),
        ))
    ]
    for copy in copies:
        copy.start()
    copies[0].wait()
    widen(g, mass, mass_wide)
    copies[2].wait()
    for p in range(g.e):
        rows = pl.ds(p * g.plane, g.plane)
        start = wave[p].astype(f32).reshape(g.plane, LANES)
        slab[rows, :] = (mass_wide[rows, :] * start).astype(bf16).astype(f32)
    gather_out(g, slab, x_top, x_held, ucol[0])
    for k, copy in enumerate(copies):
        if k not in (0, 2):
            copy.wait()
    for k in range(8):
        one = scale_in[k // 4, k % 4 // 2 : k % 4 // 2 + 1, k % 2 : k % 2 + 1]
        scale[k : k + 1, :] = jnp.broadcast_to(one, (1, LANES))
    size = stiff.shape[0]
    first = g.face_rows // LANES * LANES
    natural[1] = jnp.zeros((g.used, LANES), f32)
    natural[0, :size, : 2 * ch] = proj[...].astype(f32).T
    natural[1, :size, : size - first] = stiff[:, first:].astype(f32)
    reorder_rows(g, natural, pair)
    turned = pair[:, : 2 * ch]
    both[...] = turned
    both_t[...] = pair[:, :LANES].astype(f32).T[: 2 * ch].astype(bf16)
    kface = dot_nt(onehot_rows(perm[:, :LANES] - first, LANES)[:FACE], pair[:, LANES:]).astype(bf16)
    outgoing(g, acol[0], scale, slab, x_top, x_held, kface, both_t, face_sums, up, down, own_out, held_out)
    at = g.plane + ch
    folded = [turned[k : k + FOLD, ch:] for k in range(0, FACE, FOLD)]
    rest = LANES - len(folded) * ch
    if rest:
        folded.append(jnp.zeros((FOLD, rest), bf16))
    up[at : at + FOLD, :] = jnp.concatenate(folded, axis=1)
    shape = (CONST_ROWS, LANES)
    row = lax.broadcasted_iota(jnp.int32, shape, 0)
    values = jnp.zeros(shape, f32)
    for k in range(4):
        chosen = jnp.where(acol[0] == k, 1.0, 0.0)
        values = jnp.where(row == k, chosen, values)
        full = jnp.broadcast_to(scale[4 + k : 5 + k, :], shape)
        high = full.astype(bf16).astype(f32)
        values = jnp.where(row == 4 + k, high, values)
        values = jnp.where(row == 8 + k, full - high, values)
    weights = live_weights(kb[...], count[0])
    weights = jnp.concatenate([weights, jnp.zeros((1, LANES - ch), f32)], axis=1)
    full = jnp.broadcast_to(weights, shape)
    high = full.astype(bf16).astype(f32)
    values = jnp.where(row == 12, high, values)
    values = jnp.where(row == 13, full - high, values)
    up[at + FOLD :, :] = values.astype(bf16)
    post(up, down, inner, outer)


def reorder_rows(g, natural, rows):
    d, n = g.d, g.d + 1
    places = [((d * n + j) * n, 1) for j in range(n)] + [(d * n * n + d, n), (d * n * n + d * n + d, 0)]
    places += [((i * n + j) * n, 1) for i in range(d) for j in range(d)]
    places += [((i * n + d) * n, 1) for i in range(d)]
    places += [(i * n * n + d, n) for i in range(d)]
    places += [(d * n + d, n * n)]
    for t in range(natural.shape[0]):
        groups = []
        for start, stride in places:
            group = natural[t, pl.ds(start, d, stride=max(stride, 1)), :]
            if stride == 0:
                group = jnp.where(lax.broadcasted_iota(jnp.int32, group.shape, 0) == 0, group, 0.0)
            groups.append(group)
        g.pack(rows, t * LANES, groups)
    rows[g.used :, :] = jnp.zeros((g.padded - g.used, rows.shape[1]), bf16)


def order_kernel(g, stiff, perm, pot, ordered, pot_wide, natural, rows):
    size = stiff.shape[0]
    tiles = natural.shape[0]
    for t in range(tiles):
        lanes = min(LANES, size - t * LANES)
        if lanes < LANES:
            natural[t] = jnp.zeros((g.used, LANES), f32)
        natural[t, :size, :lanes] = stiff[:, t * LANES : t * LANES + lanes].astype(f32)
    reorder_rows(g, natural, rows)
    sublane = lax.broadcasted_iota(jnp.int32, (rows.shape[1], g.padded), 0).astype(f32)
    pick_t = (perm[...] == sublane).astype(f32).astype(bf16)
    ordered[...] = dot(rows[...], pick_t).astype(bf16)
    widen(g, pot, pot_wide)


def bulk_sums(g, scale, ordered, x_top, slab, pot_wide, face_own, x_face, total, z, x_low):
    d = g.d
    for p in range(g.e):
        rows = pl.ds(p * g.plane, g.plane)
        total[rows, :] = pot_wide[rows, :] * slab[rows, :]
    for k, (a, b) in enumerate(g.columns):
        g.gather_element(slab, x_low, k * LANES, 0, a, b, True)
        g.gather_face(slab, x_face, k * LANES, 0, a, b)
    for layer, x in enumerate((x_low, x_top)):
        for a in range(2):
            lane = a * 2 * LANES
            z[...] = dot(ordered[: g.used, :], x[:, lane : lane + 2 * LANES])
            for b in range(2):
                k = layer * 4 + a * 2 + b
                factor = scale[k : k + 1, :]

                def load(n):
                    return z[n * d : (n + 1) * d, b * LANES : (b + 1) * LANES] * factor

                if layer == 0:
                    g.add_face(total, d * g.plane, a, b, load)
                g.add_layer(total, layer * d * g.plane, a, b, load)
    face_own[...] = dot(ordered[:FACE, :LANES], x_face[...])


def bulk_kernel(
    g, scale, ordered, x_top, slab, pot_wide, mass_wide, wave,
    before, low_step, low_slab, face_own, x_face, total, z, x_low,
):
    bulk_sums(g, scale, ordered, x_top, slab, pot_wide, face_own, x_face, total, z, x_low)
    for p in range(g.e):
        rows = pl.ds(p * g.plane, g.plane)
        wide = mass_wide[rows, :]
        base = wave[p].astype(f32).reshape(g.plane, LANES)
        value = (wide * total[rows, :] - spectrum_center * base) * (1.0 / spectrum_half)
        before[rows, :] = value
        if p < g.d:
            one = value.astype(bf16).astype(f32)
            low_step[rows, :] = one
            low_slab[rows, :] = (wide * one).astype(bf16).astype(f32)


def bulk_last_kernel(
    g, scale, ordered, x_top, slab, pot_wide, mass_wide, wave, step,
    before, low_new, face_own, x_face, total, z, x_low,
):
    bulk_sums(g, scale, ordered, x_top, slab, pot_wide, face_own, x_face, total, z, x_low)
    for p in range(g.e):
        rows = pl.ds(p * g.plane, g.plane)
        base = wave[p].astype(f32).reshape(g.plane, LANES)
        image = mass_wide[rows, :] * total[rows, :]
        value = (image - spectrum_center * step[rows, :]) * (2.0 / spectrum_half) - base
        before[rows, :] = value
        if p < g.d:
            low_new[rows, :] = value.astype(bf16).astype(f32)


def neighbour_terms(g, acol, count, both_t, own, held, kb, face_low, const, up, down, x_face, next_plane, x_next):
    ch = g.ch
    next_plane[...] = down[: g.plane, :].astype(f32)
    for k, (a, b) in enumerate(g.columns):
        g.gather_face(next_plane, x_next, k * LANES, 0, a, b)
    mine = own[...] + down[g.plane :, :].astype(f32)
    column = pl.ds(pl.multiple_of(acol * LANES, LANES), LANES)
    mine = mine + dot(both_t[ch:, :LANES], x_next[:, column])
    mine = (as_column(live_weights(kb[...], count)) * mine).astype(bf16)
    weights_low = as_column(const[12:13, :ch] + const[13:14, :ch])
    low = up[g.plane : g.plane + ch, :].astype(f32) + held[...]
    low = low + dot_chosen(face_low, x_face, const)
    low = (weights_low * low).astype(bf16)
    return mine, low


def dot_chosen(face, x_face, const):
    rows = face.shape[0]
    chosen = jnp.zeros((rows, LANES), f32)
    for k in range(4):
        chosen = chosen + x_face[:rows, k * LANES : (k + 1) * LANES].astype(f32) * const[k : k + 1, :]
    face_t = face.astype(f32).T.astype(bf16)
    return dot(face_t, chosen.astype(bf16))


def rim_sums(g, ucol, const, face_own, face_low, low, lifted_up, up, rim):
    d = g.d
    lifted_low = dot(face_low, low)
    rim[...] = up[: g.plane, :].astype(f32)
    for k, (a, b) in enumerate(g.columns):
        part = face_own[:, k * LANES : (k + 1) * LANES] * (const[4 + k : 5 + k, :] + const[8 + k : 9 + k, :])
        part = part + lifted_low * const[k : k + 1, :]
        g.add_face(rim, 0, a, b, lambda n: part[n * d : (n + 1) * d])
    a, b = split_element(ucol)
    for start, place in zip(g.lower_face_rows, g.face_places(0, a, b)):
        g.put_add(rim, place, lifted_up[start : start + d])


def upper_sums(g, acol, scale, ordered, both, x_next, mine, sums):
    d = g.d
    upper = dot(ordered[: g.used, :LANES], x_next[...])
    lifted = dot(both[: g.used, g.ch :], mine)

    def loader(k):
        factor = scale[4 + k : 5 + k, :]
        lane = k * LANES
        return lambda n: upper[n * d : (n + 1) * d, lane : lane + LANES] * factor

    for k, (a, b) in enumerate(g.columns):
        load = loader(k)
        near = a * d * g.e + b * d
        for i in range(d):
            for j in range(d):
                sums[pl.ds(near + i * g.plane + j * g.e, d), :] = load(g.face_groups + i * d + j)
    for k, (a, b) in enumerate(g.columns):
        g.add_layer(sums, 0, a, b, loader(k), start=d * d)
    a, b = split_element(acol)
    g.add_layer(sums, 0, a, b, lambda n: lifted[n * d : (n + 1) * d])


def held_places(g, ucol, lifted_up):
    d = g.d
    a, b = split_element(ucol)
    for n, place in enumerate(g.layer_places(0, a, b)):
        row = (g.face_groups + n) * d
        if row not in g.lower_face_rows[:-1]:
            start, stride = place
            rows = pl.ds(start, d, stride=stride) if stride > 1 else pl.ds(start, d)
            yield rows, None if lifted_up is None else lifted_up[row : row + d]


def middle_kernel(
    g, acol, ucol, count, scale, mass_wide, before, low_step, low_slab, face_own, x_face, ordered, both, both_t,
    own, held, kb, inner, outer,
    slab, x_top, step, own_out, held_out, inner_out, outer_out, kept,
    sums, next_plane, x_next, face_sums, up, down, up_out, down_out, rim, x_held,
):
    at = g.plane + g.ch
    d = g.d
    half = d * g.plane
    collect(inner, outer, up, down)
    for k in range(FACE // FOLD):
        kept[k * FOLD : (k + 1) * FOLD, : g.ch] = up[at : at + FOLD, k * g.ch : (k + 1) * g.ch]
    kept[FACE:, :] = up[at + FOLD :, :]
    face_low = kept[:FACE, : g.ch]
    const = kept[FACE:, :].astype(f32)
    mine, low = neighbour_terms(
        g, acol[0], count[0], both_t, own, held, kb, face_low, const, up, down, x_face, next_plane, x_next
    )
    lifted_up = dot(both[: g.used, : g.ch], low)
    upper_sums(g, acol[0], scale, ordered, both, x_next, mine, sums)
    a, b = split_element(ucol[0])
    g.add_face(sums, 0, a, b, lambda n: lifted_up[n * d : (n + 1) * d])
    rim_sums(g, ucol[0], const, face_own, face_low, low, lifted_up, up, rim)
    step[:half, :] = low_step[...]
    slab[:half, :] = low_slab[...]

    def finish(rows, added):
        wide = mass_wide[rows, :]
        one = (before[rows, :] + wide * (added * (1.0 / spectrum_half))).astype(bf16).astype(f32)
        step[rows, :] = one
        slab[rows, :] = (wide * one).astype(bf16).astype(f32)

    for rows, added in held_places(g, ucol[0], lifted_up):
        finish(rows, added)
    finish(pl.ds(0, g.plane), rim[...])
    for p in range(d):
        finish(pl.ds(half + p * g.plane, g.plane), sums[p * g.plane : (p + 1) * g.plane, :])
    gather_out(g, slab, x_top, x_held, ucol[0])
    outgoing(
        g, acol[0], scale, slab, x_top, x_held, ordered[:FACE, :], both_t, face_sums, up_out, down_out,
        own_out, held_out,
    )
    post(up_out, down_out, inner_out, outer_out)


def last_low_kernel(
    g, acol, ucol, count, scale, mass_wide, before, face_own, x_face, ordered, both, both_t,
    own, held, kb, kept, inner, outer,
    held_out, new, mine_out, x_next,
    sums, next_plane, x_held, x_rim, up, down, rim,
):
    d, ch = g.d, g.ch
    half = d * g.plane
    collect(inner, outer, up, down)
    face_low = kept[:FACE, :ch]
    const = kept[FACE:, :].astype(f32)
    mine, low = neighbour_terms(
        g, acol[0], count[0], both_t, own, held, kb, face_low, const, up, down, x_face, next_plane, x_next
    )
    mine_out[...] = mine
    lifted_up = dot(both[: g.used, :ch], low)
    starts = g.lower_face_rows
    pieces = [slice(starts[0] - d, starts[0] + (d + 1) * d)] + [slice(s - d, s + d) for s in starts[d:]]
    offsets = [d + n * d for n in range(d)] + [(d + 2) * d + n * 2 * d + d for n in range(3)]
    upper = dot(jnp.concatenate([ordered[p, :LANES] for p in pieces], axis=0), x_next[...])
    lifted = dot(jnp.concatenate([both[p, ch:] for p in pieces], axis=0), mine)
    sums[...] = jnp.zeros_like(sums)
    for k, (a, b) in enumerate(g.columns):
        here = jnp.where(acol[0] == k, 1.0, 0.0)
        factor = scale[4 + k : 5 + k, :]
        part = upper[:, k * LANES : (k + 1) * LANES] * factor + lifted * here
        g.add_face(sums, 0, a, b, lambda n: part[offsets[n] : offsets[n] + d])
    a, b = split_element(ucol[0])
    g.add_face(sums, 0, a, b, lambda n: lifted_up[n * d : (n + 1) * d])
    rim_sums(g, ucol[0], const, face_own, face_low, low, lifted_up, up, rim)

    def finish(rows, added):
        value = before[rows, :] + mass_wide[rows, :] * (added * (2.0 / spectrum_half))
        new[rows, :] = value.astype(bf16).astype(f32)

    for rows, added in held_places(g, ucol[0], lifted_up):
        finish(rows, added)
    finish(pl.ds(0, g.plane), rim[...])
    finish(pl.ds(half, g.plane), sums[...])
    g.gather_element(new, x_held, 0, 0, a, b, True)
    for k, (a, b) in enumerate(g.columns):
        g.gather_face(new, x_rim, k * LANES, 0, a, b)
    held_out[...] = dot(both_t[:ch, :], x_held[...]) + dot_chosen(face_low, x_rim, const)


def last_high_kernel(
    g, acol, ucol, count, scale, mass_wide, before, low_new, ordered, both, both_t, new, mine, x_next,
    filtered, own_out, sums, field, x_own, done, sems,
):
    d = g.d
    half = d * g.plane
    copies = [
        pltpu.make_async_copy(done.at[pl.ds(p, n)], filtered.at[pl.ds(p, n)], sems.at[k])
        for k, (p, n) in enumerate(((0, d), (d, d)))
    ]

    def give(planes):
        for p in planes:
            done[p] = field[p * g.plane : (p + 1) * g.plane, :].astype(bf16).reshape(g.e, g.e, LANES)

    field[:half, :] = low_new[...]
    for rows, _ in held_places(g, ucol[0], None):
        field[rows, :] = new[rows, :]
    field[: g.plane, :] = new[: g.plane, :]
    give(range(d))
    copies[0].start()
    field[half : half + g.plane, :] = new[half : half + g.plane, :]
    upper_sums(g, acol[0], scale, ordered, both, x_next, mine[...], sums)
    for p in range(1, d):
        rows = pl.ds(half + p * g.plane, g.plane)
        added = sums[p * g.plane : (p + 1) * g.plane, :]
        value = before[rows, :] + mass_wide[rows, :] * (added * (2.0 / spectrum_half))
        field[rows, :] = value.astype(bf16).astype(f32)
    give(range(d, g.e))
    copies[1].start()
    a, b = split_element(acol[0])
    g.gather_element(field, x_own, 0, half, a, b, False)
    own_out[...] = dot(both_t[g.ch :, :], x_own[...])
    for copy in copies:
        copy.wait()


def call(kernel, scalars, operands, outs, scratch, flops, limit=24 << 20, hbm=False, far_outs=0):
    smem = pl.BlockSpec(memory_space=pltpu.SMEM)
    vmem = pl.BlockSpec(memory_space=pltpu.VMEM)
    far = pl.BlockSpec(memory_space=pltpu.MemorySpace.HBM)
    moved = sum(v.size * v.dtype.itemsize for v in operands)
    if hbm:
        operands = [pltpu.with_memory_space_constraint(v, pltpu.MemorySpace.HBM) for v in operands]
    return pl.pallas_call(
        kernel,
        out_shape=[jax.ShapeDtypeStruct(s, t) for s, t in outs],
        in_specs=[smem] * len(scalars) + [far if hbm else vmem] * len(operands),
        out_specs=[far] * far_outs + [vmem] * (len(outs) - far_outs),
        scratch_shapes=[pltpu.VMEM(*s) if isinstance(s, tuple) else s for s in scratch],
        compiler_params=pltpu.CompilerParams(vmem_limit_bytes=limit),
        cost_estimate=pl.CostEstimate(flops=flops, bytes_accessed=moved, transcendentals=0),
    )(*scalars, *operands)


def per_device(
    wave_in, mass_scale, potential, elem_scale, stiffness, proj_lower, proj_upper, kb_coef,
    atom_column, chan_count, upper_column,
):
    extent = wave_in.shape[0]
    degree = extent // 2
    ch = kb_coef.shape[-1]
    order, used = row_order(degree)
    padded = order.shape[0]
    perm = jnp.asarray(order, f32)[None, :]
    g = Mesh1(degree, ch, used, padded)
    plane, nodes = g.plane, g.nodes
    scalars = (atom_column, upper_column, chan_count)
    part = ((ch, LANES), f32)
    slab_s, half_s, plane_s = ((nodes, LANES), f32), ((nodes // 2, LANES), f32), ((plane, LANES), f32)
    x_s, x_one_s = ((padded, 4 * LANES), bf16), ((padded, LANES), bf16)
    wire_s = ((plane + ch, LANES), bf16)
    wire_first_s = ((plane + ch + FOLD + CONST_ROWS, LANES), bf16)
    face_s = ((LANES, 4 * LANES), bf16)
    face_sum_s = ((FACE, 4 * LANES), f32)

    slab, x_top, mass_wide, wave, stiff, scale, order_row, pot, kb, both, both_t, own, held, inner, outer = call(
        functools.partial(start_kernel, g), scalars,
        (wave_in, mass_scale, elem_scale, stiffness, jnp.swapaxes(proj_lower, 1, 2), jnp.swapaxes(proj_upper, 1, 2),
         kb_coef, perm, potential),
        [slab_s, x_s, slab_s, (wave_in.shape, bf16), (stiffness.shape, bf16), ((8, LANES), f32), (perm.shape, f32),
         (potential.shape, f32), (kb_coef.shape, f32), ((padded, 2 * ch), bf16), ((2 * ch, padded), bf16), part, part,
         wire_first_s, wire_first_s],
        [plane_s, wire_first_s, wire_s, (mass_scale.shape, f32), (elem_scale.shape, f32),
         ((2 * ch, stiffness.shape[0]), bf16), x_one_s, ((2, used, LANES), f32), ((padded, 2 * LANES), bf16),
         pltpu.SemaphoreType.DMA((9,))], 10**8, hbm=True,
    )
    inner, outer = swapped(inner, outer, "space")
    ordered, pot_wide = call(
        functools.partial(order_kernel, g), (), (stiff, order_row, pot),
        [((padded, padded), bf16), slab_s],
        [((-(-stiffness.shape[0] // LANES), used, LANES), f32), ((padded, padded), bf16)], 2 * 10**9,
    )
    bulk_scratch = [slab_s, ((used, 2 * LANES), f32), x_s]
    before, low_step, low_slab, face_own, x_face = call(
        functools.partial(bulk_kernel, g), (), (scale, ordered, x_top, slab, pot_wide, mass_wide, wave),
        [slab_s, half_s, half_s, face_sum_s, face_s], bulk_scratch, 2 * 10**9,
    )
    shared = (ordered, both, both_t)
    slab, x_top, step, own, held, inner, outer, kept = call(
        functools.partial(middle_kernel, g), scalars,
        (scale, mass_wide, before, low_step, low_slab, face_own, x_face, *shared, own, held, kb, inner, outer),
        [slab_s, x_s, slab_s, part, part, wire_s, wire_s, ((FACE + CONST_ROWS, LANES), bf16)],
        [half_s, plane_s, face_s, plane_s, wire_first_s, wire_s, wire_s, wire_s, plane_s, x_one_s], 10**8,
    )
    inner, outer = swapped(inner, outer, "space")
    before, low_new, face_own, x_face = call(
        functools.partial(bulk_last_kernel, g), (),
        (scale, ordered, x_top, slab, pot_wide, mass_wide, wave, step),
        [slab_s, half_s, face_sum_s, face_s], bulk_scratch, 2 * 10**9,
    )
    held, new, mine, x_next = call(
        functools.partial(last_low_kernel, g), scalars,
        (scale, mass_wide, before, face_own, x_face, *shared, own, held, kb, kept, inner, outer),
        [part, ((nodes // 2 + plane, LANES), f32), ((ch, LANES), bf16), face_s],
        [plane_s, plane_s, x_one_s, face_s, wire_s, wire_s, plane_s], 10**8,
    )
    held = shifted(held, "space", -1)
    filtered, own = call(
        functools.partial(last_high_kernel, g), scalars,
        (scale, mass_wide, before, low_new, *shared, new, mine, x_next),
        [(wave_in.shape, bf16), part],
        [half_s, slab_s, x_one_s, (wave_in.shape, bf16), pltpu.SemaphoreType.DMA((2,))], 10**9, far_outs=1,
    )
    return filtered, (own + held)[None]


def solution(mesh):
    in_specs = (
        P("space", None, None, "band"),
        P("space", None),
        P("space", None),
        P("space", None, None),
        P(),
        P("space", None, None),
        P("space", None, None),
        P("space", None),
        P("space"),
        P("space"),
        P("space"),
    )
    out_specs = (P("space", None, None, "band"), P("space", None, "band"))
    return jax.shard_map(
        per_device, mesh=mesh, in_specs=in_specs, out_specs=out_specs, check_vma=False
    )
```

```python
import functools

import jax
import jax.numpy as jnp
import numpy as np
from jax import lax
from jax.experimental import pallas as pl
from jax.experimental.pallas import tpu as pltpu
from jax.sharding import PartitionSpec as P


spectrum_center = 1.0
spectrum_half = 6.0
f32 = jnp.float32
bf16 = jnp.bfloat16
LANES = 128
FACE = 96
FOLD = 32
CONST_ROWS = 16


def shifted(value, axis, steps):
    count = lax.axis_size(axis)
    pairs = [(source, (source + steps) % count) for source in range(count)]
    return lax.ppermute(value, axis, pairs)


def swapped(inner, outer, axis):
    count = lax.axis_size(axis)
    within = [(source, source ^ 1) for source in range(count)]
    across = [(source, (source + (1 if source % 2 else -1)) % count) for source in range(count)]
    outer = lax.ppermute(outer, axis, across)
    inner = lax.ppermute(inner, axis, within)
    return inner, outer


def is_odd():
    return lax.rem(lax.axis_index("space"), 2) == 1


def post(up, down, inner, outer):
    @pl.when(is_odd())
    def _():
        inner[: down.shape[0], :] = down[...]
        outer[: up.shape[0], :] = up[...]

    @pl.when(jnp.logical_not(is_odd()))
    def _():
        inner[: up.shape[0], :] = up[...]
        outer[: down.shape[0], :] = down[...]


def collect(inner, outer, up, down):
    @pl.when(is_odd())
    def _():
        up[...] = inner[: up.shape[0], :]
        down[...] = outer[: down.shape[0], :]

    @pl.when(jnp.logical_not(is_odd()))
    def _():
        up[...] = outer[: up.shape[0], :]
        down[...] = inner[: down.shape[0], :]


def row_order(degree):
    points = degree + 1

    def natural(i, j, l):
        return (i * points + j) * points + l

    inner = range(degree)
    order = [natural(degree, j, l) for j in inner for l in inner]
    order += [natural(degree, degree, l) for l in inner]
    order += [natural(degree, j, degree) for j in inner]
    order += [natural(degree, degree, degree)] + [-1] * (degree - 1)
    order += [natural(i, j, l) for i in inner for j in inner for l in inner]
    order += [natural(i, degree, l) for i in inner for l in inner]
    order += [natural(i, j, degree) for i in inner for j in inner]
    order += [natural(i, degree, degree) for i in inner]
    used = len(order)
    order += [-1] * (-used % 256)
    return np.asarray(order, np.int32), used


def dot(a, b):
    return jnp.dot(a, b, preferred_element_type=f32)


def dot_nt(a, b):
    return lax.dot_general(a, b, (((1,), (1,)), ((), ())), preferred_element_type=f32)


def onehot_rows(perm, count):
    rows = perm.shape[1]
    column = jnp.broadcast_to(perm, (8, rows)).T[:, :1]
    lane = lax.broadcasted_iota(jnp.int32, (rows, count), 1).astype(f32)
    return (column == lane).astype(bf16)


class Mesh1:
    def __init__(self, degree, channels, used, padded):
        self.d = degree
        self.e = 2 * degree
        self.plane = self.e * self.e
        self.nodes = self.e * self.plane
        self.ch = channels
        self.face_groups = degree + 3
        self.used = used
        self.padded = padded
        self.columns = [(a, b) for a in range(2) for b in range(2)]
        self.face_rows = degree * (degree + 1) ** 2
        rest = self.face_groups * degree
        lines = rest + degree**3
        self.lower_face_rows = [rest + j * degree for j in range(degree)]
        self.lower_face_rows += [lines, lines + degree**2, lines + 2 * degree**2]

    def far(self, index):
        return (1 - index) * self.d

    def aligned(self, value):
        return value if isinstance(value, int) else pl.multiple_of(value, self.d)

    def face_places(self, base, a, b):
        d, e = self.d, self.e
        near = base + a * d * e + b * d
        places = [(self.aligned(near + j * e), 1) for j in range(d)]
        places.append((self.aligned(base + self.far(a) * e + b * d), 1))
        places.append((base + a * d * e + self.far(b), e))
        places.append((self.aligned(base + self.far(a) * e + self.far(b)), 0))
        return places

    def layer_places(self, base, a, b):
        d, e, plane = self.d, self.e, self.plane
        near = base + a * d * e + b * d
        places = [(self.aligned(near + i * plane + j * e), 1) for i in range(d) for j in range(d)]
        places += [
            (self.aligned(base + i * plane + self.far(a) * e + b * d), 1) for i in range(d)
        ]
        places += [(base + i * plane + a * d * e + self.far(b), e) for i in range(d)]
        places.append((base + self.far(a) * e + self.far(b), plane))
        return places

    def take(self, ref, place):
        start, stride = place
        if stride > 1:
            return ref[pl.ds(start, self.d, stride=stride), :]
        value = ref[pl.ds(start, self.d), :]
        if stride == 0:
            first = lax.broadcasted_iota(jnp.int32, value.shape, 0) == 0
            value = jnp.where(first, value, 0.0)
        return value

    def put_add(self, ref, place, value):
        start, stride = place
        if stride > 1:
            rows = pl.ds(start, self.d, stride=stride)
        else:
            rows = pl.ds(start, self.d)
            if stride == 0:
                first = lax.broadcasted_iota(jnp.int32, value.shape, 0) == 0
                value = jnp.where(first, value, 0.0)
        ref[rows, :] = ref[rows, :] + value

    def pack(self, ref, lane, groups, first_row=0):
        lanes = pl.ds(lane, LANES)
        for at in range(0, len(groups), 2):
            pair = jnp.concatenate([groups[at], groups[at + 1]], axis=0).astype(bf16)
            ref[pl.ds(first_row + at * self.d, 2 * self.d), lanes] = pair

    def gather_element(self, slab, ref, lane, base, a, b, with_face):
        d = self.d
        zero = jnp.zeros((d, LANES), f32)
        if with_face:
            groups = [self.take(slab, p) for p in self.face_places(base + d * self.plane, a, b)]
        else:
            groups = [zero] * self.face_groups
        groups += [self.take(slab, p) for p in self.layer_places(base, a, b)]
        groups += [zero] * ((self.padded - self.used) // d)
        self.pack(ref, lane, groups)

    def gather_face(self, slab, ref, lane, base, a, b):
        zero = jnp.zeros((self.d, LANES), f32)
        groups = [self.take(slab, p) for p in self.face_places(base, a, b)]
        groups += [zero] * (LANES // self.d - len(groups))
        self.pack(ref, lane, groups)

    def add_face(self, ref, base, a, b, load):
        for g, place in enumerate(self.face_places(base, a, b)):
            self.put_add(ref, place, load(g))

    def add_layer(self, ref, base, a, b, load, start=0):
        for g, place in enumerate(self.layer_places(base, a, b)):
            if g >= start:
                self.put_add(ref, place, load(self.face_groups + g))


def live_weights(kb, count):
    lane = lax.broadcasted_iota(jnp.int32, kb.shape, 1)
    return kb * jnp.where(lane < count, 1.0, 0.0)


def as_column(row):
    size = row.shape[1]
    shape = (size, size)
    eye = lax.broadcasted_iota(jnp.int32, shape, 0) == lax.broadcasted_iota(jnp.int32, shape, 1)
    return jnp.sum(jnp.where(eye, jnp.broadcast_to(row, shape), 0.0), axis=1, keepdims=True)


def split_element(column):
    return column // 2, column % 2


def outgoing(g, acol, scale, slab, x_top, x_held, kface, both_t, face_sums, up, down, own_out, held_out):
    d, ch = g.d, g.ch
    own = dot(both_t[ch:, :], x_top[:, pl.ds(pl.multiple_of(acol * LANES, LANES), LANES)])
    held = dot(both_t[:ch, :], x_held[...])
    own_out[...] = own
    held_out[...] = held
    sums = dot(kface, x_top[...])
    face_sums[...] = jnp.zeros_like(face_sums)
    for k, (a, b) in enumerate(g.columns):
        part = sums[:, k * LANES : (k + 1) * LANES] * scale[4 + k : 5 + k, :]
        g.add_face(face_sums, 0, a, b, lambda n: part[n * d : (n + 1) * d])
    up[: g.plane, :] = face_sums[...].astype(bf16)
    up[g.plane : g.plane + ch, :] = own.astype(bf16)
    down[: g.plane, :] = slab[: g.plane, :].astype(bf16)
    down[g.plane :, :] = held.astype(bf16)


def gather_out(g, slab, x_top, x_held, ucol):
    for k, (a, b) in enumerate(g.columns):
        g.gather_element(slab, x_top, k * LANES, g.d * g.plane, a, b, False)
    a, b = split_element(ucol)
    g.gather_element(slab, x_held, 0, 0, a, b, True)


def widen(g, source, target):
    value = source[...]
    high = value.astype(bf16).astype(f32)
    middle = (value - high).astype(bf16).astype(f32)
    parts = jnp.concatenate([high, middle, value - high - middle], axis=0).T.astype(bf16)
    shape = (3 * g.e, 2 * LANES)
    row = lax.rem(lax.broadcasted_iota(jnp.int32, shape, 0), g.e)
    second = (lax.broadcasted_iota(jnp.int32, shape, 1) >= LANES).astype(jnp.int32)
    for p in range(0, g.e, 2):
        wide = dot(parts, (row == p + second).astype(f32).astype(bf16))
        target[p * g.plane : (p + 1) * g.plane, :] = wide[:, :LANES]
        target[(p + 1) * g.plane : (p + 2) * g.plane, :] = wide[:, LANES:]


def start_kernel(
    g, acol, ucol, count, wave_hbm, mass_hbm, scale_hbm, stiff_hbm, low_hbm, up_hbm, kb_hbm, perm_hbm, pot_hbm,
    slab, x_top, mass_wide, wave, stiff, scale, perm, pot, kb, both, both_t, own_out, held_out, inner, outer,
    face_sums, up, down, mass, scale_in, proj, x_held, natural, pair, sems,
):
    ch = g.ch
    quarter = g.e // 4
    copies = [
        pltpu.make_async_copy(source, target, sems.at[k])
        for k, (source, target) in enumerate((
            (mass_hbm, mass),
            *((wave_hbm.at[pl.ds(p, quarter)], wave.at[pl.ds(p, quarter)]) for p in range(0, g.e, quarter)),
            (up_hbm.at[0], proj.at[:ch]), (low_hbm.at[0], proj.at[ch:]), (perm_hbm, perm), (stiff_hbm, stiff),
            (scale_hbm, scale_in), (kb_hbm, kb), (pot_hbm, pot),
        ))
    ]
    for copy in copies:
        copy.start()
    copies[0].wait()
    widen(g, mass, mass_wide)
    for p in range(g.e):
        if p % quarter == 0:
            copies[1 + p // quarter].wait()
        rows = pl.ds(p * g.plane, g.plane)
        start = wave[p].astype(f32).reshape(g.plane, LANES)
        slab[rows, :] = (mass_wide[rows, :] * start).astype(bf16).astype(f32)
    gather_out(g, slab, x_top, x_held, ucol[0])
    for copy in copies[5:]:
        copy.wait()
    for k in range(8):
        one = scale_in[k // 4, k % 4 // 2 : k % 4 // 2 + 1, k % 2 : k % 2 + 1]
        scale[k : k + 1, :] = jnp.broadcast_to(one, (1, LANES))
    size = stiff.shape[0]
    first = g.face_rows // LANES * LANES
    natural[1] = jnp.zeros((g.used, LANES), f32)
    natural[0, :size, : 2 * ch] = proj[...].astype(f32).T
    natural[1, :size, : size - first] = stiff[:, first:].astype(f32)
    reorder_rows(g, natural, pair)
    turned = pair[:, : 2 * ch]
    both[...] = turned
    both_t[...] = pair[:, :LANES].astype(f32).T[: 2 * ch].astype(bf16)
    kface = dot_nt(onehot_rows(perm[:, :LANES] - first, LANES)[:FACE], pair[:, LANES:]).astype(bf16)
    outgoing(g, acol[0], scale, slab, x_top, x_held, kface, both_t, face_sums, up, down, own_out, held_out)
    at = g.plane + ch
    folded = [turned[k : k + FOLD, ch:] for k in range(0, FACE, FOLD)]
    rest = LANES - len(folded) * ch
    if rest:
        folded.append(jnp.zeros((FOLD, rest), bf16))
    up[at : at + FOLD, :] = jnp.concatenate(folded, axis=1)
    shape = (CONST_ROWS, LANES)
    row = lax.broadcasted_iota(jnp.int32, shape, 0)
    values = jnp.zeros(shape, f32)
    for k in range(4):
        chosen = jnp.where(acol[0] == k, 1.0, 0.0)
        values = jnp.where(row == k, chosen, values)
        full = jnp.broadcast_to(scale[4 + k : 5 + k, :], shape)
        high = full.astype(bf16).astype(f32)
        values = jnp.where(row == 4 + k, high, values)
        values = jnp.where(row == 8 + k, full - high, values)
    weights = live_weights(kb[...], count[0])
    weights = jnp.concatenate([weights, jnp.zeros((1, LANES - ch), f32)], axis=1)
    full = jnp.broadcast_to(weights, shape)
    high = full.astype(bf16).astype(f32)
    values = jnp.where(row == 12, high, values)
    values = jnp.where(row == 13, full - high, values)
    up[at + FOLD :, :] = values.astype(bf16)
    post(up, down, inner, outer)


def reorder_rows(g, natural, rows):
    d, n = g.d, g.d + 1
    places = [((d * n + j) * n, 1) for j in range(n)] + [(d * n * n + d, n), (d * n * n + d * n + d, 0)]
    places += [((i * n + j) * n, 1) for i in range(d) for j in range(d)]
    places += [((i * n + d) * n, 1) for i in range(d)]
    places += [(i * n * n + d, n) for i in range(d)]
    places += [(d * n + d, n * n)]
    for t in range(natural.shape[0]):
        groups = []
        for start, stride in places:
            group = natural[t, pl.ds(start, d, stride=max(stride, 1)), :]
            if stride == 0:
                group = jnp.where(lax.broadcasted_iota(jnp.int32, group.shape, 0) == 0, group, 0.0)
            groups.append(group)
        g.pack(rows, t * LANES, groups)
    rows[g.used :, :] = jnp.zeros((g.padded - g.used, rows.shape[1]), bf16)


def order_kernel(g, stiff, perm, pot, ordered, pot_wide, natural, rows):
    size = stiff.shape[0]
    tiles = natural.shape[0]
    for t in range(tiles):
        lanes = min(LANES, size - t * LANES)
        if lanes < LANES:
            natural[t] = jnp.zeros((g.used, LANES), f32)
        natural[t, :size, :lanes] = stiff[:, t * LANES : t * LANES + lanes].astype(f32)
    reorder_rows(g, natural, rows)
    sublane = lax.broadcasted_iota(jnp.int32, (rows.shape[1], g.padded), 0).astype(f32)
    pick_t = (perm[...] == sublane).astype(f32).astype(bf16)
    ordered[...] = dot(rows[...], pick_t).astype(bf16)
    widen(g, pot, pot_wide)


def bulk_sums(g, scale, ordered, x_top, slab, pot_wide, face_own, x_face, total, z, x_low):
    d = g.d
    for p in range(g.e):
        rows = pl.ds(p * g.plane, g.plane)
        total[rows, :] = pot_wide[rows, :] * slab[rows, :]
    for k, (a, b) in enumerate(g.columns):
        g.gather_element(slab, x_low, k * LANES, 0, a, b, True)
        g.gather_face(slab, x_face, k * LANES, 0, a, b)
    for layer, x in enumerate((x_low, x_top)):
        for a in range(2):
            lane = a * 2 * LANES
            z[...] = dot(ordered[: g.used, :], x[:, lane : lane + 2 * LANES])
            for b in range(2):
                k = layer * 4 + a * 2 + b
                factor = scale[k : k + 1, :]

                def load(n):
                    return z[n * d : (n + 1) * d, b * LANES : (b + 1) * LANES] * factor

                if layer == 0:
                    g.add_face(total, d * g.plane, a, b, load)
                g.add_layer(total, layer * d * g.plane, a, b, load)
    face_own[...] = dot(ordered[:FACE, :LANES], x_face[...])


def bulk_kernel(
    g, scale, ordered, x_top, slab, pot_wide, mass_wide, wave,
    before, low_step, low_slab, face_own, x_face, total, z, x_low,
):
    bulk_sums(g, scale, ordered, x_top, slab, pot_wide, face_own, x_face, total, z, x_low)
    for p in range(g.e):
        rows = pl.ds(p * g.plane, g.plane)
        wide = mass_wide[rows, :]
        base = wave[p].astype(f32).reshape(g.plane, LANES)
        value = (wide * total[rows, :] - spectrum_center * base) * (1.0 / spectrum_half)
        before[rows, :] = value
        if p < g.d:
            one = value.astype(bf16).astype(f32)
            low_step[rows, :] = one
            low_slab[rows, :] = (wide * one).astype(bf16).astype(f32)


def bulk_last_kernel(
    g, scale, ordered, x_top, slab, pot_wide, mass_wide, wave, step,
    before, low_new, face_own, x_face, total, z, x_low,
):
    bulk_sums(g, scale, ordered, x_top, slab, pot_wide, face_own, x_face, total, z, x_low)
    for p in range(g.e):
        rows = pl.ds(p * g.plane, g.plane)
        base = wave[p].astype(f32).reshape(g.plane, LANES)
        image = mass_wide[rows, :] * total[rows, :]
        value = (image - spectrum_center * step[rows, :]) * (2.0 / spectrum_half) - base
        before[rows, :] = value
        if p < g.d:
            low_new[rows, :] = value.astype(bf16).astype(f32)


def neighbour_terms(g, acol, count, both_t, own, held, kb, face_low, const, up, down, x_face, next_plane, x_next):
    ch = g.ch
    next_plane[...] = down[: g.plane, :].astype(f32)
    for k, (a, b) in enumerate(g.columns):
        g.gather_face(next_plane, x_next, k * LANES, 0, a, b)
    mine = own[...] + down[g.plane :, :].astype(f32)
    column = pl.ds(pl.multiple_of(acol * LANES, LANES), LANES)
    mine = mine + dot(both_t[ch:, :LANES], x_next[:, column])
    mine = (as_column(live_weights(kb[...], count)) * mine).astype(bf16)
    weights_low = as_column(const[12:13, :ch] + const[13:14, :ch])
    low = up[g.plane : g.plane + ch, :].astype(f32) + held[...]
    low = low + dot_chosen(face_low, x_face, const)
    low = (weights_low * low).astype(bf16)
    return mine, low


def dot_chosen(face, x_face, const):
    rows = face.shape[0]
    chosen = jnp.zeros((rows, LANES), f32)
    for k in range(4):
        chosen = chosen + x_face[:rows, k * LANES : (k + 1) * LANES].astype(f32) * const[k : k + 1, :]
    face_t = face.astype(f32).T.astype(bf16)
    return dot(face_t, chosen.astype(bf16))


def rim_sums(g, ucol, const, face_own, face_low, low, lifted_up, up, rim):
    d = g.d
    lifted_low = dot(face_low, low)
    rim[...] = up[: g.plane, :].astype(f32)
    for k, (a, b) in enumerate(g.columns):
        part = face_own[:, k * LANES : (k + 1) * LANES] * (const[4 + k : 5 + k, :] + const[8 + k : 9 + k, :])
        part = part + lifted_low * const[k : k + 1, :]
        g.add_face(rim, 0, a, b, lambda n: part[n * d : (n + 1) * d])
    a, b = split_element(ucol)
    for start, place in zip(g.lower_face_rows, g.face_places(0, a, b)):
        g.put_add(rim, place, lifted_up[start : start + d])


def upper_sums(g, acol, scale, ordered, both, x_next, mine, sums):
    d = g.d
    upper = dot(ordered[: g.used, :LANES], x_next[...])
    lifted = dot(both[: g.used, g.ch :], mine)

    def loader(k):
        factor = scale[4 + k : 5 + k, :]
        lane = k * LANES
        return lambda n: upper[n * d : (n + 1) * d, lane : lane + LANES] * factor

    for k, (a, b) in enumerate(g.columns):
        load = loader(k)
        near = a * d * g.e + b * d
        for i in range(d):
            for j in range(d):
                sums[pl.ds(near + i * g.plane + j * g.e, d), :] = load(g.face_groups + i * d + j)
    for k, (a, b) in enumerate(g.columns):
        g.add_layer(sums, 0, a, b, loader(k), start=d * d)
    a, b = split_element(acol)
    g.add_layer(sums, 0, a, b, lambda n: lifted[n * d : (n + 1) * d])


def held_places(g, ucol, lifted_up):
    d = g.d
    a, b = split_element(ucol)
    for n, place in enumerate(g.layer_places(0, a, b)):
        row = (g.face_groups + n) * d
        if row not in g.lower_face_rows[:-1]:
            start, stride = place
            rows = pl.ds(start, d, stride=stride) if stride > 1 else pl.ds(start, d)
            yield rows, None if lifted_up is None else lifted_up[row : row + d]


def middle_kernel(
    g, acol, ucol, count, scale, mass_wide, before, low_step, low_slab, face_own, x_face, ordered, both, both_t,
    own, held, kb, inner, outer,
    slab, x_top, step, own_out, held_out, inner_out, outer_out, kept,
    sums, next_plane, x_next, face_sums, up, down, up_out, down_out, rim, x_held,
):
    at = g.plane + g.ch
    d = g.d
    half = d * g.plane
    collect(inner, outer, up, down)
    for k in range(FACE // FOLD):
        kept[k * FOLD : (k + 1) * FOLD, : g.ch] = up[at : at + FOLD, k * g.ch : (k + 1) * g.ch]
    kept[FACE:, :] = up[at + FOLD :, :]
    face_low = kept[:FACE, : g.ch]
    const = kept[FACE:, :].astype(f32)
    mine, low = neighbour_terms(
        g, acol[0], count[0], both_t, own, held, kb, face_low, const, up, down, x_face, next_plane, x_next
    )
    lifted_up = dot(both[: g.used, : g.ch], low)
    upper_sums(g, acol[0], scale, ordered, both, x_next, mine, sums)
    a, b = split_element(ucol[0])
    g.add_face(sums, 0, a, b, lambda n: lifted_up[n * d : (n + 1) * d])
    rim_sums(g, ucol[0], const, face_own, face_low, low, lifted_up, up, rim)
    step[:half, :] = low_step[...]
    slab[:half, :] = low_slab[...]

    def finish(rows, added):
        wide = mass_wide[rows, :]
        one = (before[rows, :] + wide * (added * (1.0 / spectrum_half))).astype(bf16).astype(f32)
        step[rows, :] = one
        slab[rows, :] = (wide * one).astype(bf16).astype(f32)

    for rows, added in held_places(g, ucol[0], lifted_up):
        finish(rows, added)
    finish(pl.ds(0, g.plane), rim[...])
    for p in range(d):
        finish(pl.ds(half + p * g.plane, g.plane), sums[p * g.plane : (p + 1) * g.plane, :])
    gather_out(g, slab, x_top, x_held, ucol[0])
    outgoing(
        g, acol[0], scale, slab, x_top, x_held, ordered[:FACE, :], both_t, face_sums, up_out, down_out,
        own_out, held_out,
    )
    post(up_out, down_out, inner_out, outer_out)


def last_low_kernel(
    g, acol, ucol, count, scale, mass_wide, before, face_own, x_face, ordered, both, both_t,
    own, held, kb, kept, inner, outer,
    held_out, new, mine_out, x_next,
    sums, next_plane, x_held, x_rim, up, down, rim,
):
    d, ch = g.d, g.ch
    half = d * g.plane
    collect(inner, outer, up, down)
    face_low = kept[:FACE, :ch]
    const = kept[FACE:, :].astype(f32)
    mine, low = neighbour_terms(
        g, acol[0], count[0], both_t, own, held, kb, face_low, const, up, down, x_face, next_plane, x_next
    )
    mine_out[...] = mine
    lifted_up = dot(both[: g.used, :ch], low)
    starts = g.lower_face_rows
    pieces = [slice(starts[0] - d, starts[0] + (d + 1) * d)] + [slice(s - d, s + d) for s in starts[d:]]
    offsets = [d + n * d for n in range(d)] + [(d + 2) * d + n * 2 * d + d for n in range(3)]
    upper = dot(jnp.concatenate([ordered[p, :LANES] for p in pieces], axis=0), x_next[...])
    lifted = dot(jnp.concatenate([both[p, ch:] for p in pieces], axis=0), mine)
    sums[...] = jnp.zeros_like(sums)
    for k, (a, b) in enumerate(g.columns):
        here = jnp.where(acol[0] == k, 1.0, 0.0)
        factor = scale[4 + k : 5 + k, :]
        part = upper[:, k * LANES : (k + 1) * LANES] * factor + lifted * here
        g.add_face(sums, 0, a, b, lambda n: part[offsets[n] : offsets[n] + d])
    a, b = split_element(ucol[0])
    g.add_face(sums, 0, a, b, lambda n: lifted_up[n * d : (n + 1) * d])
    rim_sums(g, ucol[0], const, face_own, face_low, low, lifted_up, up, rim)

    def finish(rows, added):
        value = before[rows, :] + mass_wide[rows, :] * (added * (2.0 / spectrum_half))
        new[rows, :] = value.astype(bf16).astype(f32)

    for rows, added in held_places(g, ucol[0], lifted_up):
        finish(rows, added)
    finish(pl.ds(0, g.plane), rim[...])
    finish(pl.ds(half, g.plane), sums[...])
    g.gather_element(new, x_held, 0, 0, a, b, True)
    for k, (a, b) in enumerate(g.columns):
        g.gather_face(new, x_rim, k * LANES, 0, a, b)
    held_out[...] = dot(both_t[:ch, :], x_held[...]) + dot_chosen(face_low, x_rim, const)


def last_high_kernel(
    g, acol, ucol, count, scale, mass_wide, before, low_new, ordered, both, both_t, new, mine, x_next,
    filtered, own_out, sums, field, x_own, done, sems,
):
    d = g.d
    half = d * g.plane
    copies = [
        pltpu.make_async_copy(done.at[pl.ds(p, n)], filtered.at[pl.ds(p, n)], sems.at[k])
        for k, (p, n) in enumerate(((0, d), (d, d // 2), (d + d // 2, d // 2)))
    ]

    def give(planes):
        for p in planes:
            done[p] = field[p * g.plane : (p + 1) * g.plane, :].astype(bf16).reshape(g.e, g.e, LANES)

    field[:half, :] = low_new[...]
    for rows, _ in held_places(g, ucol[0], None):
        field[rows, :] = new[rows, :]
    field[: g.plane, :] = new[: g.plane, :]
    give(range(d))
    copies[0].start()
    field[half : half + g.plane, :] = new[half : half + g.plane, :]
    upper_sums(g, acol[0], scale, ordered, both, x_next, mine[...], sums)
    for p in range(d):
        if p:
            rows = pl.ds(half + p * g.plane, g.plane)
            added = sums[p * g.plane : (p + 1) * g.plane, :]
            value = before[rows, :] + mass_wide[rows, :] * (added * (2.0 / spectrum_half))
            field[rows, :] = value.astype(bf16).astype(f32)
        give([d + p])
        if (p + 1) % (d // 2) == 0:
            copies[1 + p // (d // 2)].start()
    a, b = split_element(acol[0])
    g.gather_element(field, x_own, 0, half, a, b, False)
    own_out[...] = dot(both_t[g.ch :, :], x_own[...])
    for copy in copies:
        copy.wait()


def call(kernel, scalars, operands, outs, scratch, flops, limit=24 << 20, hbm=False, far_outs=0):
    smem = pl.BlockSpec(memory_space=pltpu.SMEM)
    vmem = pl.BlockSpec(memory_space=pltpu.VMEM)
    far = pl.BlockSpec(memory_space=pltpu.MemorySpace.HBM)
    moved = sum(v.size * v.dtype.itemsize for v in operands)
    if hbm:
        operands = [pltpu.with_memory_space_constraint(v, pltpu.MemorySpace.HBM) for v in operands]
    return pl.pallas_call(
        kernel,
        out_shape=[jax.ShapeDtypeStruct(s, t) for s, t in outs],
        in_specs=[smem] * len(scalars) + [far if hbm else vmem] * len(operands),
        out_specs=[far] * far_outs + [vmem] * (len(outs) - far_outs),
        scratch_shapes=[pltpu.VMEM(*s) if isinstance(s, tuple) else s for s in scratch],
        compiler_params=pltpu.CompilerParams(vmem_limit_bytes=limit),
        cost_estimate=pl.CostEstimate(flops=flops, bytes_accessed=moved, transcendentals=0),
    )(*scalars, *operands)


def per_device(
    wave_in, mass_scale, potential, elem_scale, stiffness, proj_lower, proj_upper, kb_coef,
    atom_column, chan_count, upper_column,
):
    extent = wave_in.shape[0]
    degree = extent // 2
    ch = kb_coef.shape[-1]
    order, used = row_order(degree)
    padded = order.shape[0]
    perm = jnp.asarray(order, f32)[None, :]
    g = Mesh1(degree, ch, used, padded)
    plane, nodes = g.plane, g.nodes
    scalars = (atom_column, upper_column, chan_count)
    part = ((ch, LANES), f32)
    slab_s, half_s, plane_s = ((nodes, LANES), f32), ((nodes // 2, LANES), f32), ((plane, LANES), f32)
    x_s, x_one_s = ((padded, 4 * LANES), bf16), ((padded, LANES), bf16)
    wire_s = ((plane + ch, LANES), bf16)
    wire_first_s = ((plane + ch + FOLD + CONST_ROWS, LANES), bf16)
    face_s = ((LANES, 4 * LANES), bf16)
    face_sum_s = ((FACE, 4 * LANES), f32)

    slab, x_top, mass_wide, wave, stiff, scale, order_row, pot, kb, both, both_t, own, held, inner, outer = call(
        functools.partial(start_kernel, g), scalars,
        (wave_in, mass_scale, elem_scale, stiffness, jnp.swapaxes(proj_lower, 1, 2), jnp.swapaxes(proj_upper, 1, 2),
         kb_coef, perm, potential),
        [slab_s, x_s, slab_s, (wave_in.shape, bf16), (stiffness.shape, bf16), ((8, LANES), f32), (perm.shape, f32),
         (potential.shape, f32), (kb_coef.shape, f32), ((padded, 2 * ch), bf16), ((2 * ch, padded), bf16), part, part,
         wire_first_s, wire_first_s],
        [plane_s, wire_first_s, wire_s, (mass_scale.shape, f32), (elem_scale.shape, f32),
         ((2 * ch, stiffness.shape[0]), bf16), x_one_s, ((2, used, LANES), f32), ((padded, 2 * LANES), bf16),
         pltpu.SemaphoreType.DMA((12,))], 10**8, hbm=True,
    )
    inner, outer = swapped(inner, outer, "space")
    ordered, pot_wide = call(
        functools.partial(order_kernel, g), (), (stiff, order_row, pot),
        [((padded, padded), bf16), slab_s],
        [((-(-stiffness.shape[0] // LANES), used, LANES), f32), ((padded, padded), bf16)], 2 * 10**9,
    )
    bulk_scratch = [slab_s, ((used, 2 * LANES), f32), x_s]
    before, low_step, low_slab, face_own, x_face = call(
        functools.partial(bulk_kernel, g), (), (scale, ordered, x_top, slab, pot_wide, mass_wide, wave),
        [slab_s, half_s, half_s, face_sum_s, face_s], bulk_scratch, 2 * 10**9,
    )
    shared = (ordered, both, both_t)
    slab, x_top, step, own, held, inner, outer, kept = call(
        functools.partial(middle_kernel, g), scalars,
        (scale, mass_wide, before, low_step, low_slab, face_own, x_face, *shared, own, held, kb, inner, outer),
        [slab_s, x_s, slab_s, part, part, wire_s, wire_s, ((FACE + CONST_ROWS, LANES), bf16)],
        [half_s, plane_s, face_s, plane_s, wire_first_s, wire_s, wire_s, wire_s, plane_s, x_one_s], 10**8,
    )
    inner, outer = swapped(inner, outer, "space")
    before, low_new, face_own, x_face = call(
        functools.partial(bulk_last_kernel, g), (),
        (scale, ordered, x_top, slab, pot_wide, mass_wide, wave, step),
        [slab_s, half_s, face_sum_s, face_s], bulk_scratch, 2 * 10**9,
    )
    held, new, mine, x_next = call(
        functools.partial(last_low_kernel, g), scalars,
        (scale, mass_wide, before, face_own, x_face, *shared, own, held, kb, kept, inner, outer),
        [part, ((nodes // 2 + plane, LANES), f32), ((ch, LANES), bf16), face_s],
        [plane_s, plane_s, x_one_s, face_s, wire_s, wire_s, plane_s], 10**8,
    )
    held = shifted(held, "space", -1)
    filtered, own = call(
        functools.partial(last_high_kernel, g), scalars,
        (scale, mass_wide, before, low_new, *shared, new, mine, x_next),
        [(wave_in.shape, bf16), part],
        [half_s, slab_s, x_one_s, (wave_in.shape, bf16), pltpu.SemaphoreType.DMA((3,))], 10**9, far_outs=1,
    )
    return filtered, (own + held)[None]


def solution(mesh):
    in_specs = (
        P("space", None, None, "band"),
        P("space", None),
        P("space", None),
        P("space", None, None),
        P(),
        P("space", None, None),
        P("space", None, None),
        P("space", None),
        P("space"),
        P("space"),
        P("space"),
    )
    out_specs = (P("space", None, None, "band"), P("space", None, "band"))
    return jax.shard_map(
        per_device, mesh=mesh, in_specs=in_specs, out_specs=out_specs, check_vma=False
    )
```

```python
import functools

import jax
import jax.numpy as jnp
import numpy as np
from jax import lax
from jax.experimental import pallas as pl
from jax.experimental.pallas import tpu as pltpu
from jax.sharding import PartitionSpec as P


spectrum_center = 1.0
spectrum_half = 6.0
f32 = jnp.float32
bf16 = jnp.bfloat16
LANES = 128
FACE = 96
FOLD = 32
CONST_ROWS = 16


def shifted(value, axis, steps):
    count = lax.axis_size(axis)
    pairs = [(source, (source + steps) % count) for source in range(count)]
    return lax.ppermute(value, axis, pairs)


def swapped(inner, outer, axis):
    count = lax.axis_size(axis)
    within = [(source, source ^ 1) for source in range(count)]
    across = [(source, (source + (1 if source % 2 else -1)) % count) for source in range(count)]
    outer = lax.ppermute(outer, axis, across)
    inner = lax.ppermute(inner, axis, within)
    return inner, outer


def is_odd():
    return lax.rem(lax.axis_index("space"), 2) == 1


def post(up, down, inner, outer):
    @pl.when(is_odd())
    def _():
        inner[: down.shape[0], :] = down[...]
        outer[: up.shape[0], :] = up[...]

    @pl.when(jnp.logical_not(is_odd()))
    def _():
        inner[: up.shape[0], :] = up[...]
        outer[: down.shape[0], :] = down[...]


def collect(inner, outer, up, down):
    @pl.when(is_odd())
    def _():
        up[...] = inner[: up.shape[0], :]
        down[...] = outer[: down.shape[0], :]

    @pl.when(jnp.logical_not(is_odd()))
    def _():
        up[...] = outer[: up.shape[0], :]
        down[...] = inner[: down.shape[0], :]


def row_order(degree):
    points = degree + 1

    def natural(i, j, l):
        return (i * points + j) * points + l

    inner = range(degree)
    order = [natural(degree, j, l) for j in inner for l in inner]
    order += [natural(degree, degree, l) for l in inner]
    order += [natural(degree, j, degree) for j in inner]
    order += [natural(degree, degree, degree)] + [-1] * (degree - 1)
    order += [natural(i, j, l) for i in inner for j in inner for l in inner]
    order += [natural(i, degree, l) for i in inner for l in inner]
    order += [natural(i, j, degree) for i in inner for j in inner]
    order += [natural(i, degree, degree) for i in inner]
    used = len(order)
    order += [-1] * (-used % 256)
    return np.asarray(order, np.int32), used


def dot(a, b):
    return jnp.dot(a, b, preferred_element_type=f32)


def dot_nt(a, b):
    return lax.dot_general(a, b, (((1,), (1,)), ((), ())), preferred_element_type=f32)


def onehot_rows(perm, count):
    rows = perm.shape[1]
    column = jnp.broadcast_to(perm, (8, rows)).T[:, :1]
    lane = lax.broadcasted_iota(jnp.int32, (rows, count), 1).astype(f32)
    return (column == lane).astype(bf16)


class Mesh1:
    def __init__(self, degree, channels, used, padded):
        self.d = degree
        self.e = 2 * degree
        self.plane = self.e * self.e
        self.nodes = self.e * self.plane
        self.ch = channels
        self.face_groups = degree + 3
        self.used = used
        self.padded = padded
        self.columns = [(a, b) for a in range(2) for b in range(2)]
        self.face_rows = degree * (degree + 1) ** 2
        rest = self.face_groups * degree
        lines = rest + degree**3
        self.lower_face_rows = [rest + j * degree for j in range(degree)]
        self.lower_face_rows += [lines, lines + degree**2, lines + 2 * degree**2]

    def far(self, index):
        return (1 - index) * self.d

    def aligned(self, value):
        return value if isinstance(value, int) else pl.multiple_of(value, self.d)

    def face_places(self, base, a, b):
        d, e = self.d, self.e
        near = base + a * d * e + b * d
        places = [(self.aligned(near + j * e), 1) for j in range(d)]
        places.append((self.aligned(base + self.far(a) * e + b * d), 1))
        places.append((base + a * d * e + self.far(b), e))
        places.append((self.aligned(base + self.far(a) * e + self.far(b)), 0))
        return places

    def layer_places(self, base, a, b):
        d, e, plane = self.d, self.e, self.plane
        near = base + a * d * e + b * d
        places = [(self.aligned(near + i * plane + j * e), 1) for i in range(d) for j in range(d)]
        places += [
            (self.aligned(base + i * plane + self.far(a) * e + b * d), 1) for i in range(d)
        ]
        places += [(base + i * plane + a * d * e + self.far(b), e) for i in range(d)]
        places.append((base + self.far(a) * e + self.far(b), plane))
        return places

    def take(self, ref, place):
        start, stride = place
        if stride > 1:
            return ref[pl.ds(start, self.d, stride=stride), :]
        value = ref[pl.ds(start, self.d), :]
        if stride == 0:
            first = lax.broadcasted_iota(jnp.int32, value.shape, 0) == 0
            value = jnp.where(first, value, 0.0)
        return value

    def put_add(self, ref, place, value):
        start, stride = place
        if stride > 1:
            rows = pl.ds(start, self.d, stride=stride)
        else:
            rows = pl.ds(start, self.d)
            if stride == 0:
                first = lax.broadcasted_iota(jnp.int32, value.shape, 0) == 0
                value = jnp.where(first, value, 0.0)
        ref[rows, :] = ref[rows, :] + value

    def pack(self, ref, lane, groups, first_row=0):
        lanes = pl.ds(lane, LANES)
        for at in range(0, len(groups), 2):
            pair = jnp.concatenate([groups[at], groups[at + 1]], axis=0).astype(bf16)
            ref[pl.ds(first_row + at * self.d, 2 * self.d), lanes] = pair

    def gather_element(self, slab, ref, lane, base, a, b, with_face):
        d = self.d
        zero = jnp.zeros((d, LANES), f32)
        if with_face:
            groups = [self.take(slab, p) for p in self.face_places(base + d * self.plane, a, b)]
        else:
            groups = [zero] * self.face_groups
        groups += [self.take(slab, p) for p in self.layer_places(base, a, b)]
        groups += [zero] * ((self.padded - self.used) // d)
        self.pack(ref, lane, groups)

    def gather_face(self, slab, ref, lane, base, a, b):
        zero = jnp.zeros((self.d, LANES), f32)
        groups = [self.take(slab, p) for p in self.face_places(base, a, b)]
        groups += [zero] * (LANES // self.d - len(groups))
        self.pack(ref, lane, groups)

    def add_face(self, ref, base, a, b, load):
        for g, place in enumerate(self.face_places(base, a, b)):
            self.put_add(ref, place, load(g))

    def add_layer(self, ref, base, a, b, load, start=0):
        for g, place in enumerate(self.layer_places(base, a, b)):
            if g >= start:
                self.put_add(ref, place, load(self.face_groups + g))


def live_weights(kb, count):
    lane = lax.broadcasted_iota(jnp.int32, kb.shape, 1)
    return kb * jnp.where(lane < count, 1.0, 0.0)


def as_column(row):
    size = row.shape[1]
    shape = (size, size)
    eye = lax.broadcasted_iota(jnp.int32, shape, 0) == lax.broadcasted_iota(jnp.int32, shape, 1)
    return jnp.sum(jnp.where(eye, jnp.broadcast_to(row, shape), 0.0), axis=1, keepdims=True)


def split_element(column):
    return column // 2, column % 2


def outgoing(g, acol, scale, slab, x_top, x_held, kface, both_t, face_sums, up, down, own_out, held_out):
    d, ch = g.d, g.ch
    own = dot(both_t[ch:, :], x_top[:, pl.ds(pl.multiple_of(acol * LANES, LANES), LANES)])
    held = dot(both_t[:ch, :], x_held[...])
    own_out[...] = own
    held_out[...] = held
    sums = dot(kface, x_top[...])
    face_sums[...] = jnp.zeros_like(face_sums)
    for k, (a, b) in enumerate(g.columns):
        part = sums[:, k * LANES : (k + 1) * LANES] * scale[4 + k : 5 + k, :]
        g.add_face(face_sums, 0, a, b, lambda n: part[n * d : (n + 1) * d])
    up[: g.plane, :] = face_sums[...].astype(bf16)
    up[g.plane : g.plane + ch, :] = own.astype(bf16)
    down[: g.plane, :] = slab[: g.plane, :].astype(bf16)
    down[g.plane :, :] = held.astype(bf16)


def gather_out(g, slab, x_top, x_held, ucol):
    for k, (a, b) in enumerate(g.columns):
        g.gather_element(slab, x_top, k * LANES, g.d * g.plane, a, b, False)
    a, b = split_element(ucol)
    g.gather_element(slab, x_held, 0, 0, a, b, True)


def widen(g, source, target):
    value = source[...]
    high = value.astype(bf16).astype(f32)
    middle = (value - high).astype(bf16).astype(f32)
    parts = jnp.concatenate([high, middle, value - high - middle], axis=0).T.astype(bf16)
    shape = (3 * g.e, 2 * LANES)
    row = lax.rem(lax.broadcasted_iota(jnp.int32, shape, 0), g.e)
    second = (lax.broadcasted_iota(jnp.int32, shape, 1) >= LANES).astype(jnp.int32)
    for p in range(0, g.e, 2):
        wide = dot(parts, (row == p + second).astype(f32).astype(bf16))
        target[p * g.plane : (p + 1) * g.plane, :] = wide[:, :LANES]
        target[(p + 1) * g.plane : (p + 2) * g.plane, :] = wide[:, LANES:]


def start_kernel(
    g, acol, ucol, count, wave_hbm, mass_hbm, scale_hbm, stiff_hbm, low_hbm, up_hbm, kb_hbm, perm_hbm, pot_hbm,
    slab, x_top, mass_wide, wave, stiff, scale, perm, pot, kb, both, both_t, own_out, held_out, inner, outer,
    face_sums, up, down, mass, scale_in, proj, x_held, natural, pair, sems,
):
    ch = g.ch
    quarter = g.e // 4
    copies = [
        pltpu.make_async_copy(source, target, sems.at[k])
        for k, (source, target) in enumerate((
            (mass_hbm, mass),
            *((wave_hbm.at[pl.ds(p, quarter)], wave.at[pl.ds(p, quarter)]) for p in range(0, g.e, quarter)),
            (up_hbm.at[0], proj.at[:ch]), (low_hbm.at[0], proj.at[ch:]), (perm_hbm, perm), (stiff_hbm, stiff),
            (scale_hbm, scale_in), (kb_hbm, kb), (pot_hbm, pot),
        ))
    ]
    for copy in copies:
        copy.start()
    copies[0].wait()
    widen(g, mass, mass_wide)
    for p in range(g.e):
        if p % quarter == 0:
            copies[1 + p // quarter].wait()
        rows = pl.ds(p * g.plane, g.plane)
        start = wave[p].astype(f32).reshape(g.plane, LANES)
        slab[rows, :] = (mass_wide[rows, :] * start).astype(bf16).astype(f32)
    gather_out(g, slab, x_top, x_held, ucol[0])
    for copy in copies[5:]:
        copy.wait()
    for k in range(8):
        one = scale_in[k // 4, k % 4 // 2 : k % 4 // 2 + 1, k % 2 : k % 2 + 1]
        scale[k : k + 1, :] = jnp.broadcast_to(one, (1, LANES))
    size = stiff.shape[0]
    first = g.face_rows // LANES * LANES
    natural[1] = jnp.zeros((g.used, LANES), f32)
    natural[0, :size, : 2 * ch] = proj[...].astype(f32).T
    natural[1, :size, : size - first] = stiff[:, first:].astype(f32)
    reorder_rows(g, natural, pair)
    turned = pair[:, : 2 * ch]
    both[...] = turned
    both_t[...] = pair[:, :LANES].astype(f32).T[: 2 * ch].astype(bf16)
    kface = dot_nt(onehot_rows(perm[:, :LANES] - first, LANES)[:FACE], pair[:, LANES:]).astype(bf16)
    outgoing(g, acol[0], scale, slab, x_top, x_held, kface, both_t, face_sums, up, down, own_out, held_out)
    at = g.plane + ch
    folded = [turned[k : k + FOLD, ch:] for k in range(0, FACE, FOLD)]
    rest = LANES - len(folded) * ch
    if rest:
        folded.append(jnp.zeros((FOLD, rest), bf16))
    up[at : at + FOLD, :] = jnp.concatenate(folded, axis=1)
    shape = (CONST_ROWS, LANES)
    row = lax.broadcasted_iota(jnp.int32, shape, 0)
    values = jnp.zeros(shape, f32)
    for k in range(4):
        chosen = jnp.where(acol[0] == k, 1.0, 0.0)
        values = jnp.where(row == k, chosen, values)
        full = jnp.broadcast_to(scale[4 + k : 5 + k, :], shape)
        high = full.astype(bf16).astype(f32)
        values = jnp.where(row == 4 + k, high, values)
        values = jnp.where(row == 8 + k, full - high, values)
    weights = live_weights(kb[...], count[0])
    weights = jnp.concatenate([weights, jnp.zeros((1, LANES - ch), f32)], axis=1)
    full = jnp.broadcast_to(weights, shape)
    high = full.astype(bf16).astype(f32)
    values = jnp.where(row == 12, high, values)
    values = jnp.where(row == 13, full - high, values)
    up[at + FOLD :, :] = values.astype(bf16)
    post(up, down, inner, outer)


def reorder_rows(g, natural, rows):
    d, n = g.d, g.d + 1
    places = [((d * n + j) * n, 1) for j in range(n)] + [(d * n * n + d, n), (d * n * n + d * n + d, 0)]
    places += [((i * n + j) * n, 1) for i in range(d) for j in range(d)]
    places += [((i * n + d) * n, 1) for i in range(d)]
    places += [(i * n * n + d, n) for i in range(d)]
    places += [(d * n + d, n * n)]
    for t in range(natural.shape[0]):
        groups = []
        for start, stride in places:
            group = natural[t, pl.ds(start, d, stride=max(stride, 1)), :]
            if stride == 0:
                group = jnp.where(lax.broadcasted_iota(jnp.int32, group.shape, 0) == 0, group, 0.0)
            groups.append(group)
        g.pack(rows, t * LANES, groups)
    rows[g.used :, :] = jnp.zeros((g.padded - g.used, rows.shape[1]), bf16)


def order_kernel(g, stiff, perm, pot, ordered, pot_wide, natural, rows):
    size = stiff.shape[0]
    tiles = natural.shape[0]
    for t in range(tiles):
        lanes = min(LANES, size - t * LANES)
        if lanes < LANES:
            natural[t] = jnp.zeros((g.used, LANES), f32)
        natural[t, :size, :lanes] = stiff[:, t * LANES : t * LANES + lanes].astype(f32)
    reorder_rows(g, natural, rows)
    sublane = lax.broadcasted_iota(jnp.int32, (rows.shape[1], g.padded), 0).astype(f32)
    pick_t = (perm[...] == sublane).astype(f32).astype(bf16)
    ordered[...] = dot(rows[...], pick_t).astype(bf16)
    widen(g, pot, pot_wide)


def bulk_sums(g, scale, ordered, x_top, slab, pot_wide, face_own, x_face, total, z, x_low):
    d = g.d
    for p in range(g.e):
        rows = pl.ds(p * g.plane, g.plane)
        total[rows, :] = pot_wide[rows, :] * slab[rows, :]
    for k, (a, b) in enumerate(g.columns):
        g.gather_element(slab, x_low, k * LANES, 0, a, b, True)
        g.gather_face(slab, x_face, k * LANES, 0, a, b)
    for layer, x in enumerate((x_low, x_top)):
        for a in range(2):
            lane = a * 2 * LANES
            z[...] = dot(ordered[: g.used, :], x[:, lane : lane + 2 * LANES])
            for b in range(2):
                k = layer * 4 + a * 2 + b
                factor = scale[k : k + 1, :]

                def load(n):
                    return z[n * d : (n + 1) * d, b * LANES : (b + 1) * LANES] * factor

                if layer == 0:
                    g.add_face(total, d * g.plane, a, b, load)
                g.add_layer(total, layer * d * g.plane, a, b, load)
    face_own[...] = dot(ordered[:FACE, :LANES], x_face[...])


def bulk_kernel(
    g, scale, ordered, x_top, slab, pot_wide, mass_wide, wave,
    before, low_step, low_slab, face_own, x_face, total, z, x_low,
):
    bulk_sums(g, scale, ordered, x_top, slab, pot_wide, face_own, x_face, total, z, x_low)
    for p in range(g.e):
        rows = pl.ds(p * g.plane, g.plane)
        wide = mass_wide[rows, :]
        base = wave[p].astype(f32).reshape(g.plane, LANES)
        value = (wide * total[rows, :] - spectrum_center * base) * (1.0 / spectrum_half)
        before[rows, :] = value
        if p < g.d:
            one = value.astype(bf16).astype(f32)
            low_step[rows, :] = one
            low_slab[rows, :] = (wide * one).astype(bf16).astype(f32)


def bulk_last_kernel(
    g, scale, ordered, x_top, slab, pot_wide, mass_wide, wave, step,
    before, low_new, face_own, x_face, total, z, x_low,
):
    bulk_sums(g, scale, ordered, x_top, slab, pot_wide, face_own, x_face, total, z, x_low)
    for p in range(g.e):
        rows = pl.ds(p * g.plane, g.plane)
        base = wave[p].astype(f32).reshape(g.plane, LANES)
        image = mass_wide[rows, :] * total[rows, :]
        value = (image - spectrum_center * step[rows, :]) * (2.0 / spectrum_half) - base
        before[rows, :] = value
        if p < g.d:
            low_new[rows, :] = value.astype(bf16).astype(f32)


def neighbour_terms(g, acol, count, both_t, own, held, kb, face_low, const, up, down, x_face, next_plane, x_next):
    ch = g.ch
    next_plane[...] = down[: g.plane, :].astype(f32)
    for k, (a, b) in enumerate(g.columns):
        g.gather_face(next_plane, x_next, k * LANES, 0, a, b)
    mine = own[...] + down[g.plane :, :].astype(f32)
    column = pl.ds(pl.multiple_of(acol * LANES, LANES), LANES)
    mine = mine + dot(both_t[ch:, :LANES], x_next[:, column])
    mine = (as_column(live_weights(kb[...], count)) * mine).astype(bf16)
    weights_low = as_column(const[12:13, :ch] + const[13:14, :ch])
    low = up[g.plane : g.plane + ch, :].astype(f32) + held[...]
    low = low + dot_chosen(face_low, x_face, const)
    low = (weights_low * low).astype(bf16)
    return mine, low


def dot_chosen(face, x_face, const):
    rows = face.shape[0]
    chosen = jnp.zeros((rows, LANES), f32)
    for k in range(4):
        chosen = chosen + x_face[:rows, k * LANES : (k + 1) * LANES].astype(f32) * const[k : k + 1, :]
    face_t = face.astype(f32).T.astype(bf16)
    return dot(face_t, chosen.astype(bf16))


def rim_sums(g, ucol, const, face_own, face_low, low, lifted_up, up, rim):
    d = g.d
    lifted_low = dot(face_low, low)
    rim[...] = up[: g.plane, :].astype(f32)
    for k, (a, b) in enumerate(g.columns):
        part = face_own[:, k * LANES : (k + 1) * LANES] * (const[4 + k : 5 + k, :] + const[8 + k : 9 + k, :])
        part = part + lifted_low * const[k : k + 1, :]
        g.add_face(rim, 0, a, b, lambda n: part[n * d : (n + 1) * d])
    a, b = split_element(ucol)
    for start, place in zip(g.lower_face_rows, g.face_places(0, a, b)):
        g.put_add(rim, place, lifted_up[start : start + d])


def upper_sums(g, acol, scale, ordered, both, x_next, mine, sums):
    d = g.d
    skip = g.face_groups * d // 16 * 16
    upper = dot(ordered[skip : g.used, :LANES], x_next[...])
    lifted = dot(both[skip : g.used, g.ch :], mine)

    def loader(k):
        factor = scale[4 + k : 5 + k, :]
        lane = k * LANES
        return lambda n: upper[n * d - skip : (n + 1) * d - skip, lane : lane + LANES] * factor

    for k, (a, b) in enumerate(g.columns):
        load = loader(k)
        near = a * d * g.e + b * d
        for i in range(d):
            for j in range(d):
                sums[pl.ds(near + i * g.plane + j * g.e, d), :] = load(g.face_groups + i * d + j)
    for k, (a, b) in enumerate(g.columns):
        g.add_layer(sums, 0, a, b, loader(k), start=d * d)
    a, b = split_element(acol)
    g.add_layer(sums, 0, a, b, lambda n: lifted[n * d - skip : (n + 1) * d - skip])


def held_places(g, ucol, lifted_up):
    d = g.d
    a, b = split_element(ucol)
    for n, place in enumerate(g.layer_places(0, a, b)):
        row = (g.face_groups + n) * d
        if row not in g.lower_face_rows[:-1]:
            start, stride = place
            rows = pl.ds(start, d, stride=stride) if stride > 1 else pl.ds(start, d)
            yield rows, None if lifted_up is None else lifted_up[row : row + d]


def middle_kernel(
    g, acol, ucol, count, scale, mass_wide, before, low_step, low_slab, face_own, x_face, ordered, both, both_t,
    own, held, kb, inner, outer,
    slab, x_top, step, own_out, held_out, inner_out, outer_out, kept,
    sums, next_plane, x_next, face_sums, up, down, up_out, down_out, rim, x_held,
):
    at = g.plane + g.ch
    d = g.d
    half = d * g.plane
    collect(inner, outer, up, down)
    for k in range(FACE // FOLD):
        kept[k * FOLD : (k + 1) * FOLD, : g.ch] = up[at : at + FOLD, k * g.ch : (k + 1) * g.ch]
    kept[FACE:, :] = up[at + FOLD :, :]
    face_low = kept[:FACE, : g.ch]
    const = kept[FACE:, :].astype(f32)
    mine, low = neighbour_terms(
        g, acol[0], count[0], both_t, own, held, kb, face_low, const, up, down, x_face, next_plane, x_next
    )
    lifted_up = dot(both[: g.used, : g.ch], low)
    upper_sums(g, acol[0], scale, ordered, both, x_next, mine, sums)
    a, b = split_element(ucol[0])
    g.add_face(sums, 0, a, b, lambda n: lifted_up[n * d : (n + 1) * d])
    rim_sums(g, ucol[0], const, face_own, face_low, low, lifted_up, up, rim)
    step[:half, :] = low_step[...]
    slab[:half, :] = low_slab[...]

    def finish(rows, added):
        wide = mass_wide[rows, :]
        one = (before[rows, :] + wide * (added * (1.0 / spectrum_half))).astype(bf16).astype(f32)
        step[rows, :] = one
        slab[rows, :] = (wide * one).astype(bf16).astype(f32)

    for rows, added in held_places(g, ucol[0], lifted_up):
        finish(rows, added)
    finish(pl.ds(0, g.plane), rim[...])
    for p in range(d):
        finish(pl.ds(half + p * g.plane, g.plane), sums[p * g.plane : (p + 1) * g.plane, :])
    gather_out(g, slab, x_top, x_held, ucol[0])
    outgoing(
        g, acol[0], scale, slab, x_top, x_held, ordered[:FACE, :], both_t, face_sums, up_out, down_out,
        own_out, held_out,
    )
    post(up_out, down_out, inner_out, outer_out)


def last_low_kernel(
    g, acol, ucol, count, scale, mass_wide, before, face_own, x_face, ordered, both, both_t,
    own, held, kb, kept, inner, outer,
    held_out, new, mine_out, x_next,
    sums, next_plane, x_held, x_rim, up, down, rim,
):
    d, ch = g.d, g.ch
    half = d * g.plane
    collect(inner, outer, up, down)
    face_low = kept[:FACE, :ch]
    const = kept[FACE:, :].astype(f32)
    mine, low = neighbour_terms(
        g, acol[0], count[0], both_t, own, held, kb, face_low, const, up, down, x_face, next_plane, x_next
    )
    mine_out[...] = mine
    lifted_up = dot(both[: g.used, :ch], low)
    starts = g.lower_face_rows
    pieces = [slice(starts[0] - d, starts[0] + (d + 1) * d)] + [slice(s - d, s + d) for s in starts[d:]]
    offsets = [d + n * d for n in range(d)] + [(d + 2) * d + n * 2 * d + d for n in range(3)]
    upper = dot(jnp.concatenate([ordered[p, :LANES] for p in pieces], axis=0), x_next[...])
    lifted = dot(jnp.concatenate([both[p, ch:] for p in pieces], axis=0), mine)
    sums[...] = jnp.zeros_like(sums)
    for k, (a, b) in enumerate(g.columns):
        here = jnp.where(acol[0] == k, 1.0, 0.0)
        factor = scale[4 + k : 5 + k, :]
        part = upper[:, k * LANES : (k + 1) * LANES] * factor + lifted * here
        g.add_face(sums, 0, a, b, lambda n: part[offsets[n] : offsets[n] + d])
    a, b = split_element(ucol[0])
    g.add_face(sums, 0, a, b, lambda n: lifted_up[n * d : (n + 1) * d])
    rim_sums(g, ucol[0], const, face_own, face_low, low, lifted_up, up, rim)

    def finish(rows, added):
        value = before[rows, :] + mass_wide[rows, :] * (added * (2.0 / spectrum_half))
        new[rows, :] = value.astype(bf16).astype(f32)

    for rows, added in held_places(g, ucol[0], lifted_up):
        finish(rows, added)
    finish(pl.ds(0, g.plane), rim[...])
    finish(pl.ds(half, g.plane), sums[...])
    g.gather_element(new, x_held, 0, 0, a, b, True)
    for k, (a, b) in enumerate(g.columns):
        g.gather_face(new, x_rim, k * LANES, 0, a, b)
    held_out[...] = dot(both_t[:ch, :], x_held[...]) + dot_chosen(face_low, x_rim, const)


def last_high_kernel(
    g, acol, ucol, count, scale, mass_wide, before, low_new, ordered, both, both_t, new, mine, x_next,
    filtered, own_out, sums, field, x_own, done, sems,
):
    d = g.d
    half = d * g.plane
    copies = [
        pltpu.make_async_copy(done.at[pl.ds(p, n)], filtered.at[pl.ds(p, n)], sems.at[k])
        for k, (p, n) in enumerate(((0, d), (d, d // 2), (d + d // 2, d // 2)))
    ]

    def give(planes):
        for p in planes:
            done[p] = field[p * g.plane : (p + 1) * g.plane, :].astype(bf16).reshape(g.e, g.e, LANES)

    field[:half, :] = low_new[...]
    for rows, _ in held_places(g, ucol[0], None):
        field[rows, :] = new[rows, :]
    field[: g.plane, :] = new[: g.plane, :]
    give(range(d))
    copies[0].start()
    field[half : half + g.plane, :] = new[half : half + g.plane, :]
    upper_sums(g, acol[0], scale, ordered, both, x_next, mine[...], sums)
    for p in range(d):
        if p:
            rows = pl.ds(half + p * g.plane, g.plane)
            added = sums[p * g.plane : (p + 1) * g.plane, :]
            value = before[rows, :] + mass_wide[rows, :] * (added * (2.0 / spectrum_half))
            field[rows, :] = value.astype(bf16).astype(f32)
        give([d + p])
        if (p + 1) % (d // 2) == 0:
            copies[1 + p // (d // 2)].start()
    a, b = split_element(acol[0])
    g.gather_element(field, x_own, 0, half, a, b, False)
    own_out[...] = dot(both_t[g.ch :, :], x_own[...])
    for copy in copies:
        copy.wait()


def call(kernel, scalars, operands, outs, scratch, flops, limit=24 << 20, hbm=False, far_outs=0):
    smem = pl.BlockSpec(memory_space=pltpu.SMEM)
    vmem = pl.BlockSpec(memory_space=pltpu.VMEM)
    far = pl.BlockSpec(memory_space=pltpu.MemorySpace.HBM)
    moved = sum(v.size * v.dtype.itemsize for v in operands)
    if hbm:
        operands = [pltpu.with_memory_space_constraint(v, pltpu.MemorySpace.HBM) for v in operands]
    return pl.pallas_call(
        kernel,
        out_shape=[jax.ShapeDtypeStruct(s, t) for s, t in outs],
        in_specs=[smem] * len(scalars) + [far if hbm else vmem] * len(operands),
        out_specs=[far] * far_outs + [vmem] * (len(outs) - far_outs),
        scratch_shapes=[pltpu.VMEM(*s) if isinstance(s, tuple) else s for s in scratch],
        compiler_params=pltpu.CompilerParams(vmem_limit_bytes=limit),
        cost_estimate=pl.CostEstimate(flops=flops, bytes_accessed=moved, transcendentals=0),
    )(*scalars, *operands)


def per_device(
    wave_in, mass_scale, potential, elem_scale, stiffness, proj_lower, proj_upper, kb_coef,
    atom_column, chan_count, upper_column,
):
    extent = wave_in.shape[0]
    degree = extent // 2
    ch = kb_coef.shape[-1]
    order, used = row_order(degree)
    padded = order.shape[0]
    perm = jnp.asarray(order, f32)[None, :]
    g = Mesh1(degree, ch, used, padded)
    plane, nodes = g.plane, g.nodes
    scalars = (atom_column, upper_column, chan_count)
    part = ((ch, LANES), f32)
    slab_s, half_s, plane_s = ((nodes, LANES), f32), ((nodes // 2, LANES), f32), ((plane, LANES), f32)
    x_s, x_one_s = ((padded, 4 * LANES), bf16), ((padded, LANES), bf16)
    wire_s = ((plane + ch, LANES), bf16)
    wire_first_s = ((plane + ch + FOLD + CONST_ROWS, LANES), bf16)
    face_s = ((LANES, 4 * LANES), bf16)
    face_sum_s = ((FACE, 4 * LANES), f32)

    slab, x_top, mass_wide, wave, stiff, scale, order_row, pot, kb, both, both_t, own, held, inner, outer = call(
        functools.partial(start_kernel, g), scalars,
        (wave_in, mass_scale, elem_scale, stiffness, jnp.swapaxes(proj_lower, 1, 2), jnp.swapaxes(proj_upper, 1, 2),
         kb_coef, perm, potential),
        [slab_s, x_s, slab_s, (wave_in.shape, bf16), (stiffness.shape, bf16), ((8, LANES), f32), (perm.shape, f32),
         (potential.shape, f32), (kb_coef.shape, f32), ((padded, 2 * ch), bf16), ((2 * ch, padded), bf16), part, part,
         wire_first_s, wire_first_s],
        [plane_s, wire_first_s, wire_s, (mass_scale.shape, f32), (elem_scale.shape, f32),
         ((2 * ch, stiffness.shape[0]), bf16), x_one_s, ((2, used, LANES), f32), ((padded, 2 * LANES), bf16),
         pltpu.SemaphoreType.DMA((12,))], 10**8, hbm=True,
    )
    inner, outer = swapped(inner, outer, "space")
    ordered, pot_wide = call(
        functools.partial(order_kernel, g), (), (stiff, order_row, pot),
        [((padded, padded), bf16), slab_s],
        [((-(-stiffness.shape[0] // LANES), used, LANES), f32), ((padded, padded), bf16)], 2 * 10**9,
    )
    bulk_scratch = [slab_s, ((used, 2 * LANES), f32), x_s]
    before, low_step, low_slab, face_own, x_face = call(
        functools.partial(bulk_kernel, g), (), (scale, ordered, x_top, slab, pot_wide, mass_wide, wave),
        [slab_s, half_s, half_s, face_sum_s, face_s], bulk_scratch, 2 * 10**9,
    )
    shared = (ordered, both, both_t)
    slab, x_top, step, own, held, inner, outer, kept = call(
        functools.partial(middle_kernel, g), scalars,
        (scale, mass_wide, before, low_step, low_slab, face_own, x_face, *shared, own, held, kb, inner, outer),
        [slab_s, x_s, slab_s, part, part, wire_s, wire_s, ((FACE + CONST_ROWS, LANES), bf16)],
        [half_s, plane_s, face_s, plane_s, wire_first_s, wire_s, wire_s, wire_s, plane_s, x_one_s], 10**8,
    )
    inner, outer = swapped(inner, outer, "space")
    before, low_new, face_own, x_face = call(
        functools.partial(bulk_last_kernel, g), (),
        (scale, ordered, x_top, slab, pot_wide, mass_wide, wave, step),
        [slab_s, half_s, face_sum_s, face_s], bulk_scratch, 2 * 10**9,
    )
    held, new, mine, x_next = call(
        functools.partial(last_low_kernel, g), scalars,
        (scale, mass_wide, before, face_own, x_face, *shared, own, held, kb, kept, inner, outer),
        [part, ((nodes // 2 + plane, LANES), f32), ((ch, LANES), bf16), face_s],
        [plane_s, plane_s, x_one_s, face_s, wire_s, wire_s, plane_s], 10**8,
    )
    held = shifted(held, "space", -1)
    filtered, own = call(
        functools.partial(last_high_kernel, g), scalars,
        (scale, mass_wide, before, low_new, *shared, new, mine, x_next),
        [(wave_in.shape, bf16), part],
        [half_s, slab_s, x_one_s, (wave_in.shape, bf16), pltpu.SemaphoreType.DMA((3,))], 10**9, far_outs=1,
    )
    return filtered, (own + held)[None]


def solution(mesh):
    in_specs = (
        P("space", None, None, "band"),
        P("space", None),
        P("space", None),
        P("space", None, None),
        P(),
        P("space", None, None),
        P("space", None, None),
        P("space", None),
        P("space"),
        P("space"),
        P("space"),
    )
    out_specs = (P("space", None, None, "band"), P("space", None, "band"))
    return jax.shard_map(
        per_device, mesh=mesh, in_specs=in_specs, out_specs=out_specs, check_vma=False
    )
```
